256 devices in a mesh: node: 4 (over y), rank: 32 (over z, x), chip: 2 (over core).
Axes of the slice: x: 4, y: 4, z: 8, core: 2. Of those that a mesh axis runs over, the one named last changes fastest.
Arguments:
- velocity: float32 [3, 8388608], P(None, ('node', 'rank', 'chip')), may hold values from -6 to 6
- refine: int32 [256], P(('node', 'rank', 'chip')), may hold values from 0 to 6
Outputs:
- filtered: float32 [3, 8388608], P(None, ('node', 'rank', 'chip'))
The draws below stay inside these ranges and needn't reach their ends.
All inputs are finite; a program needn't handle non-finite values.
Results may differ from the reference program's by a relative error of at most 0.00002.
Values sent between devices are 32-bit elements; how exact they have to be, the bound alone decides.
A program may use at most 128 MiB of HBM per device.

```python
import jax
import jax.numpy as jnp

COMP = 3
BLOCK = 32768
LEVELS = 6
BLOCKS = 256
CELLS = 8388608


def touch_ends(values, own_key, smallest, high):
    longest = values.shape.index(max(values.shape))
    spots = []
    for shift in (0, 1):
        where = [jax.random.randint(jax.random.fold_in(own_key, axis), (), 0, length) for axis, length in enumerate(values.shape)]
        where[longest] = (where[longest] + shift) % values.shape[longest]
        spots.append(tuple(where))
    return values.at[spots[0]].set(smallest).at[spots[1]].set(high)


def level_of(key, shape, split, least, top_value):
    level, own = 1.0, jax.random.fold_in(key, 6)
    for dim, shards_of in split:
        steps = jnp.exp(jax.random.uniform(jax.random.fold_in(own, dim), (shards_of,), jnp.float32, least / len(split), top_value / len(split)))
        level = level * jnp.repeat(steps, shape[dim] // shards_of).reshape([-1 if axis == dim else 1 for axis in range(len(shape))])
    return level


def centred(own_key, dims, scale, most, shards=(), kind=jnp.bfloat16):
    values = scale * jax.random.normal(own_key, dims, jnp.float32)
    if shards:
        values = values * level_of(own_key, dims, shards, -0.22, 0.18)
    return jnp.clip(values, -most, most).astype(kind)


def setup_inputs(seed: int = 0) -> dict:
    streams_of = jax.random.split(jax.random.key(seed), 3)
    return {
        "velocity": centred(streams_of[0], (COMP, CELLS), 1.0, 6.0, ((1, 256),), jnp.float32),
        "refine": touch_ends(jax.random.randint(streams_of[1], (BLOCKS,), 0, LEVELS + 1), jax.random.fold_in(streams_of[1], 1), 0, LEVELS).astype(jnp.int32),
    }


def predict(before, here, after, later):
    return (-before + 9.0 * here + 9.0 * after - later) / 16.0


def reference(velocity, refine):
    current = velocity
    details = []
    for level_index in range(LEVELS):
        even_part = current[:, 0::2]
        odd_part = current[:, 1::2]
        detail = odd_part - predict(jnp.roll(even_part, 1, axis=1), even_part, jnp.roll(even_part, -1, axis=1), jnp.roll(even_part, -2, axis=1))
        current = even_part + (jnp.roll(detail, 1, axis=1) + detail) / 4.0
        keep = jnp.repeat(refine, BLOCK // 2 ** (level_index + 1)) > level_index
        details.append(jnp.where(keep, detail, 0.0))
    for level_index in reversed(range(LEVELS)):
        detail = details[level_index]
        even_part = current - (jnp.roll(detail, 1, axis=1) + detail) / 4.0
        odd_part = detail + predict(jnp.roll(even_part, 1, axis=1), even_part, jnp.roll(even_part, -1, axis=1), jnp.roll(even_part, -2, axis=1))
        current = jnp.stack([even_part, odd_part], axis=2).reshape(COMP, -1)
    return current
```

```python
import functools

import jax
import jax.numpy as jnp
from jax import lax
from jax.experimental import pallas as pl
from jax.experimental.pallas import tpu as pltpu
from jax.sharding import PartitionSpec as P

AXES = ("node", "rank", "chip")
LEVELS = 6
LANES = 128
COMP = 3
MESH = pl.DeviceIdType.MESH
HALO = 3
WIN = 16
CHUNK = 8


def coordinates(flat, sizes):
    nodes, ranks, chips = sizes
    return (flat // (ranks * chips), (flat // chips) % ranks, flat % chips)


def neighbours(sizes):
    nodes, ranks, chips = sizes
    total = nodes * ranks * chips
    me = (lax.axis_index("node") * ranks + lax.axis_index("rank")) * chips + lax.axis_index("chip")
    return (
        coordinates(lax.rem(me + total - 1, total), sizes),
        coordinates(lax.rem(me + 1, total), sizes),
    )


def after(row, carry_lane):
    rolled = pltpu.roll(row, LANES - 1, 1)
    carried = pltpu.roll(rolled, 7, 0)
    return jnp.where(carry_lane == LANES - 1, carried, rolled)


def before(row, carry_lane):
    rolled = pltpu.roll(row, 1, 1)
    carried = pltpu.roll(rolled, 1, 0)
    return jnp.where(carry_lane == 0, carried, rolled)


def predict(e):
    n = e.shape[0] - 3
    return (e[1 : n + 1] + e[2 : n + 2]) * (9.0 / 16.0) - (e[0:n] + e[3 : n + 3]) * (1.0 / 16.0)


def forward(values, details, level, lane):
    pairs = (LANES >> level) // 2
    src = values[level]
    e_first = src[pl.ds(0, 2, stride=2)]
    e_last = src[2 * pairs - 2]
    pre = before(e_last, lane)[None]
    post = jnp.stack([after(e_first[0], lane), after(e_first[1], lane)])
    step = min(CHUNK, pairs)
    d_prev = None
    e_zero, d_zero = None, None
    for at in range(0, pairs, step):
        lo, hi = max(at - 1, 0), min(at + step + 2, pairs)
        e = src[pl.ds(2 * lo, hi - lo, stride=2)]
        if at == 0:
            e = jnp.concatenate([pre, e], axis=0)
        need = step + 3 - e.shape[0]
        if need:
            e = jnp.concatenate([e, post[:need]], axis=0)
        o = src[pl.ds(2 * at + 1, step, stride=2)]
        d = o - predict(e)
        details[level][pl.ds(at, step)] = d
        here = e[1 : step + 1]
        if at == 0:
            e_zero, d_zero = here[0], d[0]
            if step > 1:
                values[level + 1][pl.ds(1, step - 1)] = here[1:] + (d[:-1] + d[1:]) * 0.25
        else:
            back = jnp.concatenate([d_prev, d[:-1]], axis=0)
            values[level + 1][pl.ds(at, step)] = here + (back + d) * 0.25
        d_prev = d[step - 1 :]
    values[level + 1][0] = e_zero + (before(d_prev[0], lane) + d_zero) * 0.25


def inverse(values, details, level, lane, keep):
    pairs = (LANES >> level) // 2
    dst = values[level]
    coarse = values[level + 1]

    def kept(at, count):
        d = details[level][pl.ds(at, count)]
        return jnp.where(keep[None], d, 0.0)

    step = min(CHUNK, pairs)
    k_before = before(kept(pairs - 1, 1)[0], lane)[None]
    back = k_before
    for at in range(0, pairs, step):
        k = kept(at, step)
        if step > 1:
            shifted = jnp.concatenate([back, k[:-1]], axis=0)
        else:
            shifted = back
        dst[pl.ds(2 * at, step, stride=2)] = coarse[pl.ds(at, step)] - (shifted + k) * 0.25
        back = k[step - 1 :]
    e_first = dst[pl.ds(0, 2, stride=2)]
    pre = before(dst[2 * pairs - 2], lane)[None]
    post = jnp.stack([after(e_first[0], lane), after(e_first[1], lane)])
    for at in range(0, pairs, step):
        lo, hi = max(at - 1, 0), min(at + step + 2, pairs)
        e = dst[pl.ds(2 * lo, hi - lo, stride=2)]
        if at == 0:
            e = jnp.concatenate([pre, e], axis=0)
        need = step + 3 - e.shape[0]
        if need:
            e = jnp.concatenate([e, post[:need]], axis=0)
        dst[pl.ds(2 * at + 1, step, stride=2)] = kept(at, step) + predict(e)


def kernel(
    sizes, x_ref, refine_ref, out_ref, xb, win, ob, wout, own_level, near_level, v0, v1, v2, v3, v4, v5, v6,
    d0, d1, d2, d3, d4, d5, in_sem, win_sem, level_sem, send_sem, recv_sem, out_sem,
):
    values = (v0, v1, v2, v3, v4, v5, v6)
    details = (d0, d1, d2, d3, d4, d5)
    rows = x_ref.shape[0]
    left, right = neighbours(sizes)
    barrier = pltpu.get_barrier_semaphore()
    for device in (left, right):
        pl.semaphore_signal(barrier, inc=1, device_id=device, device_id_type=MESH)

    loads = []
    for c in range(COMP):
        loads.append(pltpu.make_async_copy(x_ref.at[:, c, :], xb.at[c], in_sem.at[c]))
        loads.append(
            pltpu.make_async_copy(
                x_ref.at[pl.ds(0, 8), c, :], win.at[pl.ds(c * WIN + 8, 8), :], win_sem.at[c]
            )
        )
        loads.append(
            pltpu.make_async_copy(
                x_ref.at[pl.ds(rows - 8, 8), c, :],
                win.at[pl.ds((COMP + c) * WIN, 8), :],
                win_sem.at[COMP + c],
            )
        )
    loads.append(pltpu.make_async_copy(refine_ref, own_level, level_sem))
    for copy in loads:
        copy.start()

    pl.semaphore_wait(barrier, 2)
    sends = []
    for c in range(COMP):
        sends.append(
            pltpu.make_async_remote_copy(
                src_ref=x_ref.at[pl.ds(rows - 8, 8), c, :],
                dst_ref=win.at[pl.ds(c * WIN, 8), :],
                send_sem=send_sem.at[c],
                recv_sem=recv_sem.at[c],
                device_id=right,
                device_id_type=MESH,
            )
        )
        sends.append(
            pltpu.make_async_remote_copy(
                src_ref=x_ref.at[pl.ds(0, 8), c, :],
                dst_ref=win.at[pl.ds((COMP + c) * WIN + 8, 8), :],
                send_sem=send_sem.at[COMP + c],
                recv_sem=recv_sem.at[COMP + c],
                device_id=left,
                device_id_type=MESH,
            )
        )
    for side, device in ((0, right), (1, left)):
        sends.append(
            pltpu.make_async_remote_copy(
                src_ref=refine_ref,
                dst_ref=near_level.at[side],
                send_sem=send_sem.at[2 * COMP + side],
                recv_sem=recv_sem.at[2 * COMP + side],
                device_id=device,
                device_id_type=MESH,
            )
        )
    for copy in sends:
        copy.start()
    for copy in loads:
        copy.wait()

    for c in range(COMP):
        for half in range(2):
            block = xb[c, pl.ds(half * LANES, LANES), :]
            v0[:, 2 * c + half, :] = block.T
    for copy in sends:
        copy.wait()
    v0[:, 6, :] = win[...].T

    lane = lax.broadcasted_iota(jnp.int32, (8, LANES), 1)
    sublane = lax.broadcasted_iota(jnp.int32, (8, LANES), 0)
    own = own_level[0]
    from_left = (sublane == 6) & (lane < COMP * WIN) & (lane % WIN < 8)
    from_right = (sublane == 6) & (lane >= COMP * WIN) & (lane % WIN >= 8)
    level_of = jnp.where(from_left, near_level[0, 0], jnp.where(from_right, near_level[1, 0], own))

    for level in range(LEVELS):
        forward(values, details, level, lane)
    for level in reversed(range(LEVELS)):
        inverse(values, details, level, lane, level_of > level)

    stores = []
    for c in range(COMP):
        for half in range(2):
            ob[c, pl.ds(half * LANES, LANES), :] = v0[:, 2 * c + half, :].T
        stores.append(
            pltpu.make_async_copy(
                ob.at[c, pl.ds(HALO, rows - 2 * HALO), :], out_ref.at[pl.ds(HALO, rows - 2 * HALO), c, :], out_sem.at[c]
            )
        )
        stores[-1].start()
    wout[...] = v0[:, 6, :].T
    for c in range(COMP):
        stores.append(
            pltpu.make_async_copy(
                wout.at[pl.ds(c * WIN + 8, HALO), :], out_ref.at[pl.ds(0, HALO), c, :], out_sem.at[COMP + c]
            )
        )
        stores[-1].start()
        stores.append(
            pltpu.make_async_copy(
                wout.at[pl.ds((COMP + c) * WIN + 8 - HALO, HALO), :],
                out_ref.at[pl.ds(rows - HALO, HALO), c, :],
                out_sem.at[2 * COMP + c],
            )
        )
        stores[-1].start()
    for copy in stores:
        copy.wait()


def per_device(sizes, velocity, refine):
    rows = velocity.shape[1] // LANES
    x = velocity.reshape(COMP, rows, LANES).transpose(1, 0, 2)
    f32 = jnp.float32
    out = pl.pallas_call(
        functools.partial(kernel, sizes),
        out_shape=jax.ShapeDtypeStruct(x.shape, f32),
        in_specs=[pl.BlockSpec(memory_space=pl.ANY)] * 2,
        out_specs=pl.BlockSpec(memory_space=pl.ANY),
        scratch_shapes=[
            pltpu.VMEM((COMP, rows, LANES), f32),
            pltpu.VMEM((LANES, LANES), f32),
            pltpu.VMEM((COMP, rows, LANES), f32),
            pltpu.VMEM((LANES, LANES), f32),
            pltpu.SMEM((1,), jnp.int32),
            pltpu.SMEM((2, 1), jnp.int32),
        ]
        + [pltpu.VMEM((LANES >> level, 8, LANES), f32) for level in range(LEVELS + 1)]
        + [pltpu.VMEM(((LANES >> level) // 2, 8, LANES), f32) for level in range(LEVELS)]
        + [
            pltpu.SemaphoreType.DMA((COMP,)),
            pltpu.SemaphoreType.DMA((2 * COMP,)),
            pltpu.SemaphoreType.DMA,
            pltpu.SemaphoreType.DMA((2 * COMP + 2,)),
            pltpu.SemaphoreType.DMA((2 * COMP + 2,)),
            pltpu.SemaphoreType.DMA((3 * COMP,)),
        ],
        compiler_params=pltpu.CompilerParams(collective_id=0, has_side_effects=True),
    )(x, refine)
    return out.transpose(1, 0, 2).reshape(velocity.shape)


def solution(mesh):
    sizes = tuple(mesh.shape[name] for name in AXES)
    return jax.shard_map(
        functools.partial(per_device, sizes),
        mesh=mesh,
        in_specs=(P(None, AXES), P(AXES)),
        out_specs=P(None, AXES),
        check_vma=False,
    )
```

```python
import functools

import jax
import jax.numpy as jnp
from jax import lax
from jax.experimental import pallas as pl
from jax.experimental.pallas import tpu as pltpu
from jax.sharding import PartitionSpec as P

AXES = ("node", "rank", "chip")
LEVELS = 6
LANES = 128
COMP = 3
MESH = pl.DeviceIdType.MESH
HALO = 3
WIN = 16
CHUNK = 8
VMEM_LIMIT = 8 << 20


def coordinates(flat, sizes):
    nodes, ranks, chips = sizes
    return (flat // (ranks * chips), (flat // chips) % ranks, flat % chips)


def neighbours(sizes):
    nodes, ranks, chips = sizes
    total = nodes * ranks * chips
    me = (lax.axis_index("node") * ranks + lax.axis_index("rank")) * chips + lax.axis_index("chip")
    return (
        coordinates(lax.rem(me + total - 1, total), sizes),
        coordinates(lax.rem(me + 1, total), sizes),
    )


def after_with_carry(row, lane):
    rolled = pltpu.roll(row, LANES - 1, 1)
    carried = pltpu.roll(rolled, 7, 0)
    return jnp.where(lane == LANES - 1, carried, rolled)


def before_with_carry(row, lane):
    rolled = pltpu.roll(row, 1, 1)
    carried = pltpu.roll(rolled, 1, 0)
    return jnp.where(lane == 0, carried, rolled)


def after_in_window(row, lane):
    return pltpu.roll(row, LANES - 1, 1)


def before_in_window(row, lane):
    return pltpu.roll(row, 1, 1)


def predict(e):
    n = e.shape[0] - 3
    return (e[1 : n + 1] + e[2 : n + 2]) * (9.0 / 16.0) - (e[0:n] + e[3 : n + 3]) * (1.0 / 16.0)


def forward(values, details, level, lane, before, after):
    pairs = (LANES >> level) // 2
    src = values[level]
    e_first = src[pl.ds(0, 2, stride=2)]
    pre = before(src[2 * pairs - 2], lane)[None]
    post = jnp.stack([after(e_first[0], lane), after(e_first[1], lane)])
    step = min(CHUNK, pairs)
    d_prev, e_zero, d_zero = None, None, None
    for at in range(0, pairs, step):
        lo, hi = max(at - 1, 0), min(at + step + 2, pairs)
        e = src[pl.ds(2 * lo, hi - lo, stride=2)]
        if at == 0:
            e = jnp.concatenate([pre, e], axis=0)
        need = step + 3 - e.shape[0]
        if need:
            e = jnp.concatenate([e, post[:need]], axis=0)
        d = src[pl.ds(2 * at + 1, step, stride=2)] - predict(e)
        details[level][pl.ds(at, step)] = d
        here = e[1 : step + 1]
        if at == 0:
            e_zero, d_zero = here[0], d[0]
            values[level + 1][pl.ds(1, step - 1)] = here[1:] + (d[:-1] + d[1:]) * 0.25
        else:
            back = jnp.concatenate([d_prev, d[:-1]], axis=0)
            values[level + 1][pl.ds(at, step)] = here + (back + d) * 0.25
        d_prev = d[step - 1 :]
    values[level + 1][0] = e_zero + (before(d_prev[0], lane) + d_zero) * 0.25


def inverse(values, details, level, lane, keep, before, after):
    pairs = (LANES >> level) // 2
    dst = values[level]
    coarse = values[level + 1]

    def kept(at, count):
        return jnp.where(keep[None], details[level][pl.ds(at, count)], 0.0)

    step = min(CHUNK, pairs)
    back = before(kept(pairs - 1, 1)[0], lane)[None]
    for at in range(0, pairs, step):
        k = kept(at, step)
        shifted = jnp.concatenate([back, k[:-1]], axis=0)
        dst[pl.ds(2 * at, step, stride=2)] = coarse[pl.ds(at, step)] - (shifted + k) * 0.25
        back = k[step - 1 :]
    e_first = dst[pl.ds(0, 2, stride=2)]
    pre = before(dst[2 * pairs - 2], lane)[None]
    post = jnp.stack([after(e_first[0], lane), after(e_first[1], lane)])
    for at in range(0, pairs, step):
        lo, hi = max(at - 1, 0), min(at + step + 2, pairs)
        e = dst[pl.ds(2 * lo, hi - lo, stride=2)]
        if at == 0:
            e = jnp.concatenate([pre, e], axis=0)
        need = step + 3 - e.shape[0]
        if need:
            e = jnp.concatenate([e, post[:need]], axis=0)
        dst[pl.ds(2 * at + 1, step, stride=2)] = kept(at, step) + predict(e)


def transform(values, details, lane, level_of, before, after):
    for level in range(LEVELS):
        forward(values, details, level, lane, before, after)
    for level in reversed(range(LEVELS)):
        inverse(values, details, level, lane, level_of > level, before, after)


def lanes_and_sublanes():
    return (
        lax.broadcasted_iota(jnp.int32, (8, LANES), 1),
        lax.broadcasted_iota(jnp.int32, (8, LANES), 0),
    )


def exchange_kernel(sizes, x_ref, refine_ref, ob, win, level_ref, xb, own_level, near_level, *rest):
    values, details = rest[: LEVELS + 1], rest[LEVELS + 1 : 2 * LEVELS + 1]
    in_sem, win_sem, level_sem, send_sem, recv_sem = rest[2 * LEVELS + 1 :]
    rows = x_ref.shape[0]
    left, right = neighbours(sizes)
    barrier = pltpu.get_barrier_semaphore()
    pl.semaphore_signal(barrier, inc=1, device_id=left, device_id_type=MESH)

    loads = []
    for c in range(COMP):
        loads.append(pltpu.make_async_copy(x_ref.at[:, c, :], xb.at[c], in_sem.at[c]))
    ends = [pltpu.make_async_copy(refine_ref, own_level, level_sem)]
    for c in range(COMP):
        ends.append(
            pltpu.make_async_copy(
                x_ref.at[pl.ds(0, 8), c, :], win.at[pl.ds(c * WIN + 8, 8), :], win_sem.at[c]
            )
        )
        ends.append(
            pltpu.make_async_copy(
                x_ref.at[pl.ds(rows - 8, 8), c, :],
                win.at[pl.ds((COMP + c) * WIN, 8), :],
                win_sem.at[COMP + c],
            )
        )
    for copy in loads + ends:
        copy.start()

    def remote(src, dst, index, device):
        return pltpu.make_async_remote_copy(
            src_ref=src,
            dst_ref=dst,
            send_sem=send_sem.at[index],
            recv_sem=recv_sem.at[index],
            device_id=device,
            device_id_type=MESH,
        )

    to_right = [remote(refine_ref, near_level.at[0], 2 * COMP, right)]
    to_left = [remote(refine_ref, near_level.at[1], 2 * COMP + 1, left)]
    for c in range(COMP):
        to_right.append(
            remote(
                x_ref.at[pl.ds(rows - HALO, HALO), c, :],
                win.at[pl.ds(c * WIN + 8 - HALO, HALO), :],
                c,
                right,
            )
        )
        to_left.append(
            remote(
                x_ref.at[pl.ds(0, HALO), c, :],
                win.at[pl.ds((COMP + c) * WIN + 8, HALO), :],
                COMP + c,
                left,
            )
        )
    pl.semaphore_wait(barrier, 1)
    for copy in to_right:
        copy.start()
    for copy in loads + ends:
        copy.wait()

    lane, sublane = lanes_and_sublanes()
    own = own_level[0]
    for c in range(COMP):
        for half in range(2):
            values[0][:, 2 * c + half, :] = xb[c, pl.ds(half * LANES, LANES), :].T
    transform(
        values, details, lane, jnp.full((8, LANES), own, jnp.int32), before_with_carry, after_with_carry
    )
    for c in range(COMP):
        for half in range(2):
            ob[c, pl.ds(half * LANES, LANES), :] = values[0][:, 2 * c + half, :].T

    for copy in to_right:
        copy.wait_recv()
    for copy in to_left:
        copy.start()
    for copy in to_left:
        copy.wait_recv()
    from_left = (lane < COMP * WIN) & (lane % WIN < 8)
    from_right = (lane >= COMP * WIN) & (lane % WIN >= 8)
    level_ref[...] = jnp.where(
        from_left, near_level[0, 0], jnp.where(from_right, near_level[1, 0], own)
    )
    for copy in to_right + to_left:
        copy.wait_send()


def ends_kernel(ob, win, level_ref, out_ref, wout, *rest):
    values, details = rest[: LEVELS + 1], rest[LEVELS + 1 : 2 * LEVELS + 1]
    (out_sem,) = rest[2 * LEVELS + 1 :]
    rows = out_ref.shape[0]
    stores = []
    for c in range(COMP):
        stores.append(
            pltpu.make_async_copy(
                ob.at[c, pl.ds(HALO, rows - 2 * HALO), :],
                out_ref.at[pl.ds(HALO, rows - 2 * HALO), c, :],
                out_sem.at[c],
            )
        )
        stores[-1].start()
    lane, sublane = lanes_and_sublanes()
    values[0][:, 0, :] = win[...].T
    transform(values, details, lane, level_ref[...], before_in_window, after_in_window)
    wout[...] = values[0][:, 0, :].T
    for c in range(COMP):
        stores.append(
            pltpu.make_async_copy(
                wout.at[pl.ds(c * WIN + 8, HALO), :],
                out_ref.at[pl.ds(0, HALO), c, :],
                out_sem.at[COMP + c],
            )
        )
        stores[-1].start()
        stores.append(
            pltpu.make_async_copy(
                wout.at[pl.ds((COMP + c) * WIN + 8 - HALO, HALO), :],
                out_ref.at[pl.ds(rows - HALO, HALO), c, :],
                out_sem.at[2 * COMP + c],
            )
        )
        stores[-1].start()
    for copy in stores:
        copy.wait()


def lifting_scratch():
    f32 = jnp.float32
    return [pltpu.VMEM((LANES >> level, 8, LANES), f32) for level in range(LEVELS + 1)] + [
        pltpu.VMEM(((LANES >> level) // 2, 8, LANES), f32) for level in range(LEVELS)
    ]


def per_device(sizes, velocity, refine):
    rows = velocity.shape[1] // LANES
    x = velocity.reshape(COMP, rows, LANES).transpose(1, 0, 2)
    x = pltpu.with_memory_space_constraint(x, pltpu.HBM)
    f32 = jnp.float32
    vmem = pl.BlockSpec(memory_space=pltpu.VMEM)
    ob, win, level_of = pl.pallas_call(
        functools.partial(exchange_kernel, sizes),
        out_shape=[
            jax.ShapeDtypeStruct((COMP, rows, LANES), f32),
            jax.ShapeDtypeStruct((LANES, LANES), f32),
            jax.ShapeDtypeStruct((8, LANES), jnp.int32),
        ],
        in_specs=[pl.BlockSpec(memory_space=pltpu.HBM)] * 2,
        out_specs=[vmem] * 3,
        scratch_shapes=[
            pltpu.VMEM((COMP, rows, LANES), f32),
            pltpu.SMEM((1,), jnp.int32),
            pltpu.SMEM((2, 1), jnp.int32),
        ]
        + lifting_scratch()
        + [
            pltpu.SemaphoreType.DMA((COMP,)),
            pltpu.SemaphoreType.DMA((2 * COMP,)),
            pltpu.SemaphoreType.DMA,
            pltpu.SemaphoreType.DMA((2 * COMP + 2,)),
            pltpu.SemaphoreType.DMA((2 * COMP + 2,)),
        ],
        compiler_params=pltpu.CompilerParams(
            collective_id=0, has_side_effects=True, vmem_limit_bytes=VMEM_LIMIT
        ),
    )(x, refine)
    out = pl.pallas_call(
        ends_kernel,
        out_shape=jax.ShapeDtypeStruct(x.shape, f32),
        in_specs=[vmem] * 3,
        out_specs=pl.BlockSpec(memory_space=pltpu.HBM),
        scratch_shapes=[pltpu.VMEM((LANES, LANES), f32)]
        + lifting_scratch()
        + [pltpu.SemaphoreType.DMA((3 * COMP,))],
        compiler_params=pltpu.CompilerParams(vmem_limit_bytes=VMEM_LIMIT),
    )(ob, win, level_of)
    return out.transpose(1, 0, 2).reshape(velocity.shape)


def solution(mesh):
    sizes = tuple(mesh.shape[name] for name in AXES)
    return jax.shard_map(
        functools.partial(per_device, sizes),
        mesh=mesh,
        in_specs=(P(None, AXES), P(AXES)),
        out_specs=P(None, AXES),
        check_vma=False,
    )
```

```python
import functools

import jax
import jax.numpy as jnp
from jax import lax
from jax.experimental import pallas as pl
from jax.experimental.pallas import tpu as pltpu
from jax.sharding import PartitionSpec as P

AXES = ("node", "rank", "chip")
LEVELS = 6
LANES = 128
COMP = 3
MESH = pl.DeviceIdType.MESH
HALO = 3
WIN = 16
CHUNK = 8
VMEM_LIMIT = 8 << 20


def coordinates(flat, sizes):
    nodes, ranks, chips = sizes
    return (flat // (ranks * chips), (flat // chips) % ranks, flat % chips)


def neighbours(sizes):
    nodes, ranks, chips = sizes
    total = nodes * ranks * chips
    me = (lax.axis_index("node") * ranks + lax.axis_index("rank")) * chips + lax.axis_index("chip")
    return (
        coordinates(lax.rem(me + total - 1, total), sizes),
        coordinates(lax.rem(me + 1, total), sizes),
    )


def after_with_carry(row, lane):
    rolled = pltpu.roll(row, LANES - 1, 1)
    carried = pltpu.roll(rolled, 7, 0)
    return jnp.where(lane == LANES - 1, carried, rolled)


def before_with_carry(row, lane):
    rolled = pltpu.roll(row, 1, 1)
    carried = pltpu.roll(rolled, 1, 0)
    return jnp.where(lane == 0, carried, rolled)


def after_in_window(row, lane):
    return pltpu.roll(row, LANES - 1, 1)


def before_in_window(row, lane):
    return pltpu.roll(row, 1, 1)


def predict(e):
    n = e.shape[0] - 3
    return (e[1 : n + 1] + e[2 : n + 2]) * (9.0 / 16.0) - (e[0:n] + e[3 : n + 3]) * (1.0 / 16.0)


def forward(values, details, level, lane, before, after):
    pairs = (LANES >> level) // 2
    src = values[level]
    e_first = src[pl.ds(0, 2, stride=2)]
    pre = before(src[2 * pairs - 2], lane)[None]
    post = jnp.stack([after(e_first[0], lane), after(e_first[1], lane)])
    step = min(CHUNK, pairs)
    d_prev, e_zero, d_zero = None, None, None
    for at in range(0, pairs, step):
        lo, hi = max(at - 1, 0), min(at + step + 2, pairs)
        e = src[pl.ds(2 * lo, hi - lo, stride=2)]
        if at == 0:
            e = jnp.concatenate([pre, e], axis=0)
        need = step + 3 - e.shape[0]
        if need:
            e = jnp.concatenate([e, post[:need]], axis=0)
        d = src[pl.ds(2 * at + 1, step, stride=2)] - predict(e)
        details[level][pl.ds(at, step)] = d
        here = e[1 : step + 1]
        if at == 0:
            e_zero, d_zero = here[0], d[0]
            values[level + 1][pl.ds(1, step - 1)] = here[1:] + (d[:-1] + d[1:]) * 0.25
        else:
            back = jnp.concatenate([d_prev, d[:-1]], axis=0)
            values[level + 1][pl.ds(at, step)] = here + (back + d) * 0.25
        d_prev = d[step - 1 :]
    values[level + 1][0] = e_zero + (before(d_prev[0], lane) + d_zero) * 0.25


def inverse(values, details, level, lane, keep, before, after):
    pairs = (LANES >> level) // 2
    dst = values[level]
    coarse = values[level + 1]

    def kept(at, count):
        return jnp.where(keep[None], details[level][pl.ds(at, count)], 0.0)

    step = min(CHUNK, pairs)
    back = before(kept(pairs - 1, 1)[0], lane)[None]
    for at in range(0, pairs, step):
        k = kept(at, step)
        shifted = jnp.concatenate([back, k[:-1]], axis=0)
        dst[pl.ds(2 * at, step, stride=2)] = coarse[pl.ds(at, step)] - (shifted + k) * 0.25
        back = k[step - 1 :]
    e_first = dst[pl.ds(0, 2, stride=2)]
    pre = before(dst[2 * pairs - 2], lane)[None]
    post = jnp.stack([after(e_first[0], lane), after(e_first[1], lane)])
    for at in range(0, pairs, step):
        lo, hi = max(at - 1, 0), min(at + step + 2, pairs)
        e = dst[pl.ds(2 * lo, hi - lo, stride=2)]
        if at == 0:
            e = jnp.concatenate([pre, e], axis=0)
        need = step + 3 - e.shape[0]
        if need:
            e = jnp.concatenate([e, post[:need]], axis=0)
        dst[pl.ds(2 * at + 1, step, stride=2)] = kept(at, step) + predict(e)


def transform(values, details, lane, level_of, before, after):
    for level in range(LEVELS):
        forward(values, details, level, lane, before, after)
    for level in reversed(range(LEVELS)):
        inverse(values, details, level, lane, level_of > level, before, after)


def lanes_and_sublanes():
    return (
        lax.broadcasted_iota(jnp.int32, (8, LANES), 1),
        lax.broadcasted_iota(jnp.int32, (8, LANES), 0),
    )


def exchange_kernel(sizes, x_ref, refine_ref, ob, win, level_ref, xb, own_level, near_level, *rest):
    values, details = rest[: LEVELS + 1], rest[LEVELS + 1 : 2 * LEVELS + 1]
    in_sem, win_sem, level_sem, send_sem, recv_sem, here_sem = rest[2 * LEVELS + 1 :]
    rows = x_ref.shape[0]
    left, right = neighbours(sizes)
    barrier = pltpu.get_barrier_semaphore()
    pl.semaphore_signal(barrier, inc=1, device_id=left, device_id_type=MESH)

    loads = []
    for c in range(COMP):
        loads.append(pltpu.make_async_copy(x_ref.at[:, c, :], xb.at[c], in_sem.at[c]))
    ends = [pltpu.make_async_copy(refine_ref, own_level, level_sem)]
    for c in range(COMP):
        ends.append(
            pltpu.make_async_copy(
                x_ref.at[pl.ds(0, 8), c, :], win.at[pl.ds(c * WIN + 8, 8), :], win_sem.at[c]
            )
        )
        ends.append(
            pltpu.make_async_copy(
                x_ref.at[pl.ds(rows - 8, 8), c, :],
                win.at[pl.ds((COMP + c) * WIN, 8), :],
                win_sem.at[COMP + c],
            )
        )
    for copy in loads + ends:
        copy.start()

    def remote(src, dst, index, device):
        return pltpu.make_async_remote_copy(
            src_ref=src,
            dst_ref=dst,
            send_sem=send_sem.at[index],
            recv_sem=recv_sem.at[index],
            device_id=device,
            device_id_type=MESH,
        )

    to_right = [remote(refine_ref, near_level.at[0], 2 * COMP, right)]
    to_left = [remote(refine_ref, near_level.at[1], 2 * COMP + 1, left)]
    for c in range(COMP):
        to_right.append(
            remote(
                x_ref.at[pl.ds(rows - HALO, HALO), c, :],
                win.at[pl.ds(c * WIN + 8 - HALO, HALO), :],
                c,
                right,
            )
        )
        to_left.append(
            remote(
                x_ref.at[pl.ds(0, HALO), c, :],
                win.at[pl.ds((COMP + c) * WIN + 8, HALO), :],
                COMP + c,
                left,
            )
        )
    pl.semaphore_wait(barrier, 1)
    pl.semaphore_signal(here_sem, inc=1, device_id=right, device_id_type=MESH)
    for copy in to_right:
        copy.start()
    for copy in loads + ends:
        copy.wait()

    lane, sublane = lanes_and_sublanes()
    own = own_level[0]
    for c in range(COMP):
        for half in range(2):
            values[0][:, 2 * c + half, :] = xb[c, pl.ds(half * LANES, LANES), :].T
    transform(
        values, details, lane, jnp.full((8, LANES), own, jnp.int32), before_with_carry, after_with_carry
    )
    for c in range(COMP):
        for half in range(2):
            ob[c, pl.ds(half * LANES, LANES), :] = values[0][:, 2 * c + half, :].T

    pl.semaphore_wait(here_sem, 1)
    for copy in to_left:
        copy.start()
    for copy in to_right + to_left:
        copy.wait_recv()
    from_left = (lane < COMP * WIN) & (lane % WIN < 8)
    from_right = (lane >= COMP * WIN) & (lane % WIN >= 8)
    level_ref[...] = jnp.where(
        from_left, near_level[0, 0], jnp.where(from_right, near_level[1, 0], own)
    )
    for copy in to_right + to_left:
        copy.wait_send()


def ends_kernel(ob, win, level_ref, out_ref, wout, *rest):
    values, details = rest[: LEVELS + 1], rest[LEVELS + 1 : 2 * LEVELS + 1]
    (out_sem,) = rest[2 * LEVELS + 1 :]
    rows = out_ref.shape[0]
    stores = []
    for c in range(COMP):
        stores.append(
            pltpu.make_async_copy(
                ob.at[c, pl.ds(HALO, rows - 2 * HALO), :],
                out_ref.at[pl.ds(HALO, rows - 2 * HALO), c, :],
                out_sem.at[c],
            )
        )
        stores[-1].start()
    lane, sublane = lanes_and_sublanes()
    values[0][:, 0, :] = win[...].T
    transform(values, details, lane, level_ref[...], before_in_window, after_in_window)
    wout[...] = values[0][:, 0, :].T
    for c in range(COMP):
        stores.append(
            pltpu.make_async_copy(
                wout.at[pl.ds(c * WIN + 8, HALO), :],
                out_ref.at[pl.ds(0, HALO), c, :],
                out_sem.at[COMP + c],
            )
        )
        stores[-1].start()
        stores.append(
            pltpu.make_async_copy(
                wout.at[pl.ds((COMP + c) * WIN + 8 - HALO, HALO), :],
                out_ref.at[pl.ds(rows - HALO, HALO), c, :],
                out_sem.at[2 * COMP + c],
            )
        )
        stores[-1].start()
    for copy in stores:
        copy.wait()


def lifting_scratch():
    f32 = jnp.float32
    return [pltpu.VMEM((LANES >> level, 8, LANES), f32) for level in range(LEVELS + 1)] + [
        pltpu.VMEM(((LANES >> level) // 2, 8, LANES), f32) for level in range(LEVELS)
    ]


def per_device(sizes, velocity, refine):
    rows = velocity.shape[1] // LANES
    x = velocity.reshape(COMP, rows, LANES).transpose(1, 0, 2)
    x = pltpu.with_memory_space_constraint(x, pltpu.HBM)
    f32 = jnp.float32
    vmem = pl.BlockSpec(memory_space=pltpu.VMEM)
    ob, win, level_of = pl.pallas_call(
        functools.partial(exchange_kernel, sizes),
        out_shape=[
            jax.ShapeDtypeStruct((COMP, rows, LANES), f32),
            jax.ShapeDtypeStruct((LANES, LANES), f32),
            jax.ShapeDtypeStruct((8, LANES), jnp.int32),
        ],
        in_specs=[pl.BlockSpec(memory_space=pltpu.HBM)] * 2,
        out_specs=[vmem] * 3,
        scratch_shapes=[
            pltpu.VMEM((COMP, rows, LANES), f32),
            pltpu.SMEM((1,), jnp.int32),
            pltpu.SMEM((2, 1), jnp.int32),
        ]
        + lifting_scratch()
        + [
            pltpu.SemaphoreType.DMA((COMP,)),
            pltpu.SemaphoreType.DMA((2 * COMP,)),
            pltpu.SemaphoreType.DMA,
            pltpu.SemaphoreType.DMA((2 * COMP + 2,)),
            pltpu.SemaphoreType.DMA((2 * COMP + 2,)),
            pltpu.SemaphoreType.REGULAR,
        ],
        compiler_params=pltpu.CompilerParams(
            collective_id=0, has_side_effects=True, vmem_limit_bytes=VMEM_LIMIT
        ),
    )(x, refine)
    out = pl.pallas_call(
        ends_kernel,
        out_shape=jax.ShapeDtypeStruct(x.shape, f32),
        in_specs=[vmem] * 3,
        out_specs=pl.BlockSpec(memory_space=pltpu.HBM),
        scratch_shapes=[pltpu.VMEM((LANES, LANES), f32)]
        + lifting_scratch()
        + [pltpu.SemaphoreType.DMA((3 * COMP,))],
        compiler_params=pltpu.CompilerParams(vmem_limit_bytes=VMEM_LIMIT),
    )(ob, win, level_of)
    return out.transpose(1, 0, 2).reshape(velocity.shape)


def solution(mesh):
    sizes = tuple(mesh.shape[name] for name in AXES)
    return jax.shard_map(
        functools.partial(per_device, sizes),
        mesh=mesh,
        in_specs=(P(None, AXES), P(AXES)),
        out_specs=P(None, AXES),
        check_vma=False,
    )
```

```python
import functools

import jax
import jax.numpy as jnp
from jax import lax
from jax.experimental import pallas as pl
from jax.experimental.pallas import tpu as pltpu
from jax.sharding import PartitionSpec as P

AXES = ("node", "rank", "chip")
LEVELS = 6
LANES = 128
COMP = 3
MESH = pl.DeviceIdType.MESH
HALO = 3
WIN = 16
CHUNK = 8
VMEM_LIMIT = 8 << 20


def coordinates(flat, sizes):
    nodes, ranks, chips = sizes
    return (flat // (ranks * chips), (flat // chips) % ranks, flat % chips)


def neighbours(sizes):
    nodes, ranks, chips = sizes
    total = nodes * ranks * chips
    me = (lax.axis_index("node") * ranks + lax.axis_index("rank")) * chips + lax.axis_index("chip")
    return (
        me,
        coordinates(lax.rem(me + total - 1, total), sizes),
        coordinates(lax.rem(me + 1, total), sizes),
    )


def on_seam(device, sizes):
    place = lax.rem(device, sizes[1] * sizes[2])
    return (place == 0) | (place == sizes[1] * sizes[2] - 1)


def after_with_carry(row, lane):
    rolled = pltpu.roll(row, LANES - 1, 1)
    carried = pltpu.roll(rolled, 7, 0)
    return jnp.where(lane == LANES - 1, carried, rolled)


def before_with_carry(row, lane):
    rolled = pltpu.roll(row, 1, 1)
    carried = pltpu.roll(rolled, 1, 0)
    return jnp.where(lane == 0, carried, rolled)


def predict(e):
    n = e.shape[0] - 3
    return (e[1 : n + 1] + e[2 : n + 2]) * (9.0 / 16.0) - (e[0:n] + e[3 : n + 3]) * (1.0 / 16.0)


def forward(values, details, level, lane, before, after):
    pairs = (LANES >> level) // 2
    src = values[level]
    e_first = src[pl.ds(0, 2, stride=2)]
    pre = before(src[2 * pairs - 2], lane)[None]
    post = jnp.stack([after(e_first[0], lane), after(e_first[1], lane)])
    step = min(CHUNK, pairs)
    d_prev, e_zero, d_zero = None, None, None
    for at in range(0, pairs, step):
        lo, hi = max(at - 1, 0), min(at + step + 2, pairs)
        e = src[pl.ds(2 * lo, hi - lo, stride=2)]
        if at == 0:
            e = jnp.concatenate([pre, e], axis=0)
        need = step + 3 - e.shape[0]
        if need:
            e = jnp.concatenate([e, post[:need]], axis=0)
        d = src[pl.ds(2 * at + 1, step, stride=2)] - predict(e)
        details[level][pl.ds(at, step)] = d
        here = e[1 : step + 1]
        if at == 0:
            e_zero, d_zero = here[0], d[0]
            values[level + 1][pl.ds(1, step - 1)] = here[1:] + (d[:-1] + d[1:]) * 0.25
        else:
            back = jnp.concatenate([d_prev, d[:-1]], axis=0)
            values[level + 1][pl.ds(at, step)] = here + (back + d) * 0.25
        d_prev = d[step - 1 :]
    values[level + 1][0] = e_zero + (before(d_prev[0], lane) + d_zero) * 0.25


def inverse(values, details, level, lane, keep, before, after):
    pairs = (LANES >> level) // 2
    dst = values[level]
    coarse = values[level + 1]

    def kept(at, count):
        return jnp.where(keep[None], details[level][pl.ds(at, count)], 0.0)

    step = min(CHUNK, pairs)
    back = before(kept(pairs - 1, 1)[0], lane)[None]
    for at in range(0, pairs, step):
        k = kept(at, step)
        shifted = jnp.concatenate([back, k[:-1]], axis=0)
        dst[pl.ds(2 * at, step, stride=2)] = coarse[pl.ds(at, step)] - (shifted + k) * 0.25
        back = k[step - 1 :]
    e_first = dst[pl.ds(0, 2, stride=2)]
    pre = before(dst[2 * pairs - 2], lane)[None]
    post = jnp.stack([after(e_first[0], lane), after(e_first[1], lane)])
    for at in range(0, pairs, step):
        lo, hi = max(at - 1, 0), min(at + step + 2, pairs)
        e = dst[pl.ds(2 * lo, hi - lo, stride=2)]
        if at == 0:
            e = jnp.concatenate([pre, e], axis=0)
        need = step + 3 - e.shape[0]
        if need:
            e = jnp.concatenate([e, post[:need]], axis=0)
        dst[pl.ds(2 * at + 1, step, stride=2)] = kept(at, step) + predict(e)


def transform(values, details, lane, level_of, before, after):
    for level in range(LEVELS):
        forward(values, details, level, lane, before, after)
    for level in reversed(range(LEVELS)):
        inverse(values, details, level, lane, level_of > level, before, after)


def lanes_and_sublanes():
    return (
        lax.broadcasted_iota(jnp.int32, (8, LANES), 1),
        lax.broadcasted_iota(jnp.int32, (8, LANES), 0),
    )


PARTS = 8
PART = LANES // PARTS


def shifted(value, by, sublane):
    if by == 0:
        return value
    if by > 0:
        turned = pltpu.roll(value, LANES - 1, 1)
        if by == PARTS:
            return turned
        return pltpu.roll(jnp.where(sublane < by, turned, value), PARTS - by, 0)
    turned = pltpu.roll(value, 1, 1)
    if by == -PARTS:
        return turned
    return pltpu.roll(jnp.where(sublane >= PARTS + by, turned, value), -by, 0)


class Line:
    def __init__(self, values, sublane):
        self.values, self.sublane, self.seen = values, sublane, {}

    def __getitem__(self, place):
        if place not in self.seen:
            part, slot = divmod(place, len(self.values))
            self.seen[place] = shifted(self.values[slot], part, self.sublane)
        return self.seen[place]


def predicted(before, here, after, later):
    return (here + after) * (9.0 / 16.0) - (before + later) * (1.0 / 16.0)


def lift_window(rows_in_parts, level_of, sublane):
    line = Line(rows_in_parts, sublane)
    kept = []
    level = 0
    while len(line.values) > 1:
        half = len(line.values) // 2
        detail = {}
        for i in range(-1, half):
            detail[i] = line[2 * i + 1] - predicted(
                line[2 * i - 2], line[2 * i], line[2 * i + 2], line[2 * i + 4]
            )
        scaling = [line[2 * i] + (detail[i - 1] + detail[i]) * 0.25 for i in range(half)]
        keep = level_of > level
        kept.append(Line([jnp.where(keep, detail[i], 0.0) for i in range(half)], sublane))
        line = Line(scaling, sublane)
        level += 1
    inner = []
    for apart in (1, 2):
        at = lambda place: line[place * apart]
        detail = at(0) - predicted(at(-3), at(-1), at(1), at(3))
        left = at(-1) - predicted(at(-4), at(-2), at(0), at(2))
        right = at(1) - predicted(at(-2), at(0), at(2), at(4))
        inner.append(Line([jnp.where(level_of > level, detail, 0.0)], sublane))
        line = Line([at(0) + (left + right) * 0.25], sublane)
        level += 1
    for apart in (2, 1):
        k = inner.pop()
        at = lambda place: k[place * apart]
        even = line[0] - (at(-1) + at(1)) * 0.25
        odd = (
            at(0) * (23.0 / 32.0)
            - (at(-2) + at(2)) * (1.0 / 8.0)
            + (at(-4) + at(4)) * (1.0 / 64.0)
            + predicted(line[-3 * apart], line[-apart], line[apart], line[3 * apart])
        )
        line = Line([jnp.where(sublane % (2 * apart) == 0, even, odd)], sublane)
    wanted = [range(0, PART)]
    for _ in kept:
        low = [n // 2 - 1 if n % 2 else n // 2 for n in wanted[-1]]
        high = [n // 2 + 2 if n % 2 else n // 2 for n in wanted[-1]]
        wanted.append(range(min(low), max(high) + 1))
    current = {place: line[place] for place in wanted.pop()}
    while kept:
        k = kept.pop()
        even = {i: value - (k[i - 1] + k[i]) * 0.25 for i, value in current.items()}
        current = {}
        for n in wanted.pop():
            i = n // 2
            if n % 2:
                current[n] = k[i] + predicted(even[i - 1], even[i], even[i + 1], even[i + 2])
            else:
                current[n] = even[i]
    return [current[n] for n in range(PART)]


def exchange_kernel(sizes, x_ref, refine_ref, ob, win, level_ref, xb, own_level, near_level, *rest):
    values, details = rest[: LEVELS + 1], rest[LEVELS + 1 : 2 * LEVELS + 1]
    in_sem, win_sem, level_sem, send_sem, recv_sem, here_sem = rest[2 * LEVELS + 1 :]
    rows = x_ref.shape[0]
    me, left, right = neighbours(sizes)
    left_seam, right_seam = on_seam(me, sizes), on_seam(me + 1, sizes)
    barrier = pltpu.get_barrier_semaphore()
    pl.semaphore_signal(barrier, inc=1, device_id=left, device_id_type=MESH)

    @pl.when(jnp.logical_not(right_seam))
    def _():
        pl.semaphore_signal(barrier, inc=1, device_id=right, device_id_type=MESH)

    loads = []
    for c in range(COMP):
        loads.append(pltpu.make_async_copy(x_ref.at[:, c, :], xb.at[c], in_sem.at[c]))
    ends = [pltpu.make_async_copy(refine_ref, own_level, level_sem)]
    for c in range(COMP):
        ends.append(
            pltpu.make_async_copy(
                x_ref.at[pl.ds(0, 8), c, :], win.at[pl.ds(c * WIN + 8, 8), :], win_sem.at[c]
            )
        )
        ends.append(
            pltpu.make_async_copy(
                x_ref.at[pl.ds(rows - 8, 8), c, :],
                win.at[pl.ds((COMP + c) * WIN, 8), :],
                win_sem.at[COMP + c],
            )
        )
    for copy in loads + ends:
        copy.start()

    def remote(src, dst, index, device):
        return pltpu.make_async_remote_copy(
            src_ref=src,
            dst_ref=dst,
            send_sem=send_sem.at[index],
            recv_sem=recv_sem.at[index],
            device_id=device,
            device_id_type=MESH,
        )

    to_right = [remote(refine_ref, near_level.at[0], 2 * COMP, right)]
    to_left = [remote(refine_ref, near_level.at[1], 2 * COMP + 1, left)]
    for c in range(COMP):
        to_right.append(
            remote(
                x_ref.at[pl.ds(rows - HALO, HALO), c, :],
                win.at[pl.ds(c * WIN + 8 - HALO, HALO), :],
                c,
                right,
            )
        )
        to_left.append(
            remote(
                x_ref.at[pl.ds(0, HALO), c, :],
                win.at[pl.ds((COMP + c) * WIN + 8, HALO), :],
                COMP + c,
                left,
            )
        )
    pl.semaphore_wait(barrier, jnp.where(left_seam, 1, 2))
    for copy in to_right:
        copy.start()

    @pl.when(right_seam)
    def _():
        pl.semaphore_signal(here_sem, inc=1, device_id=right, device_id_type=MESH)

    @pl.when(jnp.logical_not(left_seam))
    def _():
        for copy in to_left:
            copy.start()

    for copy in loads + ends:
        copy.wait()

    lane, sublane = lanes_and_sublanes()
    own = own_level[0]
    for c in range(COMP):
        for half in range(2):
            values[0][:, 2 * c + half, :] = xb[c, pl.ds(half * LANES, LANES), :].T
    transform(
        values, details, lane, jnp.full((8, LANES), own, jnp.int32), before_with_carry, after_with_carry
    )
    for c in range(COMP):
        for half in range(2):
            ob[c, pl.ds(half * LANES, LANES), :] = values[0][:, 2 * c + half, :].T

    @pl.when(left_seam)
    def _():
        pl.semaphore_wait(here_sem, 1)
        for copy in to_left:
            copy.start()

    for copy in to_right + to_left:
        copy.wait_recv()
    from_left = (lane < COMP * WIN) & (lane % WIN < 8)
    from_right = (lane >= COMP * WIN) & (lane % WIN >= 8)
    level_ref[...] = jnp.where(
        from_left, near_level[0, 0], jnp.where(from_right, near_level[1, 0], own)
    )
    for copy in to_right + to_left:
        copy.wait_send()


def ends_kernel(ob, win, level_ref, out_ref, wout, turned, out_sem):
    rows = out_ref.shape[0]
    stores = []
    for c in range(COMP):
        stores.append(
            pltpu.make_async_copy(
                ob.at[c, pl.ds(HALO, rows - 2 * HALO), :],
                out_ref.at[pl.ds(HALO, rows - 2 * HALO), c, :],
                out_sem.at[c],
            )
        )
        stores[-1].start()
    lane, sublane = lanes_and_sublanes()
    turned[...] = win[...].T
    parts = [turned[pl.ds(k, PARTS, stride=PART), :] for k in range(PART)]
    for k, value in enumerate(lift_window(parts, level_ref[...], sublane)):
        turned[pl.ds(k, PARTS, stride=PART), :] = value
    wout[...] = turned[...].T
    for c in range(COMP):
        stores.append(
            pltpu.make_async_copy(
                wout.at[pl.ds(c * WIN + 8, HALO), :],
                out_ref.at[pl.ds(0, HALO), c, :],
                out_sem.at[COMP + c],
            )
        )
        stores[-1].start()
        stores.append(
            pltpu.make_async_copy(
                wout.at[pl.ds((COMP + c) * WIN + 8 - HALO, HALO), :],
                out_ref.at[pl.ds(rows - HALO, HALO), c, :],
                out_sem.at[2 * COMP + c],
            )
        )
        stores[-1].start()
    for copy in stores:
        copy.wait()


def lifting_scratch():
    f32 = jnp.float32
    return [pltpu.VMEM((LANES >> level, 8, LANES), f32) for level in range(LEVELS + 1)] + [
        pltpu.VMEM(((LANES >> level) // 2, 8, LANES), f32) for level in range(LEVELS)
    ]


def per_device(sizes, velocity, refine):
    rows = velocity.shape[1] // LANES
    x = velocity.reshape(COMP, rows, LANES).transpose(1, 0, 2)
    x = pltpu.with_memory_space_constraint(x, pltpu.HBM)
    f32 = jnp.float32
    vmem = pl.BlockSpec(memory_space=pltpu.VMEM)
    ob, win, level_of = pl.pallas_call(
        functools.partial(exchange_kernel, sizes),
        out_shape=[
            jax.ShapeDtypeStruct((COMP, rows, LANES), f32),
            jax.ShapeDtypeStruct((LANES, LANES), f32),
            jax.ShapeDtypeStruct((8, LANES), jnp.int32),
        ],
        in_specs=[pl.BlockSpec(memory_space=pltpu.HBM)] * 2,
        out_specs=[vmem] * 3,
        scratch_shapes=[
            pltpu.VMEM((COMP, rows, LANES), f32),
            pltpu.SMEM((1,), jnp.int32),
            pltpu.SMEM((2, 1), jnp.int32),
        ]
        + lifting_scratch()
        + [
            pltpu.SemaphoreType.DMA((COMP,)),
            pltpu.SemaphoreType.DMA((2 * COMP,)),
            pltpu.SemaphoreType.DMA,
            pltpu.SemaphoreType.DMA((2 * COMP + 2,)),
            pltpu.SemaphoreType.DMA((2 * COMP + 2,)),
            pltpu.SemaphoreType.REGULAR,
        ],
        compiler_params=pltpu.CompilerParams(
            collective_id=0, has_side_effects=True, vmem_limit_bytes=VMEM_LIMIT
        ),
    )(x, refine)
    out = pl.pallas_call(
        ends_kernel,
        out_shape=jax.ShapeDtypeStruct(x.shape, f32),
        in_specs=[vmem] * 3,
        out_specs=pl.BlockSpec(memory_space=pltpu.HBM),
        scratch_shapes=[pltpu.VMEM((LANES, LANES), f32)] * 2
        + [pltpu.SemaphoreType.DMA((3 * COMP,))],
        compiler_params=pltpu.CompilerParams(vmem_limit_bytes=VMEM_LIMIT),
    )(ob, win, level_of)
    return out.transpose(1, 0, 2).reshape(velocity.shape)


def solution(mesh):
    sizes = tuple(mesh.shape[name] for name in AXES)
    return jax.shard_map(
        functools.partial(per_device, sizes),
        mesh=mesh,
        in_specs=(P(None, AXES), P(AXES)),
        out_specs=P(None, AXES),
        check_vma=False,
    )
```

```python
import functools

import jax
import jax.numpy as jnp
from jax import lax
from jax.experimental import pallas as pl
from jax.experimental.pallas import tpu as pltpu
from jax.sharding import PartitionSpec as P

AXES = ("node", "rank", "chip")
LEVELS = 6
LANES = 128
COMP = 3
MESH = pl.DeviceIdType.MESH
HALO = 3
WIN = 3 * HALO
SIDES = 8
CHUNK = 8
VMEM_LIMIT = 8 << 20


def coordinates(flat, sizes):
    nodes, ranks, chips = sizes
    return (flat // (ranks * chips), (flat // chips) % ranks, flat % chips)


def neighbours(sizes):
    nodes, ranks, chips = sizes
    total = nodes * ranks * chips
    me = (lax.axis_index("node") * ranks + lax.axis_index("rank")) * chips + lax.axis_index("chip")
    return (
        me,
        coordinates(lax.rem(me + total - 1, total), sizes),
        coordinates(lax.rem(me + 1, total), sizes),
    )


def on_seam(device, sizes):
    place = lax.rem(device, sizes[1] * sizes[2])
    return (place == 0) | (place == sizes[1] * sizes[2] - 1)


def after_with_carry(row, lane):
    rolled = pltpu.roll(row, LANES - 1, 1)
    carried = pltpu.roll(rolled, 7, 0)
    return jnp.where(lane == LANES - 1, carried, rolled)


def before_with_carry(row, lane):
    rolled = pltpu.roll(row, 1, 1)
    carried = pltpu.roll(rolled, 1, 0)
    return jnp.where(lane == 0, carried, rolled)


def predict(e):
    n = e.shape[0] - 3
    return (e[1 : n + 1] + e[2 : n + 2]) * (9.0 / 16.0) - (e[0:n] + e[3 : n + 3]) * (1.0 / 16.0)


def forward(values, details, level, lane, before, after):
    pairs = (LANES >> level) // 2
    src = values[level]
    e_first = src[pl.ds(0, 2, stride=2)]
    pre = before(src[2 * pairs - 2], lane)[None]
    post = jnp.stack([after(e_first[0], lane), after(e_first[1], lane)])
    step = min(CHUNK, pairs)
    d_prev, e_zero, d_zero = None, None, None
    for at in range(0, pairs, step):
        lo, hi = max(at - 1, 0), min(at + step + 2, pairs)
        e = src[pl.ds(2 * lo, hi - lo, stride=2)]
        if at == 0:
            e = jnp.concatenate([pre, e], axis=0)
        need = step + 3 - e.shape[0]
        if need:
            e = jnp.concatenate([e, post[:need]], axis=0)
        d = src[pl.ds(2 * at + 1, step, stride=2)] - predict(e)
        details[level][pl.ds(at, step)] = d
        here = e[1 : step + 1]
        if at == 0:
            e_zero, d_zero = here[0], d[0]
            values[level + 1][pl.ds(1, step - 1)] = here[1:] + (d[:-1] + d[1:]) * 0.25
        else:
            back = jnp.concatenate([d_prev, d[:-1]], axis=0)
            values[level + 1][pl.ds(at, step)] = here + (back + d) * 0.25
        d_prev = d[step - 1 :]
    values[level + 1][0] = e_zero + (before(d_prev[0], lane) + d_zero) * 0.25


def inverse(values, details, level, lane, keep, before, after):
    pairs = (LANES >> level) // 2
    dst = values[level]
    coarse = values[level + 1]

    def kept(at, count):
        return jnp.where(keep[None], details[level][pl.ds(at, count)], 0.0)

    step = min(CHUNK, pairs)
    back = before(kept(pairs - 1, 1)[0], lane)[None]
    for at in range(0, pairs, step):
        k = kept(at, step)
        shifted = jnp.concatenate([back, k[:-1]], axis=0)
        dst[pl.ds(2 * at, step, stride=2)] = coarse[pl.ds(at, step)] - (shifted + k) * 0.25
        back = k[step - 1 :]
    e_first = dst[pl.ds(0, 2, stride=2)]
    pre = before(dst[2 * pairs - 2], lane)[None]
    post = jnp.stack([after(e_first[0], lane), after(e_first[1], lane)])
    for at in range(0, pairs, step):
        lo, hi = max(at - 1, 0), min(at + step + 2, pairs)
        e = dst[pl.ds(2 * lo, hi - lo, stride=2)]
        if at == 0:
            e = jnp.concatenate([pre, e], axis=0)
        need = step + 3 - e.shape[0]
        if need:
            e = jnp.concatenate([e, post[:need]], axis=0)
        dst[pl.ds(2 * at + 1, step, stride=2)] = kept(at, step) + predict(e)


def transform(values, details, lane, level_of, before, after):
    for level in range(LEVELS):
        forward(values, details, level, lane, before, after)
    for level in reversed(range(LEVELS)):
        inverse(values, details, level, lane, level_of > level, before, after)


def lanes_and_sublanes():
    return (
        lax.broadcasted_iota(jnp.int32, (8, LANES), 1),
        lax.broadcasted_iota(jnp.int32, (8, LANES), 0),
    )


PARTS = 8
PART = LANES // PARTS


def shifted(value, by, sublane):
    if by == 0:
        return value
    if by > 0:
        turned = pltpu.roll(value, LANES - SIDES, 1)
        if by == PARTS:
            return turned
        return pltpu.roll(jnp.where(sublane < by, turned, value), PARTS - by, 0)
    turned = pltpu.roll(value, SIDES, 1)
    if by == -PARTS:
        return turned
    return pltpu.roll(jnp.where(sublane >= PARTS + by, turned, value), -by, 0)


class Line:
    def __init__(self, values, sublane):
        self.values, self.sublane, self.seen = values, sublane, {}

    def __getitem__(self, place):
        if place not in self.seen:
            part, slot = divmod(place, len(self.values))
            self.seen[place] = shifted(self.values[slot], part, self.sublane)
        return self.seen[place]


def predicted(before, here, after, later):
    return (here + after) * (9.0 / 16.0) - (before + later) * (1.0 / 16.0)


def lift_window(rows_in_parts, level_of, sublane):
    line = Line(rows_in_parts, sublane)
    kept = []
    level = 0
    while len(line.values) > 1:
        half = len(line.values) // 2
        detail = {}
        for i in range(-1, half):
            detail[i] = line[2 * i + 1] - predicted(
                line[2 * i - 2], line[2 * i], line[2 * i + 2], line[2 * i + 4]
            )
        scaling = [line[2 * i] + (detail[i - 1] + detail[i]) * 0.25 for i in range(half)]
        keep = level_of > level
        kept.append(Line([jnp.where(keep, detail[i], 0.0) for i in range(half)], sublane))
        line = Line(scaling, sublane)
        level += 1
    inner = []
    for apart in (1, 2):
        at = lambda place: line[place * apart]
        detail = at(0) - predicted(at(-3), at(-1), at(1), at(3))
        left = at(-1) - predicted(at(-4), at(-2), at(0), at(2))
        right = at(1) - predicted(at(-2), at(0), at(2), at(4))
        inner.append(Line([jnp.where(level_of > level, detail, 0.0)], sublane))
        line = Line([at(0) + (left + right) * 0.25], sublane)
        level += 1
    for apart in (2, 1):
        k = inner.pop()
        at = lambda place: k[place * apart]
        even = line[0] - (at(-1) + at(1)) * 0.25
        odd = (
            at(0) * (23.0 / 32.0)
            - (at(-2) + at(2)) * (1.0 / 8.0)
            + (at(-4) + at(4)) * (1.0 / 64.0)
            + predicted(line[-3 * apart], line[-apart], line[apart], line[3 * apart])
        )
        line = Line([jnp.where(sublane % (2 * apart) == 0, even, odd)], sublane)
    wanted = [range(0, PART)]
    for _ in kept:
        low = [n // 2 - 1 if n % 2 else n // 2 for n in wanted[-1]]
        high = [n // 2 + 2 if n % 2 else n // 2 for n in wanted[-1]]
        wanted.append(range(min(low), max(high) + 1))
    current = {place: line[place] for place in wanted.pop()}
    while kept:
        k = kept.pop()
        even = {i: value - (k[i - 1] + k[i]) * 0.25 for i, value in current.items()}
        current = {}
        for n in wanted.pop():
            i = n // 2
            if n % 2:
                current[n] = k[i] + predicted(even[i - 1], even[i], even[i + 1], even[i + 2])
            else:
                current[n] = even[i]
    return [current[n] for n in range(PART)]


def exchange_kernel(sizes, x_ref, refine_ref, ob, win, level_ref, xb, own_level, near_level, *rest):
    values, details = rest[: LEVELS + 1], rest[LEVELS + 1 : 2 * LEVELS + 1]
    in_sem, win_sem, level_sem, send_sem, recv_sem, here_sem = rest[2 * LEVELS + 1 :]
    rows = x_ref.shape[0]
    me, left, right = neighbours(sizes)
    left_seam, right_seam = on_seam(me, sizes), on_seam(me + 1, sizes)
    barrier = pltpu.get_barrier_semaphore()
    pl.semaphore_signal(barrier, inc=1, device_id=left, device_id_type=MESH)

    @pl.when(jnp.logical_not(right_seam))
    def _():
        pl.semaphore_signal(barrier, inc=1, device_id=right, device_id_type=MESH)

    def remote(src, dst, index, device):
        return pltpu.make_async_remote_copy(
            src_ref=src,
            dst_ref=dst,
            send_sem=send_sem.at[index],
            recv_sem=recv_sem.at[index],
            device_id=device,
            device_id_type=MESH,
        )

    low, high = pl.ds(0, COMP), pl.ds(COMP, COMP)
    to_right = [
        remote(x_ref.at[pl.ds(rows - HALO, HALO)], win.at[pl.ds(0, HALO), low, :], 0, right),
        remote(refine_ref, near_level.at[0], 1, right),
    ]
    to_left = [
        remote(x_ref.at[pl.ds(0, HALO)], win.at[pl.ds(2 * HALO, HALO), high, :], 2, left),
        remote(refine_ref, near_level.at[1], 3, left),
    ]
    pl.semaphore_wait(barrier, jnp.where(left_seam, 1, 2))
    for copy in to_right:
        copy.start()

    @pl.when(right_seam)
    def _():
        pl.semaphore_signal(here_sem, inc=1, device_id=right, device_id_type=MESH)

    @pl.when(jnp.logical_not(left_seam))
    def _():
        for copy in to_left:
            copy.start()

    loads = [
        pltpu.make_async_copy(x_ref.at[:, c, :], xb.at[c], in_sem.at[c]) for c in range(COMP)
    ] + [
        pltpu.make_async_copy(refine_ref, own_level, level_sem),
        pltpu.make_async_copy(
            x_ref.at[pl.ds(0, 2 * HALO)], win.at[pl.ds(HALO, 2 * HALO), low, :], win_sem.at[0]
        ),
        pltpu.make_async_copy(
            x_ref.at[pl.ds(rows - 2 * HALO, 2 * HALO)], win.at[pl.ds(0, 2 * HALO), high, :], win_sem.at[1]
        ),
    ]
    for copy in loads:
        copy.start()
    for copy in loads:
        copy.wait()

    lane, sublane = lanes_and_sublanes()
    own = own_level[0]
    for c in range(COMP):
        for half in range(2):
            values[0][:, 2 * c + half, :] = xb[c, pl.ds(half * LANES, LANES), :].T
    transform(
        values, details, lane, jnp.full((8, LANES), own, jnp.int32), before_with_carry, after_with_carry
    )
    for c in range(COMP):
        for half in range(2):
            ob[c, pl.ds(half * LANES, LANES), :] = values[0][:, 2 * c + half, :].T

    @pl.when(left_seam)
    def _():
        pl.semaphore_wait(here_sem, 1)
        for copy in to_left:
            copy.start()

    for copy in to_right + to_left:
        copy.wait_send()
    for copy in to_right + to_left:
        copy.wait_recv()
    side, row = lane % SIDES, lane // SIDES
    from_left = (side < COMP) & (row < HALO)
    from_right = (side >= COMP) & (row >= 2 * HALO)
    level_ref[...] = jnp.where(
        from_left, near_level[0, 0], jnp.where(from_right, near_level[1, 0], own)
    )


def ends_kernel(ob, win, level_ref, out_ref, wout, turned, out_sem):
    rows = out_ref.shape[0]
    stores = []
    for c in range(COMP):
        stores.append(
            pltpu.make_async_copy(
                ob.at[c, pl.ds(HALO, rows - 2 * HALO), :],
                out_ref.at[pl.ds(HALO, rows - 2 * HALO), c, :],
                out_sem.at[c],
            )
        )
        stores[-1].start()
    lane, sublane = lanes_and_sublanes()
    used = WIN * SIDES
    turned[:, :used] = win[...].reshape(used, LANES).T
    parts = [turned[pl.ds(k, PARTS, stride=PART), :] for k in range(PART)]
    for k, value in enumerate(lift_window(parts, level_ref[...], sublane)):
        turned[pl.ds(k, PARTS, stride=PART), :] = value
    redone = turned[...].T[HALO * SIDES : 2 * HALO * SIDES]
    wout[...] = redone.reshape(HALO, SIDES, LANES)
    for side, first in ((0, 0), (1, rows - HALO)):
        stores.append(
            pltpu.make_async_copy(
                wout.at[:, pl.ds(side * COMP, COMP), :], out_ref.at[pl.ds(first, HALO)], out_sem.at[COMP + side]
            )
        )
        stores[-1].start()
    for copy in stores:
        copy.wait()


def lifting_scratch():
    f32 = jnp.float32
    return [pltpu.VMEM((LANES >> level, 8, LANES), f32) for level in range(LEVELS + 1)] + [
        pltpu.VMEM(((LANES >> level) // 2, 8, LANES), f32) for level in range(LEVELS)
    ]


def per_device(sizes, velocity, refine):
    rows = velocity.shape[1] // LANES
    x = velocity.reshape(COMP, rows, LANES).transpose(1, 0, 2)
    x = pltpu.with_memory_space_constraint(x, pltpu.HBM)
    f32 = jnp.float32
    vmem = pl.BlockSpec(memory_space=pltpu.VMEM)
    ob, win, level_of = pl.pallas_call(
        functools.partial(exchange_kernel, sizes),
        out_shape=[
            jax.ShapeDtypeStruct((COMP, rows, LANES), f32),
            jax.ShapeDtypeStruct((WIN, SIDES, LANES), f32),
            jax.ShapeDtypeStruct((8, LANES), jnp.int32),
        ],
        in_specs=[pl.BlockSpec(memory_space=pltpu.HBM)] * 2,
        out_specs=[vmem] * 3,
        scratch_shapes=[
            pltpu.VMEM((COMP, rows, LANES), f32),
            pltpu.SMEM((1,), jnp.int32),
            pltpu.SMEM((2, 1), jnp.int32),
        ]
        + lifting_scratch()
        + [
            pltpu.SemaphoreType.DMA((COMP,)),
            pltpu.SemaphoreType.DMA((2,)),
            pltpu.SemaphoreType.DMA,
            pltpu.SemaphoreType.DMA((4,)),
            pltpu.SemaphoreType.DMA((4,)),
            pltpu.SemaphoreType.REGULAR,
        ],
        compiler_params=pltpu.CompilerParams(
            collective_id=0, has_side_effects=True, vmem_limit_bytes=VMEM_LIMIT
        ),
    )(x, refine)
    out = pl.pallas_call(
        ends_kernel,
        out_shape=jax.ShapeDtypeStruct(x.shape, f32),
        in_specs=[vmem] * 3,
        out_specs=pl.BlockSpec(memory_space=pltpu.HBM),
        scratch_shapes=[
            pltpu.VMEM((HALO, SIDES, LANES), f32),
            pltpu.VMEM((LANES, LANES), f32),
            pltpu.SemaphoreType.DMA((COMP + 2,)),
        ],
        compiler_params=pltpu.CompilerParams(vmem_limit_bytes=VMEM_LIMIT),
    )(ob, win, level_of)
    return out.transpose(1, 0, 2).reshape(velocity.shape)


def solution(mesh):
    sizes = tuple(mesh.shape[name] for name in AXES)
    return jax.shard_map(
        functools.partial(per_device, sizes),
        mesh=mesh,
        in_specs=(P(None, AXES), P(AXES)),
        out_specs=P(None, AXES),
        check_vma=False,
    )
```

```python
import functools

import jax
import jax.numpy as jnp
from jax import lax
from jax.experimental import pallas as pl
from jax.experimental.pallas import tpu as pltpu
from jax.sharding import PartitionSpec as P

AXES = ("node", "rank", "chip")
LEVELS = 6
LANES = 128
COMP = 3
MESH = pl.DeviceIdType.MESH
HALO = 3
WIN = 3 * HALO
SIDES = 8
CHUNK = 8
VMEM_LIMIT = 8 << 20


def coordinates(flat, sizes):
    nodes, ranks, chips = sizes
    return (flat // (ranks * chips), (flat // chips) % ranks, flat % chips)


def neighbours(sizes):
    nodes, ranks, chips = sizes
    total = nodes * ranks * chips
    me = (lax.axis_index("node") * ranks + lax.axis_index("rank")) * chips + lax.axis_index("chip")
    return (
        me,
        coordinates(lax.rem(me + total - 1, total), sizes),
        coordinates(lax.rem(me + 1, total), sizes),
    )


def on_seam(device, sizes):
    place = lax.rem(device, sizes[1] * sizes[2])
    return (place == 0) | (place == sizes[1] * sizes[2] - 1)


def after_with_carry(row, lane):
    rolled = pltpu.roll(row, LANES - 1, 1)
    carried = pltpu.roll(rolled, 7, 0)
    return jnp.where(lane == LANES - 1, carried, rolled)


def before_with_carry(row, lane):
    rolled = pltpu.roll(row, 1, 1)
    carried = pltpu.roll(rolled, 1, 0)
    return jnp.where(lane == 0, carried, rolled)


def predict(e):
    n = e.shape[0] - 3
    return (e[1 : n + 1] + e[2 : n + 2]) * (9.0 / 16.0) - (e[0:n] + e[3 : n + 3]) * (1.0 / 16.0)


def forward(values, details, level, lane, before, after):
    pairs = (LANES >> level) // 2
    src = values[level]
    e_first = src[pl.ds(0, 2, stride=2)]
    pre = before(src[2 * pairs - 2], lane)[None]
    post = jnp.stack([after(e_first[0], lane), after(e_first[1], lane)])
    step = min(CHUNK, pairs)
    d_prev, e_zero, d_zero = None, None, None
    for at in range(0, pairs, step):
        lo, hi = max(at - 1, 0), min(at + step + 2, pairs)
        e = src[pl.ds(2 * lo, hi - lo, stride=2)]
        if at == 0:
            e = jnp.concatenate([pre, e], axis=0)
        need = step + 3 - e.shape[0]
        if need:
            e = jnp.concatenate([e, post[:need]], axis=0)
        d = src[pl.ds(2 * at + 1, step, stride=2)] - predict(e)
        details[level][pl.ds(at, step)] = d
        here = e[1 : step + 1]
        if at == 0:
            e_zero, d_zero = here[0], d[0]
            values[level + 1][pl.ds(1, step - 1)] = here[1:] + (d[:-1] + d[1:]) * 0.25
        else:
            back = jnp.concatenate([d_prev, d[:-1]], axis=0)
            values[level + 1][pl.ds(at, step)] = here + (back + d) * 0.25
        d_prev = d[step - 1 :]
    values[level + 1][0] = e_zero + (before(d_prev[0], lane) + d_zero) * 0.25


def inverse(values, details, level, lane, keep, before, after):
    pairs = (LANES >> level) // 2
    dst = values[level]
    coarse = values[level + 1]

    def kept(at, count):
        return jnp.where(keep[None], details[level][pl.ds(at, count)], 0.0)

    step = min(CHUNK, pairs)
    back = before(kept(pairs - 1, 1)[0], lane)[None]
    for at in range(0, pairs, step):
        k = kept(at, step)
        shifted = jnp.concatenate([back, k[:-1]], axis=0)
        dst[pl.ds(2 * at, step, stride=2)] = coarse[pl.ds(at, step)] - (shifted + k) * 0.25
        back = k[step - 1 :]
    e_first = dst[pl.ds(0, 2, stride=2)]
    pre = before(dst[2 * pairs - 2], lane)[None]
    post = jnp.stack([after(e_first[0], lane), after(e_first[1], lane)])
    for at in range(0, pairs, step):
        lo, hi = max(at - 1, 0), min(at + step + 2, pairs)
        e = dst[pl.ds(2 * lo, hi - lo, stride=2)]
        if at == 0:
            e = jnp.concatenate([pre, e], axis=0)
        need = step + 3 - e.shape[0]
        if need:
            e = jnp.concatenate([e, post[:need]], axis=0)
        dst[pl.ds(2 * at + 1, step, stride=2)] = kept(at, step) + predict(e)


def transform(values, details, lane, level_of, before, after):
    for level in range(LEVELS):
        forward(values, details, level, lane, before, after)
    for level in reversed(range(LEVELS)):
        inverse(values, details, level, lane, level_of > level, before, after)


def lanes_and_sublanes():
    return (
        lax.broadcasted_iota(jnp.int32, (8, LANES), 1),
        lax.broadcasted_iota(jnp.int32, (8, LANES), 0),
    )


PARTS = 8
PART = LANES // PARTS


def rows_away(value, by):
    return pltpu.roll(value, (-by * SIDES) % LANES, 1) if by else value


def parts_away(here, beyond, by, sublane):
    turn = (-by) % PARTS
    inside = sublane < PARTS - by if by > 0 else sublane >= -by
    return jnp.where(inside, pltpu.roll(here, turn, 0), pltpu.roll(beyond, turn, 0))


def predicted(before, here, after, later):
    return (here + after) * (9.0 / 16.0) - (before + later) * (1.0 / 16.0)


def by_place(values, beyond, place, sublane):
    part, slot = divmod(place, len(values))
    if part == 0:
        return values[slot]
    return parts_away(values[slot], beyond[slot], part, sublane)


class Rows:
    def __init__(self, values, sublane):
        self.values, self.sublane = values, sublane

    def at(self, row, by):
        away, by = (row + by // PARTS, 0) if by % PARTS == 0 else (row, by)
        if by == 0:
            return self.values[away]
        beyond = self.values.get(away + (1 if by > 0 else -1), self.values[away])
        return parts_away(self.values[away], beyond, by, self.sublane)


class Kept:
    def __init__(self, values, sublane):
        self.values, self.sublane, self.seen = values, sublane, {}

    def __getitem__(self, place):
        if place not in self.seen:
            part, slot = divmod(place, len(self.values))
            value = self.values[slot]
            if part:
                beyond = rows_away(value, 1 if part > 0 else -1)
                value = parts_away(value, beyond, part, self.sublane)
            self.seen[place] = value
        return self.seen[place]


def lift_window(inner, outer, level_of, sublane):
    kept = []
    level = 0
    while len(inner) > 1:
        half = len(inner) // 2
        halves = []
        for mine, other in ((inner, outer), (outer, inner)):
            at = lambda place: by_place(mine, other, place, sublane)
            ahead = [at(2 * i) for i in range(-2, half + 2)]
            detail = [
                at(2 * i + 1) - predicted(*ahead[i + 1 : i + 5]) for i in range(-1, half)
            ]
            scaling = [
                ahead[i + 2] + (detail[i] + detail[i + 1]) * 0.25 for i in range(half)
            ]
            halves.append((detail[1:], scaling))
        kept.append(Kept([jnp.where(level_of > level, d, 0.0) for d in halves[0][0]], sublane))
        inner, outer = halves[0][1], halves[1][1]
        level += 1
    levels = {row: rows_away(level_of, row) for row in range(-2, 3)}
    line = Rows({row: rows_away(inner[0], row) for row in range(-4, 5)}, sublane)
    inside = []
    for apart, reach, held in ((1, 3, 1), (2, 2, 2)):
        scaling = {}
        for row in range(-reach, reach + 1):
            at = lambda by: line.at(row, by * apart)
            scaling[row] = (
                at(0) * (23.0 / 32.0)
                + (at(-1) + at(1)) * 0.25
                - (at(-2) + at(2)) * 0.125
                + (at(-4) + at(4)) * (1.0 / 64.0)
            )
        details = {}
        for row in range(-held, held + 1):
            at = lambda by: line.at(row, by * apart)
            detail = at(0) - predicted(at(-3), at(-1), at(1), at(3))
            details[row] = jnp.where(levels[row] > level, detail, 0.0)
        inside.append(Rows(details, sublane))
        line = Rows(scaling, sublane)
        level += 1
    for apart in (2, 1):
        k = inside.pop()
        values = {}
        for row in (-1, 0, 1):
            at = lambda by: k.at(row, by * apart)
            even = line.at(row, 0) - (at(-1) + at(1)) * 0.25
            odd = (
                at(0) * (23.0 / 32.0)
                - (at(-2) + at(2)) * 0.125
                + (at(-4) + at(4)) * (1.0 / 64.0)
                + predicted(*(line.at(row, by * apart) for by in (-3, -1, 1, 3)))
            )
            values[row] = jnp.where(sublane % (2 * apart) == 0, even, odd)
        line = Rows(values, sublane)
    wanted = [range(0, PART)]
    for _ in kept:
        low = [n // 2 - 1 if n % 2 else n // 2 for n in wanted[-1]]
        high = [n // 2 + 2 if n % 2 else n // 2 for n in wanted[-1]]
        wanted.append(range(min(low), max(high) + 1))
    current = {place: line.at(0, place) for place in wanted.pop()}
    while kept:
        k = kept.pop()
        even = {i: value - (k[i - 1] + k[i]) * 0.25 for i, value in current.items()}
        current = {}
        for n in wanted.pop():
            i = n // 2
            if n % 2:
                current[n] = k[i] + predicted(even[i - 1], even[i], even[i + 1], even[i + 2])
            else:
                current[n] = even[i]
    return [current[n] for n in range(PART)]


def exchange_kernel(sizes, x_ref, refine_ref, ob, win, level_ref, xb, own_level, near_level, *rest):
    values, details = rest[: LEVELS + 1], rest[LEVELS + 1 : 2 * LEVELS + 1]
    in_sem, win_sem, level_sem, send_sem, recv_sem, here_sem = rest[2 * LEVELS + 1 :]
    rows = x_ref.shape[0]
    me, left, right = neighbours(sizes)
    left_seam, right_seam = on_seam(me, sizes), on_seam(me + 1, sizes)
    barrier = pltpu.get_barrier_semaphore()
    pl.semaphore_signal(barrier, inc=1, device_id=left, device_id_type=MESH)

    @pl.when(jnp.logical_not(right_seam))
    def _():
        pl.semaphore_signal(barrier, inc=1, device_id=right, device_id_type=MESH)

    def remote(src, dst, index, device):
        return pltpu.make_async_remote_copy(
            src_ref=src,
            dst_ref=dst,
            send_sem=send_sem.at[index],
            recv_sem=recv_sem.at[index],
            device_id=device,
            device_id_type=MESH,
        )

    low, high = pl.ds(0, COMP), pl.ds(COMP, COMP)
    to_right = [
        remote(x_ref.at[pl.ds(rows - HALO, HALO)], win.at[pl.ds(0, HALO), low, :], 0, right),
        remote(refine_ref, near_level.at[0], 1, right),
    ]
    to_left = [
        remote(x_ref.at[pl.ds(0, HALO)], win.at[pl.ds(2 * HALO, HALO), high, :], 2, left),
        remote(refine_ref, near_level.at[1], 3, left),
    ]
    pl.semaphore_wait(barrier, jnp.where(left_seam, 1, 2))
    for copy in to_right:
        copy.start()

    @pl.when(right_seam)
    def _():
        pl.semaphore_signal(here_sem, inc=1, device_id=right, device_id_type=MESH)

    @pl.when(jnp.logical_not(left_seam))
    def _():
        for copy in to_left:
            copy.start()

    loads = [
        pltpu.make_async_copy(x_ref.at[:, c, :], xb.at[c], in_sem.at[c]) for c in range(COMP)
    ] + [
        pltpu.make_async_copy(refine_ref, own_level, level_sem),
        pltpu.make_async_copy(
            x_ref.at[pl.ds(0, 2 * HALO)], win.at[pl.ds(HALO, 2 * HALO), low, :], win_sem.at[0]
        ),
        pltpu.make_async_copy(
            x_ref.at[pl.ds(rows - 2 * HALO, 2 * HALO)], win.at[pl.ds(0, 2 * HALO), high, :], win_sem.at[1]
        ),
    ]
    for copy in loads:
        copy.start()
    for copy in loads:
        copy.wait()

    lane, sublane = lanes_and_sublanes()
    own = own_level[0]
    for c in range(COMP):
        for half in range(2):
            values[0][:, 2 * c + half, :] = xb[c, pl.ds(half * LANES, LANES), :].T
    transform(
        values, details, lane, jnp.full((8, LANES), own, jnp.int32), before_with_carry, after_with_carry
    )
    for c in range(COMP):
        for half in range(2):
            ob[c, pl.ds(half * LANES, LANES), :] = values[0][:, 2 * c + half, :].T

    @pl.when(left_seam)
    def _():
        pl.semaphore_wait(here_sem, 1)
        for copy in to_left:
            copy.start()

    for copy in to_right + to_left:
        copy.wait_send()
    for copy in to_right + to_left:
        copy.wait_recv()
    side, row = lane % SIDES, lane // SIDES
    from_left = (side < COMP) & (row < HALO)
    from_right = (side >= COMP) & (row >= 2 * HALO)
    level_ref[...] = jnp.where(
        from_left, near_level[0, 0], jnp.where(from_right, near_level[1, 0], own)
    )


def ends_kernel(ob, win, level_ref, out_ref, wout, turned, beyond, out_sem):
    rows = out_ref.shape[0]
    stores = []
    for c in range(COMP):
        stores.append(
            pltpu.make_async_copy(
                ob.at[c, pl.ds(HALO, rows - 2 * HALO), :],
                out_ref.at[pl.ds(HALO, rows - 2 * HALO), c, :],
                out_sem.at[c],
            )
        )
        stores[-1].start()
    lane, sublane = lanes_and_sublanes()
    used = WIN * SIDES
    rows_here = win[...]
    rows_next = jnp.concatenate([rows_here[1:], rows_here[:1]], axis=0)
    rows_last = jnp.concatenate([rows_here[WIN - 1 :], rows_here[: WIN - 1]], axis=0)
    cell = lax.broadcasted_iota(jnp.int32, rows_here.shape, 2)
    around = jnp.where(cell < LANES // 2, rows_next, rows_last)
    turned[:, :used] = rows_here.reshape(used, LANES).T
    beyond[:, :used] = around.reshape(used, LANES).T
    inner = [turned[pl.ds(k, PARTS, stride=PART), :] for k in range(PART)]
    outer = [beyond[pl.ds(k, PARTS, stride=PART), :] for k in range(PART)]
    for k, value in enumerate(lift_window(inner, outer, level_ref[...], sublane)):
        turned[pl.ds(k, PARTS, stride=PART), :] = value
    redone = turned[...].T[HALO * SIDES : 2 * HALO * SIDES]
    wout[...] = redone.reshape(HALO, SIDES, LANES)
    for side, first in ((0, 0), (1, rows - HALO)):
        stores.append(
            pltpu.make_async_copy(
                wout.at[:, pl.ds(side * COMP, COMP), :], out_ref.at[pl.ds(first, HALO)], out_sem.at[COMP + side]
            )
        )
        stores[-1].start()
    for copy in stores:
        copy.wait()


def lifting_scratch():
    f32 = jnp.float32
    return [pltpu.VMEM((LANES >> level, 8, LANES), f32) for level in range(LEVELS + 1)] + [
        pltpu.VMEM(((LANES >> level) // 2, 8, LANES), f32) for level in range(LEVELS)
    ]


def per_device(sizes, velocity, refine):
    rows = velocity.shape[1] // LANES
    x = velocity.reshape(COMP, rows, LANES).transpose(1, 0, 2)
    x = pltpu.with_memory_space_constraint(x, pltpu.HBM)
    f32 = jnp.float32
    vmem = pl.BlockSpec(memory_space=pltpu.VMEM)
    ob, win, level_of = pl.pallas_call(
        functools.partial(exchange_kernel, sizes),
        out_shape=[
            jax.ShapeDtypeStruct((COMP, rows, LANES), f32),
            jax.ShapeDtypeStruct((WIN, SIDES, LANES), f32),
            jax.ShapeDtypeStruct((8, LANES), jnp.int32),
        ],
        in_specs=[pl.BlockSpec(memory_space=pltpu.HBM)] * 2,
        out_specs=[vmem] * 3,
        scratch_shapes=[
            pltpu.VMEM((COMP, rows, LANES), f32),
            pltpu.SMEM((1,), jnp.int32),
            pltpu.SMEM((2, 1), jnp.int32),
        ]
        + lifting_scratch()
        + [
            pltpu.SemaphoreType.DMA((COMP,)),
            pltpu.SemaphoreType.DMA((2,)),
            pltpu.SemaphoreType.DMA,
            pltpu.SemaphoreType.DMA((4,)),
            pltpu.SemaphoreType.DMA((4,)),
            pltpu.SemaphoreType.REGULAR,
        ],
        compiler_params=pltpu.CompilerParams(
            collective_id=0, has_side_effects=True, vmem_limit_bytes=VMEM_LIMIT
        ),
    )(x, refine)
    out = pl.pallas_call(
        ends_kernel,
        out_shape=jax.ShapeDtypeStruct(x.shape, f32),
        in_specs=[vmem] * 3,
        out_specs=pl.BlockSpec(memory_space=pltpu.HBM),
        scratch_shapes=[
            pltpu.VMEM((HALO, SIDES, LANES), f32),
            pltpu.VMEM((LANES, LANES), f32),
            pltpu.VMEM((LANES, LANES), f32),
            pltpu.SemaphoreType.DMA((COMP + 2,)),
        ],
        compiler_params=pltpu.CompilerParams(vmem_limit_bytes=VMEM_LIMIT),
    )(ob, win, level_of)
    return out.transpose(1, 0, 2).reshape(velocity.shape)


def solution(mesh):
    sizes = tuple(mesh.shape[name] for name in AXES)
    return jax.shard_map(
        functools.partial(per_device, sizes),
        mesh=mesh,
        in_specs=(P(None, AXES), P(AXES)),
        out_specs=P(None, AXES),
        check_vma=False,
    )
```

```python
import functools

import jax
import jax.numpy as jnp
from jax import lax
from jax.experimental import pallas as pl
from jax.experimental.pallas import tpu as pltpu
from jax.sharding import PartitionSpec as P

AXES = ("node", "rank", "chip")
LEVELS = 6
LANES = 128
COMP = 3
MESH = pl.DeviceIdType.MESH
HALO = 3
WIN = 3 * HALO
SIDES = 8
CHUNK = 8
VMEM_LIMIT = 8 << 20


def neighbours(sizes):
    nodes, ranks, chips = sizes
    node, rank, chip = (lax.axis_index(name) for name in AXES)
    first_chip, last_chip = chip == 0, chip == chips - 1
    first, last = first_chip & (rank == 0), last_chip & (rank == ranks - 1)
    left = (
        jnp.where(first, jnp.where(node == 0, nodes - 1, node - 1), node),
        jnp.where(first_chip, jnp.where(rank == 0, ranks - 1, rank - 1), rank),
        jnp.where(first_chip, chips - 1, chip - 1),
    )
    right = (
        jnp.where(last, jnp.where(node == nodes - 1, 0, node + 1), node),
        jnp.where(last_chip, jnp.where(rank == ranks - 1, 0, rank + 1), rank),
        jnp.where(last_chip, 0, chip + 1),
    )
    return (node, rank, chip), left, right


def on_seam(device, sizes):
    _, rank, chip = device
    return ((rank == 0) & (chip == 0)) | ((rank == sizes[1] - 1) & (chip == sizes[2] - 1))


def wait_for_rows(count, buffer, semaphore):
    rows = buffer.at[0, pl.ds(0, count), :]
    pltpu.make_async_copy(rows, rows, semaphore).wait()


def after_with_carry(row, lane):
    rolled = pltpu.roll(row, LANES - 1, 1)
    carried = pltpu.roll(rolled, 7, 0)
    return jnp.where(lane == LANES - 1, carried, rolled)


def before_with_carry(row, lane):
    rolled = pltpu.roll(row, 1, 1)
    carried = pltpu.roll(rolled, 1, 0)
    return jnp.where(lane == 0, carried, rolled)


def predict(e):
    n = e.shape[0] - 3
    return (e[1 : n + 1] + e[2 : n + 2]) * (9.0 / 16.0) - (e[0:n] + e[3 : n + 3]) * (1.0 / 16.0)


def forward(values, details, level, lane, before, after):
    pairs = (LANES >> level) // 2
    src = values[level]
    e_first = src[pl.ds(0, 2, stride=2)]
    pre = before(src[2 * pairs - 2], lane)[None]
    post = jnp.stack([after(e_first[0], lane), after(e_first[1], lane)])
    step = min(CHUNK, pairs)
    d_prev, e_zero, d_zero = None, None, None
    for at in range(0, pairs, step):
        lo, hi = max(at - 1, 0), min(at + step + 2, pairs)
        e = src[pl.ds(2 * lo, hi - lo, stride=2)]
        if at == 0:
            e = jnp.concatenate([pre, e], axis=0)
        need = step + 3 - e.shape[0]
        if need:
            e = jnp.concatenate([e, post[:need]], axis=0)
        d = src[pl.ds(2 * at + 1, step, stride=2)] - predict(e)
        details[level][pl.ds(at, step)] = d
        here = e[1 : step + 1]
        if at == 0:
            e_zero, d_zero = here[0], d[0]
            values[level + 1][pl.ds(1, step - 1)] = here[1:] + (d[:-1] + d[1:]) * 0.25
        else:
            back = jnp.concatenate([d_prev, d[:-1]], axis=0)
            values[level + 1][pl.ds(at, step)] = here + (back + d) * 0.25
        d_prev = d[step - 1 :]
    values[level + 1][0] = e_zero + (before(d_prev[0], lane) + d_zero) * 0.25


def inverse(values, details, level, lane, keep, before, after):
    pairs = (LANES >> level) // 2
    dst = values[level]
    coarse = values[level + 1]

    def kept(at, count):
        return jnp.where(keep[None], details[level][pl.ds(at, count)], 0.0)

    step = min(CHUNK, pairs)
    back = before(kept(pairs - 1, 1)[0], lane)[None]
    for at in range(0, pairs, step):
        k = kept(at, step)
        shifted = jnp.concatenate([back, k[:-1]], axis=0)
        dst[pl.ds(2 * at, step, stride=2)] = coarse[pl.ds(at, step)] - (shifted + k) * 0.25
        back = k[step - 1 :]
    e_first = dst[pl.ds(0, 2, stride=2)]
    pre = before(dst[2 * pairs - 2], lane)[None]
    post = jnp.stack([after(e_first[0], lane), after(e_first[1], lane)])
    for at in range(0, pairs, step):
        lo, hi = max(at - 1, 0), min(at + step + 2, pairs)
        e = dst[pl.ds(2 * lo, hi - lo, stride=2)]
        if at == 0:
            e = jnp.concatenate([pre, e], axis=0)
        need = step + 3 - e.shape[0]
        if need:
            e = jnp.concatenate([e, post[:need]], axis=0)
        dst[pl.ds(2 * at + 1, step, stride=2)] = kept(at, step) + predict(e)


def transform(values, details, lane, level_of, before, after):
    for level in range(LEVELS):
        forward(values, details, level, lane, before, after)
    for level in reversed(range(LEVELS)):
        inverse(values, details, level, lane, level_of > level, before, after)


def lanes_and_sublanes():
    return (
        lax.broadcasted_iota(jnp.int32, (8, LANES), 1),
        lax.broadcasted_iota(jnp.int32, (8, LANES), 0),
    )


PARTS = 8
PART = LANES // PARTS


def rows_away(value, by):
    return pltpu.roll(value, (-by * SIDES) % LANES, 1) if by else value


def parts_away(here, beyond, by, sublane):
    turn = (-by) % PARTS
    inside = sublane < PARTS - by if by > 0 else sublane >= -by
    return jnp.where(inside, pltpu.roll(here, turn, 0), pltpu.roll(beyond, turn, 0))


def predicted(before, here, after, later):
    return (here + after) * (9.0 / 16.0) - (before + later) * (1.0 / 16.0)


def by_place(values, beyond, place, sublane):
    part, slot = divmod(place, len(values))
    if part == 0:
        return values[slot]
    return parts_away(values[slot], beyond[slot], part, sublane)


class Rows:
    def __init__(self, values, sublane):
        self.values, self.sublane = values, sublane

    def at(self, row, by):
        away, by = (row + by // PARTS, 0) if by % PARTS == 0 else (row, by)
        if by == 0:
            return self.values[away]
        beyond = self.values.get(away + (1 if by > 0 else -1), self.values[away])
        return parts_away(self.values[away], beyond, by, self.sublane)


class Kept:
    def __init__(self, values, sublane):
        self.values, self.sublane, self.seen = values, sublane, {}

    def __getitem__(self, place):
        if place not in self.seen:
            part, slot = divmod(place, len(self.values))
            value = self.values[slot]
            if part:
                beyond = rows_away(value, 1 if part > 0 else -1)
                value = parts_away(value, beyond, part, self.sublane)
            self.seen[place] = value
        return self.seen[place]


def lift_window(inner, outer, level_of, sublane):
    kept = []
    level = 0
    while len(inner) > 1:
        half = len(inner) // 2
        halves = []
        for mine, other in ((inner, outer), (outer, inner)):
            at = lambda place: by_place(mine, other, place, sublane)
            ahead = [at(2 * i) for i in range(-2, half + 2)]
            detail = [
                at(2 * i + 1) - predicted(*ahead[i + 1 : i + 5]) for i in range(-1, half)
            ]
            scaling = [
                ahead[i + 2] + (detail[i] + detail[i + 1]) * 0.25 for i in range(half)
            ]
            halves.append((detail[1:], scaling))
        kept.append(Kept([jnp.where(level_of > level, d, 0.0) for d in halves[0][0]], sublane))
        inner, outer = halves[0][1], halves[1][1]
        level += 1
    levels = {row: rows_away(level_of, row) for row in range(-2, 3)}
    line = Rows({row: rows_away(inner[0], row) for row in range(-4, 5)}, sublane)
    inside = []
    for apart, reach, held in ((1, 3, 1), (2, 2, 2)):
        scaling = {}
        for row in range(-reach, reach + 1):
            at = lambda by: line.at(row, by * apart)
            scaling[row] = (
                at(0) * (23.0 / 32.0)
                + (at(-1) + at(1)) * 0.25
                - (at(-2) + at(2)) * 0.125
                + (at(-4) + at(4)) * (1.0 / 64.0)
            )
        details = {}
        for row in range(-held, held + 1):
            at = lambda by: line.at(row, by * apart)
            detail = at(0) - predicted(at(-3), at(-1), at(1), at(3))
            details[row] = jnp.where(levels[row] > level, detail, 0.0)
        inside.append(Rows(details, sublane))
        line = Rows(scaling, sublane)
        level += 1
    for apart in (2, 1):
        k = inside.pop()
        values = {}
        for row in (-1, 0, 1):
            at = lambda by: k.at(row, by * apart)
            even = line.at(row, 0) - (at(-1) + at(1)) * 0.25
            odd = (
                at(0) * (23.0 / 32.0)
                - (at(-2) + at(2)) * 0.125
                + (at(-4) + at(4)) * (1.0 / 64.0)
                + predicted(*(line.at(row, by * apart) for by in (-3, -1, 1, 3)))
            )
            values[row] = jnp.where(sublane % (2 * apart) == 0, even, odd)
        line = Rows(values, sublane)
    wanted = [range(0, PART)]
    for _ in kept:
        low = [n // 2 - 1 if n % 2 else n // 2 for n in wanted[-1]]
        high = [n // 2 + 2 if n % 2 else n // 2 for n in wanted[-1]]
        wanted.append(range(min(low), max(high) + 1))
    current = {place: line.at(0, place) for place in wanted.pop()}
    while kept:
        k = kept.pop()
        even = {i: value - (k[i - 1] + k[i]) * 0.25 for i, value in current.items()}
        current = {}
        for n in wanted.pop():
            i = n // 2
            if n % 2:
                current[n] = k[i] + predicted(even[i - 1], even[i], even[i + 1], even[i + 2])
            else:
                current[n] = even[i]
    return [current[n] for n in range(PART)]


def exchange_kernel(sizes, x_ref, refine_ref, ob, win, level_ref, xb, near_level, *rest):
    values, details = rest[: LEVELS + 1], rest[LEVELS + 1 : 2 * LEVELS + 1]
    in_sem, send_sem, recv_sem, level_send_sem, level_recv_sem, here_sem = rest[2 * LEVELS + 1 :]
    rows = x_ref.shape[0]
    me, left, right = neighbours(sizes)
    left_seam, right_seam = on_seam(me, sizes), on_seam(right, sizes)
    barrier = pltpu.get_barrier_semaphore()
    pl.semaphore_signal(barrier, inc=1, device_id=left, device_id_type=MESH)

    @pl.when(jnp.logical_not(right_seam))
    def _():
        pl.semaphore_signal(barrier, inc=1, device_id=right, device_id_type=MESH)

    def remote(src, dst, sent, come, device):
        return pltpu.make_async_remote_copy(
            src_ref=src,
            dst_ref=dst,
            send_sem=sent,
            recv_sem=come,
            device_id=device,
            device_id_type=MESH,
        )

    low, high = pl.ds(0, COMP), pl.ds(COMP, COMP)
    level_right = remote(
        refine_ref, near_level.at[0], level_send_sem.at[0], level_recv_sem.at[0], right
    )
    level_left = remote(refine_ref, near_level.at[1], level_send_sem.at[1], level_recv_sem.at[1], left)
    to_right = [
        remote(
            x_ref.at[pl.ds(rows - HALO, HALO)], win.at[pl.ds(0, HALO), low, :], send_sem, recv_sem, right
        ),
        level_right,
    ]
    to_left = [
        remote(
            x_ref.at[pl.ds(0, HALO)], win.at[pl.ds(2 * HALO, HALO), high, :], send_sem, recv_sem, left
        ),
        level_left,
    ]
    pl.semaphore_wait(barrier, jnp.where(left_seam, 1, 2))
    for copy in to_right:
        copy.start()

    @pl.when(right_seam)
    def _():
        pl.semaphore_signal(here_sem, inc=1, device_id=right, device_id_type=MESH)

    @pl.when(jnp.logical_not(left_seam))
    def _():
        for copy in to_left:
            copy.start()

    for c in range(COMP):
        pltpu.make_async_copy(x_ref.at[:, c, :], xb.at[c], in_sem).start()
    pltpu.make_async_copy(xb, xb, in_sem).wait()

    lane, sublane = lanes_and_sublanes()
    own = refine_ref[0]
    for c in range(COMP):
        win[pl.ds(HALO, 2 * HALO), c, :] = xb[c, pl.ds(0, 2 * HALO), :]
        win[pl.ds(0, 2 * HALO), COMP + c, :] = xb[c, pl.ds(rows - 2 * HALO, 2 * HALO), :]
    for c in range(COMP):
        for half in range(2):
            values[0][:, 2 * c + half, :] = xb[c, pl.ds(half * LANES, LANES), :].T
    transform(
        values, details, lane, jnp.full((8, LANES), own, jnp.int32), before_with_carry, after_with_carry
    )
    for c in range(COMP):
        for half in range(2):
            ob[c, pl.ds(half * LANES, LANES), :] = values[0][:, 2 * c + half, :].T

    @pl.when(left_seam)
    def _():
        pl.semaphore_wait(here_sem, 1)
        for copy in to_left:
            copy.start()

    wait_for_rows(2 * HALO * COMP, xb, send_sem)
    level_right.wait_send()
    level_left.wait_send()
    level_right.wait_recv()
    level_left.wait_recv()
    wait_for_rows(2 * HALO * COMP, xb, recv_sem)
    side, row = lane % SIDES, lane // SIDES
    from_left = (side < COMP) & (row < HALO)
    from_right = (side >= COMP) & (row >= 2 * HALO)
    level_ref[...] = jnp.where(
        from_left, near_level[0, 0], jnp.where(from_right, near_level[1, 0], own)
    )


def ends_kernel(ob, win, level_ref, out_ref, wout, turned, beyond, out_sem):
    rows = out_ref.shape[0]
    for c in range(COMP):
        pltpu.make_async_copy(
            ob.at[c, pl.ds(HALO, rows - 2 * HALO), :],
            out_ref.at[pl.ds(HALO, rows - 2 * HALO), c, :],
            out_sem,
        ).start()
    lane, sublane = lanes_and_sublanes()
    used = WIN * SIDES
    rows_here = win[...]
    rows_next = jnp.concatenate([rows_here[1:], rows_here[:1]], axis=0)
    rows_last = jnp.concatenate([rows_here[WIN - 1 :], rows_here[: WIN - 1]], axis=0)
    cell = lax.broadcasted_iota(jnp.int32, rows_here.shape, 2)
    around = jnp.where(cell < LANES // 2, rows_next, rows_last)
    turned[:, :used] = rows_here.reshape(used, LANES).T
    beyond[:, :used] = around.reshape(used, LANES).T
    inner = [turned[pl.ds(k, PARTS, stride=PART), :] for k in range(PART)]
    outer = [beyond[pl.ds(k, PARTS, stride=PART), :] for k in range(PART)]
    for k, value in enumerate(lift_window(inner, outer, level_ref[...], sublane)):
        turned[pl.ds(k, PARTS, stride=PART), :] = value
    redone = turned[...].T[HALO * SIDES : 2 * HALO * SIDES]
    wout[...] = redone.reshape(HALO, SIDES, LANES)
    for side, first in ((0, 0), (1, rows - HALO)):
        pltpu.make_async_copy(
            wout.at[:, pl.ds(side * COMP, COMP), :], out_ref.at[pl.ds(first, HALO)], out_sem
        ).start()
    pltpu.make_async_copy(ob, ob, out_sem).wait()


def lifting_scratch():
    f32 = jnp.float32
    return [pltpu.VMEM((LANES >> level, 8, LANES), f32) for level in range(LEVELS + 1)] + [
        pltpu.VMEM(((LANES >> level) // 2, 8, LANES), f32) for level in range(LEVELS)
    ]


def per_device(sizes, velocity, refine):
    rows = velocity.shape[1] // LANES
    x = velocity.reshape(COMP, rows, LANES).transpose(1, 0, 2)
    x = pltpu.with_memory_space_constraint(x, pltpu.HBM)
    f32 = jnp.float32
    vmem = pl.BlockSpec(memory_space=pltpu.VMEM)
    ob, win, level_of = pl.pallas_call(
        functools.partial(exchange_kernel, sizes),
        out_shape=[
            jax.ShapeDtypeStruct((COMP, rows, LANES), f32),
            jax.ShapeDtypeStruct((WIN, SIDES, LANES), f32),
            jax.ShapeDtypeStruct((8, LANES), jnp.int32),
        ],
        in_specs=[pl.BlockSpec(memory_space=pltpu.HBM), pl.BlockSpec(memory_space=pltpu.SMEM)],
        out_specs=[vmem] * 3,
        scratch_shapes=[
            pltpu.VMEM((COMP, rows, LANES), f32),
            pltpu.SMEM((2, 1), jnp.int32),
        ]
        + lifting_scratch()
        + [
            pltpu.SemaphoreType.DMA,
            pltpu.SemaphoreType.DMA,
            pltpu.SemaphoreType.DMA,
            pltpu.SemaphoreType.DMA((2,)),
            pltpu.SemaphoreType.DMA((2,)),
            pltpu.SemaphoreType.REGULAR,
        ],
        compiler_params=pltpu.CompilerParams(
            collective_id=0, has_side_effects=True, vmem_limit_bytes=VMEM_LIMIT
        ),
    )(x, refine)
    out = pl.pallas_call(
        ends_kernel,
        out_shape=jax.ShapeDtypeStruct(x.shape, f32),
        in_specs=[vmem] * 3,
        out_specs=pl.BlockSpec(memory_space=pltpu.HBM),
        scratch_shapes=[
            pltpu.VMEM((HALO, SIDES, LANES), f32),
            pltpu.VMEM((LANES, LANES), f32),
            pltpu.VMEM((LANES, LANES), f32),
            pltpu.SemaphoreType.DMA,
        ],
        compiler_params=pltpu.CompilerParams(vmem_limit_bytes=VMEM_LIMIT),
    )(ob, win, level_of)
    return out.transpose(1, 0, 2).reshape(velocity.shape)


def solution(mesh):
    sizes = tuple(mesh.shape[name] for name in AXES)
    return jax.shard_map(
        functools.partial(per_device, sizes),
        mesh=mesh,
        in_specs=(P(None, AXES), P(AXES)),
        out_specs=P(None, AXES),
        check_vma=False,
    )
```

```python
import functools

import jax
import jax.numpy as jnp
from jax import lax
from jax.experimental import pallas as pl
from jax.experimental.pallas import tpu as pltpu
from jax.sharding import PartitionSpec as P

AXES = ("node", "rank", "chip")
LEVELS = 6
LANES = 128
COMP = 3
MESH = pl.DeviceIdType.MESH
HALO = 3
WIN = 3 * HALO
SIDES = 8
CHUNK = 8
VMEM_LIMIT = 8 << 20


def neighbours(sizes):
    nodes, ranks, chips = sizes
    node, rank, chip = (lax.axis_index(name) for name in AXES)
    first_chip, last_chip = chip == 0, chip == chips - 1
    first, last = first_chip & (rank == 0), last_chip & (rank == ranks - 1)
    left = (
        jnp.where(first, jnp.where(node == 0, nodes - 1, node - 1), node),
        jnp.where(first_chip, jnp.where(rank == 0, ranks - 1, rank - 1), rank),
        jnp.where(first_chip, chips - 1, chip - 1),
    )
    right = (
        jnp.where(last, jnp.where(node == nodes - 1, 0, node + 1), node),
        jnp.where(last_chip, jnp.where(rank == ranks - 1, 0, rank + 1), rank),
        jnp.where(last_chip, 0, chip + 1),
    )
    return (node, rank, chip), left, right


def on_seam(device, sizes):
    _, rank, chip = device
    return ((rank == 0) & (chip == 0)) | ((rank == sizes[1] - 1) & (chip == sizes[2] - 1))


def wait_for_rows(count, buffer, semaphore):
    rows = buffer.at[0, pl.ds(0, count), :]
    pltpu.make_async_copy(rows, rows, semaphore).wait()


def after_with_carry(row, lane):
    rolled = pltpu.roll(row, LANES - 1, 1)
    carried = pltpu.roll(rolled, 7, 0)
    return jnp.where(lane == LANES - 1, carried, rolled)


def before_with_carry(row, lane):
    rolled = pltpu.roll(row, 1, 1)
    carried = pltpu.roll(rolled, 1, 0)
    return jnp.where(lane == 0, carried, rolled)


def predict(e):
    n = e.shape[0] - 3
    return (e[1 : n + 1] + e[2 : n + 2]) * (9.0 / 16.0) - (e[0:n] + e[3 : n + 3]) * (1.0 / 16.0)


def forward(values, details, level, lane, before, after):
    pairs = (LANES >> level) // 2
    src = values[level]
    e_first = src[pl.ds(0, 2, stride=2)]
    pre = before(src[2 * pairs - 2], lane)[None]
    post = jnp.stack([after(e_first[0], lane), after(e_first[1], lane)])
    step = min(CHUNK, pairs)
    d_prev, e_zero, d_zero = None, None, None
    for at in range(0, pairs, step):
        lo, hi = max(at - 1, 0), min(at + step + 2, pairs)
        e = src[pl.ds(2 * lo, hi - lo, stride=2)]
        if at == 0:
            e = jnp.concatenate([pre, e], axis=0)
        need = step + 3 - e.shape[0]
        if need:
            e = jnp.concatenate([e, post[:need]], axis=0)
        d = src[pl.ds(2 * at + 1, step, stride=2)] - predict(e)
        details[level][pl.ds(at, step)] = d
        here = e[1 : step + 1]
        if at == 0:
            e_zero, d_zero = here[0], d[0]
            values[level + 1][pl.ds(1, step - 1)] = here[1:] + (d[:-1] + d[1:]) * 0.25
        else:
            back = jnp.concatenate([d_prev, d[:-1]], axis=0)
            values[level + 1][pl.ds(at, step)] = here + (back + d) * 0.25
        d_prev = d[step - 1 :]
    values[level + 1][0] = e_zero + (before(d_prev[0], lane) + d_zero) * 0.25


def inverse(values, details, level, lane, keep, before, after):
    pairs = (LANES >> level) // 2
    dst = values[level]
    coarse = values[level + 1]

    def kept(at, count):
        return jnp.where(keep[None], details[level][pl.ds(at, count)], 0.0)

    step = min(CHUNK, pairs)
    back = before(kept(pairs - 1, 1)[0], lane)[None]
    for at in range(0, pairs, step):
        k = kept(at, step)
        shifted = jnp.concatenate([back, k[:-1]], axis=0)
        dst[pl.ds(2 * at, step, stride=2)] = coarse[pl.ds(at, step)] - (shifted + k) * 0.25
        back = k[step - 1 :]
    e_first = dst[pl.ds(0, 2, stride=2)]
    pre = before(dst[2 * pairs - 2], lane)[None]
    post = jnp.stack([after(e_first[0], lane), after(e_first[1], lane)])
    for at in range(0, pairs, step):
        lo, hi = max(at - 1, 0), min(at + step + 2, pairs)
        e = dst[pl.ds(2 * lo, hi - lo, stride=2)]
        if at == 0:
            e = jnp.concatenate([pre, e], axis=0)
        need = step + 3 - e.shape[0]
        if need:
            e = jnp.concatenate([e, post[:need]], axis=0)
        dst[pl.ds(2 * at + 1, step, stride=2)] = kept(at, step) + predict(e)


def transform(values, details, lane, level_of, before, after):
    for level in range(LEVELS):
        forward(values, details, level, lane, before, after)
    for level in reversed(range(LEVELS)):
        inverse(values, details, level, lane, level_of > level, before, after)


def lanes_and_sublanes():
    return (
        lax.broadcasted_iota(jnp.int32, (8, LANES), 1),
        lax.broadcasted_iota(jnp.int32, (8, LANES), 0),
    )


PARTS = 8
PART = LANES // PARTS
STRIP_ROWS = (72, 24, 16, 16, 16, 16, 40, 16)
STRIP_FIRST = (-32, -8, -2, -4, -3, -2, -16, -2)


def rows_away(value, by):
    return pltpu.roll(value, (-by * SIDES) % LANES, 1) if by else value


def parts_away(here, beyond, by, sublane):
    turn = (-by) % PARTS
    inside = sublane < PARTS - by if by > 0 else sublane >= -by
    return jnp.where(inside, pltpu.roll(here, turn, 0), pltpu.roll(beyond, turn, 0))


def predicted(before, here, after, later):
    return (here + after) * (9.0 / 16.0) - (before + later) * (1.0 / 16.0)


def both_away(pair, by, sublane):
    here, beyond = pair
    return parts_away(here, beyond, by, sublane), parts_away(beyond, here, by, sublane)


class Strip:
    def __init__(self, buffer, first):
        self.buffer, self.first = buffer, first

    def put(self, place, value, apart=1):
        self.buffer[pl.ds(place - self.first, 8, stride=apart), :] = value

    def get(self, place, apart=1):
        return self.buffer[pl.ds(place - self.first, 8, stride=apart), :]


class Kept:
    def __init__(self, values, sublane):
        self.values, self.sublane, self.seen = values, sublane, {}

    def __getitem__(self, place):
        if place not in self.seen:
            part, slot = divmod(place, len(self.values))
            value = self.values[slot]
            if part:
                beyond = rows_away(value, 1 if part > 0 else -1)
                value = parts_away(value, beyond, part, self.sublane)
            self.seen[place] = value
        return self.seen[place]


def scaled(before, here, after, twice_before, twice_after):
    return here * (23.0 / 32.0) - (before + after) * 0.125 + (twice_before + twice_after) * (1.0 / 64.0)


def lift_strips(value, level_of, buffers):
    line, above, evens, kept, kept_above, back, levels, done = (
        Strip(buffer, first) for buffer, first in zip(buffers, STRIP_FIRST)
    )
    for row in range(-3, 4):
        line.put(row * PARTS, rows_away(value, row))
    for row in range(-2, 3):
        levels.put(row * PARTS, rows_away(level_of, row))

    def approached(strip, first):
        at = lambda by: strip.get(2 * first + by, 2)
        return scaled(at(-2), at(0), at(2), at(-4), at(4)) + (at(-1) + at(1)) * 0.25

    def detailed(strip, first, level, apart):
        at = lambda by: strip.get(2 * first + by, 2)
        detail = at(1) - predicted(at(-2), at(0), at(2), at(4))
        return jnp.where(levels.get(apart * (2 * first + 1), 2 * apart) > level, detail, 0.0)

    for first in (-8, 0, 8):
        above.put(first, approached(line, first))
    for first in (-4, 4):
        kept.put(first, detailed(line, first, LEVELS - 2, 1))
    evens.put(-2, approached(above, -2))
    kept_above.put(-3, detailed(above, -3, LEVELS - 1, 2))
    for y, k, to in ((evens, kept_above, back), (back, kept, done)):
        to.put(-2, y.get(-1) - (k.get(-2) + k.get(-1)) * 0.25, 2)
        to.put(
            -1,
            scaled(k.get(-2), k.get(-1), k.get(0), k.get(-3), k.get(1))
            + predicted(y.get(-2), y.get(-1), y.get(0), y.get(1)),
            2,
        )
    return done


def lift_window(inner, outer, level_of, sublane, buffers):
    kept = []
    level = 0
    pairs = list(zip(inner, outer))
    while len(pairs) > 1:
        even, odd = pairs[0::2], pairs[1::2]
        half = len(even)
        last = both_away(even[-1], -1, sublane)
        ahead = [last] + even + [
            both_away(even[i % half], 1 + i // half, sublane) for i in range(2)
        ]
        detail = [
            tuple(odd[i][n] - predicted(*(e[n] for e in ahead[i : i + 4])) for n in (0, 1))
            for i in range(half)
        ]
        back = [both_away(detail[-1], -1, sublane)] + detail
        pairs = [
            tuple(even[i][n] + (back[i][n] + back[i + 1][n]) * 0.25 for n in (0, 1)) for i in range(half)
        ]
        kept.append(Kept([jnp.where(level_of > level, d[0], 0.0) for d in detail], sublane))
        level += 1
    done = lift_strips(pairs[0][0], level_of, buffers)
    wanted = [range(0, PART)]
    for _ in kept:
        low = [n // 2 - 1 if n % 2 else n // 2 for n in wanted[-1]]
        high = [n // 2 + 2 if n % 2 else n // 2 for n in wanted[-1]]
        wanted.append(range(min(low), max(high) + 1))
    current = {place: done.get(place) for place in wanted.pop()}
    while kept:
        k = kept.pop()
        even = {i: value - (k[i - 1] + k[i]) * 0.25 for i, value in current.items()}
        current = {}
        for n in wanted.pop():
            i = n // 2
            if n % 2:
                current[n] = k[i] + predicted(even[i - 1], even[i], even[i + 1], even[i + 2])
            else:
                current[n] = even[i]
    return [current[n] for n in range(PART)]


def exchange_kernel(sizes, x_ref, refine_ref, ob, win, level_ref, xb, near_level, *rest):
    values, details = rest[: LEVELS + 1], rest[LEVELS + 1 : 2 * LEVELS + 1]
    in_sem, send_sem, recv_sem, level_send_sem, level_recv_sem, here_sem = rest[2 * LEVELS + 1 :]
    rows = x_ref.shape[0]
    me, left, right = neighbours(sizes)
    left_seam, right_seam = on_seam(me, sizes), on_seam(right, sizes)
    barrier = pltpu.get_barrier_semaphore()
    pl.semaphore_signal(barrier, inc=1, device_id=left, device_id_type=MESH)

    @pl.when(jnp.logical_not(right_seam))
    def _():
        pl.semaphore_signal(barrier, inc=1, device_id=right, device_id_type=MESH)

    def remote(src, dst, sent, come, device):
        return pltpu.make_async_remote_copy(
            src_ref=src,
            dst_ref=dst,
            send_sem=sent,
            recv_sem=come,
            device_id=device,
            device_id_type=MESH,
        )

    low, high = pl.ds(0, COMP), pl.ds(COMP, COMP)
    level_right = remote(
        refine_ref, near_level.at[0], level_send_sem, level_recv_sem, right
    )
    level_left = remote(refine_ref, near_level.at[1], level_send_sem, level_recv_sem, left)
    to_right = [
        remote(
            x_ref.at[pl.ds(rows - HALO, HALO)], win.at[pl.ds(0, HALO), low, :], send_sem, recv_sem, right
        ),
        level_right,
    ]
    to_left = [
        remote(
            x_ref.at[pl.ds(0, HALO)], win.at[pl.ds(2 * HALO, HALO), high, :], send_sem, recv_sem, left
        ),
        level_left,
    ]
    pl.semaphore_wait(barrier, jnp.where(left_seam, 1, 2))
    for copy in to_right:
        copy.start()

    @pl.when(right_seam)
    def _():
        pl.semaphore_signal(here_sem, inc=1, device_id=right, device_id_type=MESH)

    @pl.when(jnp.logical_not(left_seam))
    def _():
        for copy in to_left:
            copy.start()

    for c in range(COMP):
        pltpu.make_async_copy(x_ref.at[:, c, :], xb.at[c], in_sem).start()
    pltpu.make_async_copy(xb, xb, in_sem).wait()

    lane, sublane = lanes_and_sublanes()
    own = refine_ref[0]
    for c in range(COMP):
        win[pl.ds(HALO, 2 * HALO), c, :] = xb[c, pl.ds(0, 2 * HALO), :]
        win[pl.ds(0, 2 * HALO), COMP + c, :] = xb[c, pl.ds(rows - 2 * HALO, 2 * HALO), :]
    for c in range(COMP):
        for half in range(2):
            values[0][:, 2 * c + half, :] = xb[c, pl.ds(half * LANES, LANES), :].T
    transform(
        values, details, lane, jnp.full((8, LANES), own, jnp.int32), before_with_carry, after_with_carry
    )
    for c in range(COMP):
        for half in range(2):
            ob[c, pl.ds(half * LANES, LANES), :] = values[0][:, 2 * c + half, :].T

    @pl.when(left_seam)
    def _():
        pl.semaphore_wait(here_sem, 1)
        for copy in to_left:
            copy.start()

    wait_for_rows(2 * HALO * COMP, xb, send_sem)
    for semaphore in (level_send_sem, level_recv_sem):
        pltpu.make_async_copy(near_level, near_level, semaphore).wait()
    wait_for_rows(2 * HALO * COMP, xb, recv_sem)
    side, row = lane % SIDES, lane // SIDES
    from_left = (side < COMP) & (row < HALO)
    from_right = (side >= COMP) & (row >= 2 * HALO)
    level_ref[...] = jnp.where(
        from_left, near_level[0, 0], jnp.where(from_right, near_level[1, 0], own)
    )


def ends_kernel(ob, win, level_ref, out_ref, wout, turned, beyond, out_sem, *strips):
    rows = out_ref.shape[0]
    for c in range(COMP):
        pltpu.make_async_copy(
            ob.at[c, pl.ds(HALO, rows - 2 * HALO), :],
            out_ref.at[pl.ds(HALO, rows - 2 * HALO), c, :],
            out_sem,
        ).start()
    lane, sublane = lanes_and_sublanes()
    used = WIN * SIDES
    rows_here = win[...]
    rows_next = jnp.concatenate([rows_here[1:], rows_here[:1]], axis=0)
    rows_last = jnp.concatenate([rows_here[WIN - 1 :], rows_here[: WIN - 1]], axis=0)
    cell = lax.broadcasted_iota(jnp.int32, rows_here.shape, 2)
    around = jnp.where(cell < LANES // 2, rows_next, rows_last)
    turned[:, :used] = rows_here.reshape(used, LANES).T
    beyond[:, :used] = around.reshape(used, LANES).T
    inner = [turned[pl.ds(k, PARTS, stride=PART), :] for k in range(PART)]
    outer = [beyond[pl.ds(k, PARTS, stride=PART), :] for k in range(PART)]
    for k, value in enumerate(lift_window(inner, outer, level_ref[...], sublane, strips)):
        turned[pl.ds(k, PARTS, stride=PART), :] = value
    redone = turned[...].T[HALO * SIDES : 2 * HALO * SIDES]
    wout[...] = redone.reshape(HALO, SIDES, LANES)
    for side, first in ((0, 0), (1, rows - HALO)):
        pltpu.make_async_copy(
            wout.at[:, pl.ds(side * COMP, COMP), :], out_ref.at[pl.ds(first, HALO)], out_sem
        ).start()
    pltpu.make_async_copy(ob, ob, out_sem).wait()


def lifting_scratch():
    f32 = jnp.float32
    return [pltpu.VMEM((LANES >> level, 8, LANES), f32) for level in range(LEVELS + 1)] + [
        pltpu.VMEM(((LANES >> level) // 2, 8, LANES), f32) for level in range(LEVELS)
    ]


def per_device(sizes, velocity, refine):
    rows = velocity.shape[1] // LANES
    x = velocity.reshape(COMP, rows, LANES).transpose(1, 0, 2)
    x = pltpu.with_memory_space_constraint(x, pltpu.HBM)
    f32 = jnp.float32
    vmem = pl.BlockSpec(memory_space=pltpu.VMEM)
    ob, win, level_of = pl.pallas_call(
        functools.partial(exchange_kernel, sizes),
        out_shape=[
            jax.ShapeDtypeStruct((COMP, rows, LANES), f32),
            jax.ShapeDtypeStruct((WIN, SIDES, LANES), f32),
            jax.ShapeDtypeStruct((8, LANES), jnp.int32),
        ],
        in_specs=[pl.BlockSpec(memory_space=pltpu.HBM), pl.BlockSpec(memory_space=pltpu.SMEM)],
        out_specs=[vmem] * 3,
        scratch_shapes=[
            pltpu.VMEM((COMP, rows, LANES), f32),
            pltpu.SMEM((2, 1), jnp.int32),
        ]
        + lifting_scratch()
        + [
            pltpu.SemaphoreType.DMA,
            pltpu.SemaphoreType.DMA,
            pltpu.SemaphoreType.DMA,
            pltpu.SemaphoreType.DMA,
            pltpu.SemaphoreType.DMA,
            pltpu.SemaphoreType.REGULAR,
        ],
        compiler_params=pltpu.CompilerParams(
            collective_id=0, has_side_effects=True, vmem_limit_bytes=VMEM_LIMIT
        ),
    )(x, refine)
    out = pl.pallas_call(
        ends_kernel,
        out_shape=jax.ShapeDtypeStruct(x.shape, f32),
        in_specs=[vmem] * 3,
        out_specs=pl.BlockSpec(memory_space=pltpu.HBM),
        scratch_shapes=[
            pltpu.VMEM((HALO, SIDES, LANES), f32),
            pltpu.VMEM((LANES, LANES), f32),
            pltpu.VMEM((LANES, LANES), f32),
            pltpu.SemaphoreType.DMA,
        ]
        + [
            pltpu.VMEM((count, LANES), jnp.int32 if first == -16 else f32)
            for count, first in zip(STRIP_ROWS, STRIP_FIRST)
        ],
        compiler_params=pltpu.CompilerParams(vmem_limit_bytes=VMEM_LIMIT),
    )(ob, win, level_of)
    return out.transpose(1, 0, 2).reshape(velocity.shape)


def solution(mesh):
    sizes = tuple(mesh.shape[name] for name in AXES)
    return jax.shard_map(
        functools.partial(per_device, sizes),
        mesh=mesh,
        in_specs=(P(None, AXES), P(AXES)),
        out_specs=P(None, AXES),
        check_vma=False,
    )
```

```python
import functools

import jax
import jax.numpy as jnp
from jax import lax
from jax.experimental import pallas as pl
from jax.experimental.pallas import tpu as pltpu
from jax.sharding import PartitionSpec as P

AXES = ("node", "rank", "chip")
LEVELS = 6
LANES = 128
COMP = 3
MESH = pl.DeviceIdType.MESH
HALO = 3
WIN = 3 * HALO
SIDES = 8
CHUNK = 8
VMEM_LIMIT = 8 << 20


def neighbours(sizes):
    nodes, ranks, chips = sizes
    node, rank, chip = (lax.axis_index(name) for name in AXES)
    first_chip, last_chip = chip == 0, chip == chips - 1
    first, last = first_chip & (rank == 0), last_chip & (rank == ranks - 1)
    left = (
        jnp.where(first, jnp.where(node == 0, nodes - 1, node - 1), node),
        jnp.where(first_chip, jnp.where(rank == 0, ranks - 1, rank - 1), rank),
        jnp.where(first_chip, chips - 1, chip - 1),
    )
    right = (
        jnp.where(last, jnp.where(node == nodes - 1, 0, node + 1), node),
        jnp.where(last_chip, jnp.where(rank == ranks - 1, 0, rank + 1), rank),
        jnp.where(last_chip, 0, chip + 1),
    )
    return (node, rank, chip), left, right


def on_seam(device, sizes):
    _, rank, chip = device
    return ((rank == 0) & (chip == 0)) | ((rank == sizes[1] - 1) & (chip == sizes[2] - 1))


def wait_for_rows(count, buffer, semaphore):
    rows = buffer.at[0, pl.ds(0, count), :]
    pltpu.make_async_copy(rows, rows, semaphore).wait()


def after_with_carry(row, lane):
    rolled = pltpu.roll(row, LANES - 1, 1)
    carried = pltpu.roll(rolled, 7, 0)
    return jnp.where(lane == LANES - 1, carried, rolled)


def before_with_carry(row, lane):
    rolled = pltpu.roll(row, 1, 1)
    carried = pltpu.roll(rolled, 1, 0)
    return jnp.where(lane == 0, carried, rolled)


def predict(e):
    n = e.shape[0] - 3
    return (e[1 : n + 1] + e[2 : n + 2]) * (9.0 / 16.0) - (e[0:n] + e[3 : n + 3]) * (1.0 / 16.0)


def forward(values, details, level, lane, before, after):
    pairs = (LANES >> level) // 2
    src = values[level]
    e_first = src[pl.ds(0, 2, stride=2)]
    pre = before(src[2 * pairs - 2], lane)[None]
    post = jnp.stack([after(e_first[0], lane), after(e_first[1], lane)])
    step = min(CHUNK, pairs)
    d_prev, e_zero, d_zero = None, None, None
    for at in range(0, pairs, step):
        lo, hi = max(at - 1, 0), min(at + step + 2, pairs)
        e = src[pl.ds(2 * lo, hi - lo, stride=2)]
        if at == 0:
            e = jnp.concatenate([pre, e], axis=0)
        need = step + 3 - e.shape[0]
        if need:
            e = jnp.concatenate([e, post[:need]], axis=0)
        d = src[pl.ds(2 * at + 1, step, stride=2)] - predict(e)
        details[level][pl.ds(at, step)] = d
        here = e[1 : step + 1]
        if at == 0:
            e_zero, d_zero = here[0], d[0]
            values[level + 1][pl.ds(1, step - 1)] = here[1:] + (d[:-1] + d[1:]) * 0.25
        else:
            back = jnp.concatenate([d_prev, d[:-1]], axis=0)
            values[level + 1][pl.ds(at, step)] = here + (back + d) * 0.25
        d_prev = d[step - 1 :]
    values[level + 1][0] = e_zero + (before(d_prev[0], lane) + d_zero) * 0.25


def inverse(values, details, level, lane, keep, before, after):
    pairs = (LANES >> level) // 2
    dst = values[level]
    coarse = values[level + 1]

    def kept(at, count):
        return jnp.where(keep[None], details[level][pl.ds(at, count)], 0.0)

    step = min(CHUNK, pairs)
    back = before(kept(pairs - 1, 1)[0], lane)[None]
    for at in range(0, pairs, step):
        k = kept(at, step)
        shifted = jnp.concatenate([back, k[:-1]], axis=0)
        dst[pl.ds(2 * at, step, stride=2)] = coarse[pl.ds(at, step)] - (shifted + k) * 0.25
        back = k[step - 1 :]
    e_first = dst[pl.ds(0, 2, stride=2)]
    pre = before(dst[2 * pairs - 2], lane)[None]
    post = jnp.stack([after(e_first[0], lane), after(e_first[1], lane)])
    for at in range(0, pairs, step):
        lo, hi = max(at - 1, 0), min(at + step + 2, pairs)
        e = dst[pl.ds(2 * lo, hi - lo, stride=2)]
        if at == 0:
            e = jnp.concatenate([pre, e], axis=0)
        need = step + 3 - e.shape[0]
        if need:
            e = jnp.concatenate([e, post[:need]], axis=0)
        dst[pl.ds(2 * at + 1, step, stride=2)] = kept(at, step) + predict(e)


def transform(values, details, lane, level_of, before, after):
    for level in range(LEVELS):
        forward(values, details, level, lane, before, after)
    for level in reversed(range(LEVELS)):
        inverse(values, details, level, lane, level_of > level, before, after)


def lanes_and_sublanes():
    return (
        lax.broadcasted_iota(jnp.int32, (8, LANES), 1),
        lax.broadcasted_iota(jnp.int32, (8, LANES), 0),
    )


PARTS = 8
PART = LANES // PARTS
STRIP_ROWS = (72, 24, 16, 16, 16, 16, 40, 16)
STRIP_FIRST = (-32, -8, -2, -4, -3, -2, -16, -2)


def rows_away(value, by):
    return pltpu.roll(value, (-by * SIDES) % LANES, 1) if by else value


def parts_away(here, beyond, by, sublane):
    turn = (-by) % PARTS
    inside = sublane < PARTS - by if by > 0 else sublane >= -by
    return jnp.where(inside, pltpu.roll(here, turn, 0), pltpu.roll(beyond, turn, 0))


def predicted(before, here, after, later):
    return (here + after) * (9.0 / 16.0) - (before + later) * (1.0 / 16.0)


def both_away(pair, by, sublane):
    here, beyond = pair
    return parts_away(here, beyond, by, sublane), parts_away(beyond, here, by, sublane)


class Strip:
    def __init__(self, buffer, first):
        self.buffer, self.first = buffer, first

    def put(self, place, value, apart=1):
        self.buffer[pl.ds(place - self.first, 8, stride=apart), :] = value

    def get(self, place, apart=1):
        return self.buffer[pl.ds(place - self.first, 8, stride=apart), :]


class Kept:
    def __init__(self, values, sublane):
        self.values, self.sublane, self.seen = values, sublane, {}

    def __getitem__(self, place):
        if place not in self.seen:
            part, slot = divmod(place, len(self.values))
            value = self.values[slot]
            if part:
                beyond = rows_away(value, 1 if part > 0 else -1)
                value = parts_away(value, beyond, part, self.sublane)
            self.seen[place] = value
        return self.seen[place]


def scaled(before, here, after, twice_before, twice_after):
    return here * (23.0 / 32.0) - (before + after) * 0.125 + (twice_before + twice_after) * (1.0 / 64.0)


def lift_strips(value, level_of, buffers):
    line, above, evens, kept, kept_above, back, levels, done = (
        Strip(buffer, first) for buffer, first in zip(buffers, STRIP_FIRST)
    )
    for row in range(-3, 4):
        line.put(row * PARTS, rows_away(value, row))
    for row in range(-2, 3):
        levels.put(row * PARTS, rows_away(level_of, row))

    def approached(strip, first):
        at = lambda by: strip.get(2 * first + by, 2)
        return scaled(at(-2), at(0), at(2), at(-4), at(4)) + (at(-1) + at(1)) * 0.25

    def detailed(strip, first, level, apart):
        at = lambda by: strip.get(2 * first + by, 2)
        detail = at(1) - predicted(at(-2), at(0), at(2), at(4))
        return jnp.where(levels.get(apart * (2 * first + 1), 2 * apart) > level, detail, 0.0)

    for first in (-8, 0, 8):
        above.put(first, approached(line, first))
    for first in (-4, 4):
        kept.put(first, detailed(line, first, LEVELS - 2, 1))
    evens.put(-2, approached(above, -2))
    kept_above.put(-3, detailed(above, -3, LEVELS - 1, 2))
    for y, k, to in ((evens, kept_above, back), (back, kept, done)):
        to.put(-2, y.get(-1) - (k.get(-2) + k.get(-1)) * 0.25, 2)
        to.put(
            -1,
            scaled(k.get(-2), k.get(-1), k.get(0), k.get(-3), k.get(1))
            + predicted(y.get(-2), y.get(-1), y.get(0), y.get(1)),
            2,
        )
    return done


def lift_window(inner, outer, level_of, sublane, buffers):
    kept = []
    level = 0
    pairs = list(zip(inner, outer))
    while len(pairs) > 1:
        even, odd = pairs[0::2], pairs[1::2]
        half = len(even)
        last = both_away(even[-1], -1, sublane)
        ahead = [last] + even + [
            both_away(even[i % half], 1 + i // half, sublane) for i in range(2)
        ]
        detail = [
            tuple(odd[i][n] - predicted(*(e[n] for e in ahead[i : i + 4])) for n in (0, 1))
            for i in range(half)
        ]
        back = [both_away(detail[-1], -1, sublane)] + detail
        pairs = [
            tuple(even[i][n] + (back[i][n] + back[i + 1][n]) * 0.25 for n in (0, 1)) for i in range(half)
        ]
        kept.append(Kept([jnp.where(level_of > level, d[0], 0.0) for d in detail], sublane))
        level += 1
    done = lift_strips(pairs[0][0], level_of, buffers)
    wanted = [range(0, PART)]
    for _ in kept:
        low = [n // 2 - 1 if n % 2 else n // 2 for n in wanted[-1]]
        high = [n // 2 + 2 if n % 2 else n // 2 for n in wanted[-1]]
        wanted.append(range(min(low), max(high) + 1))
    current = {place: done.get(place) for place in wanted.pop()}
    while kept:
        k = kept.pop()
        even = {i: value - (k[i - 1] + k[i]) * 0.25 for i, value in current.items()}
        current = {}
        for n in wanted.pop():
            i = n // 2
            if n % 2:
                current[n] = k[i] + predicted(even[i - 1], even[i], even[i + 1], even[i + 2])
            else:
                current[n] = even[i]
    return [current[n] for n in range(PART)]


def exchange_kernel(sizes, x_ref, refine_ref, ob, win, level_ref, xb, near_level, *rest):
    values, details = rest[: LEVELS + 1], rest[LEVELS + 1 : 2 * LEVELS + 1]
    in_sem, send_sem, recv_sem, level_send_sem, level_recv_sem, here_sem = rest[2 * LEVELS + 1 :]
    rows = x_ref.shape[0]
    me, left, right = neighbours(sizes)
    left_seam, right_seam = on_seam(me, sizes), on_seam(right, sizes)
    barrier = pltpu.get_barrier_semaphore()
    pl.semaphore_signal(barrier, inc=1, device_id=left, device_id_type=MESH)

    @pl.when(jnp.logical_not(right_seam))
    def _():
        pl.semaphore_signal(barrier, inc=1, device_id=right, device_id_type=MESH)

    def remote(src, dst, sent, come, device):
        return pltpu.make_async_remote_copy(
            src_ref=src,
            dst_ref=dst,
            send_sem=sent,
            recv_sem=come,
            device_id=device,
            device_id_type=MESH,
        )

    low, high = pl.ds(0, COMP), pl.ds(COMP, COMP)
    level_right = remote(
        refine_ref, near_level.at[0], level_send_sem, level_recv_sem, right
    )
    level_left = remote(refine_ref, near_level.at[1], level_send_sem, level_recv_sem, left)
    to_right = [
        remote(
            x_ref.at[pl.ds(rows - HALO, HALO)], win.at[pl.ds(0, HALO), low, :], send_sem, recv_sem, right
        ),
        level_right,
    ]
    to_left = [
        remote(
            x_ref.at[pl.ds(0, HALO)], win.at[pl.ds(2 * HALO, HALO), high, :], send_sem, recv_sem, left
        ),
        level_left,
    ]
    pl.semaphore_wait(barrier, jnp.where(left_seam, 1, 2))
    for copy in to_right:
        copy.start()

    @pl.when(right_seam)
    def _():
        pl.semaphore_signal(here_sem, inc=1, device_id=right, device_id_type=MESH)

    @pl.when(jnp.logical_not(left_seam))
    def _():
        for copy in to_left:
            copy.start()

    for c in range(COMP):
        pltpu.make_async_copy(x_ref.at[:, c, :], xb.at[c], in_sem).start()
    pltpu.make_async_copy(xb, xb, in_sem).wait()

    lane, sublane = lanes_and_sublanes()
    own = refine_ref[0]
    for c in range(COMP):
        win[pl.ds(HALO, 2 * HALO), c, :] = xb[c, pl.ds(0, 2 * HALO), :]
        win[pl.ds(0, 2 * HALO), COMP + c, :] = xb[c, pl.ds(rows - 2 * HALO, 2 * HALO), :]
    for c in range(COMP):
        for half in range(2):
            values[0][:, 2 * c + half, :] = xb[c, pl.ds(half * LANES, LANES), :].T
    transform(
        values, details, lane, jnp.full((8, LANES), own, jnp.int32), before_with_carry, after_with_carry
    )
    for c in range(COMP):
        for half in range(2):
            ob[c, pl.ds(half * LANES, LANES), :] = values[0][:, 2 * c + half, :].T

    @pl.when(left_seam)
    def _():
        pl.semaphore_wait(here_sem, 1)
        for c in range(COMP):
            remote(
                xb.at[c, pl.ds(0, HALO), :],
                win.at[pl.ds(2 * HALO, HALO), COMP + c, :],
                send_sem,
                recv_sem,
                left,
            ).start()
        level_left.start()

    wait_for_rows(2 * HALO * COMP, xb, send_sem)
    for semaphore in (level_send_sem, level_recv_sem):
        pltpu.make_async_copy(near_level, near_level, semaphore).wait()
    wait_for_rows(2 * HALO * COMP, xb, recv_sem)
    side, row = lane % SIDES, lane // SIDES
    from_left = (side < COMP) & (row < HALO)
    from_right = (side >= COMP) & (row >= 2 * HALO)
    level_ref[...] = jnp.where(
        from_left, near_level[0, 0], jnp.where(from_right, near_level[1, 0], own)
    )


def ends_kernel(ob, win, level_ref, out_ref, wout, turned, beyond, out_sem, *strips):
    rows = out_ref.shape[0]
    for c in range(COMP):
        pltpu.make_async_copy(
            ob.at[c, pl.ds(HALO, rows - 2 * HALO), :],
            out_ref.at[pl.ds(HALO, rows - 2 * HALO), c, :],
            out_sem,
        ).start()
    lane, sublane = lanes_and_sublanes()
    used = WIN * SIDES
    rows_here = win[...]
    rows_next = jnp.concatenate([rows_here[1:], rows_here[:1]], axis=0)
    rows_last = jnp.concatenate([rows_here[WIN - 1 :], rows_here[: WIN - 1]], axis=0)
    cell = lax.broadcasted_iota(jnp.int32, rows_here.shape, 2)
    around = jnp.where(cell < LANES // 2, rows_next, rows_last)
    turned[:, :used] = rows_here.reshape(used, LANES).T
    beyond[:, :used] = around.reshape(used, LANES).T
    inner = [turned[pl.ds(k, PARTS, stride=PART), :] for k in range(PART)]
    outer = [beyond[pl.ds(k, PARTS, stride=PART), :] for k in range(PART)]
    for k, value in enumerate(lift_window(inner, outer, level_ref[...], sublane, strips)):
        turned[pl.ds(k, PARTS, stride=PART), :] = value
    redone = turned[...].T[HALO * SIDES : 2 * HALO * SIDES]
    wout[...] = redone.reshape(HALO, SIDES, LANES)
    for side, first in ((0, 0), (1, rows - HALO)):
        pltpu.make_async_copy(
            wout.at[:, pl.ds(side * COMP, COMP), :], out_ref.at[pl.ds(first, HALO)], out_sem
        ).start()
    pltpu.make_async_copy(ob, ob, out_sem).wait()


def lifting_scratch():
    f32 = jnp.float32
    return [pltpu.VMEM((LANES >> level, 8, LANES), f32) for level in range(LEVELS + 1)] + [
        pltpu.VMEM(((LANES >> level) // 2, 8, LANES), f32) for level in range(LEVELS)
    ]


def per_device(sizes, velocity, refine):
    rows = velocity.shape[1] // LANES
    x = velocity.reshape(COMP, rows, LANES).transpose(1, 0, 2)
    x = pltpu.with_memory_space_constraint(x, pltpu.HBM)
    f32 = jnp.float32
    vmem = pl.BlockSpec(memory_space=pltpu.VMEM)
    ob, win, level_of = pl.pallas_call(
        functools.partial(exchange_kernel, sizes),
        out_shape=[
            jax.ShapeDtypeStruct((COMP, rows, LANES), f32),
            jax.ShapeDtypeStruct((WIN, SIDES, LANES), f32),
            jax.ShapeDtypeStruct((8, LANES), jnp.int32),
        ],
        in_specs=[pl.BlockSpec(memory_space=pltpu.HBM), pl.BlockSpec(memory_space=pltpu.SMEM)],
        out_specs=[vmem] * 3,
        scratch_shapes=[
            pltpu.VMEM((COMP, rows, LANES), f32),
            pltpu.SMEM((2, 1), jnp.int32),
        ]
        + lifting_scratch()
        + [
            pltpu.SemaphoreType.DMA,
            pltpu.SemaphoreType.DMA,
            pltpu.SemaphoreType.DMA,
            pltpu.SemaphoreType.DMA,
            pltpu.SemaphoreType.DMA,
            pltpu.SemaphoreType.REGULAR,
        ],
        compiler_params=pltpu.CompilerParams(
            collective_id=0, has_side_effects=True, vmem_limit_bytes=VMEM_LIMIT
        ),
    )(x, refine)
    out = pl.pallas_call(
        ends_kernel,
        out_shape=jax.ShapeDtypeStruct(x.shape, f32),
        in_specs=[vmem] * 3,
        out_specs=pl.BlockSpec(memory_space=pltpu.HBM),
        scratch_shapes=[
            pltpu.VMEM((HALO, SIDES, LANES), f32),
            pltpu.VMEM((LANES, LANES), f32),
            pltpu.VMEM((LANES, LANES), f32),
            pltpu.SemaphoreType.DMA,
        ]
        + [
            pltpu.VMEM((count, LANES), jnp.int32 if first == -16 else f32)
            for count, first in zip(STRIP_ROWS, STRIP_FIRST)
        ],
        compiler_params=pltpu.CompilerParams(vmem_limit_bytes=VMEM_LIMIT),
    )(ob, win, level_of)
    return out.transpose(1, 0, 2).reshape(velocity.shape)


def solution(mesh):
    sizes = tuple(mesh.shape[name] for name in AXES)
    return jax.shard_map(
        functools.partial(per_device, sizes),
        mesh=mesh,
        in_specs=(P(None, AXES), P(AXES)),
        out_specs=P(None, AXES),
        check_vma=False,
    )
```

```python
import functools

import jax
import jax.numpy as jnp
from jax import lax
from jax.experimental import pallas as pl
from jax.experimental.pallas import tpu as pltpu
from jax.sharding import PartitionSpec as P

AXES = ("node", "rank", "chip")
LEVELS = 6
LANES = 128
COMP = 3
LOGICAL = pl.DeviceIdType.LOGICAL
HALO = 3
WIN = 3 * HALO
SIDES = 8
CHUNK = 8
VMEM_LIMIT = 8 << 20


def neighbours(sizes):
    nodes, ranks, chips = sizes
    total = nodes * ranks * chips
    node, rank, chip = (lax.axis_index(name) for name in AXES)
    place = rank * chips + chip
    me = node * (ranks * chips) + place
    left = jnp.where(me == 0, total - 1, me - 1)
    right = jnp.where(me == total - 1, 0, me + 1)
    left_seam = (place == 0) | (place == ranks * chips - 1)
    right_seam = (place == ranks * chips - 1) | (place == ranks * chips - 2)
    return left, right, left_seam, right_seam


def wait_for_rows(count, buffer, semaphore):
    rows = buffer.at[0, pl.ds(0, count), :]
    pltpu.make_async_copy(rows, rows, semaphore).wait()


def after_with_carry(row, lane):
    rolled = pltpu.roll(row, LANES - 1, 1)
    carried = pltpu.roll(rolled, 7, 0)
    return jnp.where(lane == LANES - 1, carried, rolled)


def before_with_carry(row, lane):
    rolled = pltpu.roll(row, 1, 1)
    carried = pltpu.roll(rolled, 1, 0)
    return jnp.where(lane == 0, carried, rolled)


def predict(e):
    n = e.shape[0] - 3
    return (e[1 : n + 1] + e[2 : n + 2]) * (9.0 / 16.0) - (e[0:n] + e[3 : n + 3]) * (1.0 / 16.0)


def forward(values, details, level, lane, before, after):
    pairs = (LANES >> level) // 2
    src = values[level]
    e_first = src[pl.ds(0, 2, stride=2)]
    pre = before(src[2 * pairs - 2], lane)[None]
    post = jnp.stack([after(e_first[0], lane), after(e_first[1], lane)])
    step = min(CHUNK, pairs)
    d_prev, e_zero, d_zero = None, None, None
    for at in range(0, pairs, step):
        lo, hi = max(at - 1, 0), min(at + step + 2, pairs)
        e = src[pl.ds(2 * lo, hi - lo, stride=2)]
        if at == 0:
            e = jnp.concatenate([pre, e], axis=0)
        need = step + 3 - e.shape[0]
        if need:
            e = jnp.concatenate([e, post[:need]], axis=0)
        d = src[pl.ds(2 * at + 1, step, stride=2)] - predict(e)
        details[level][pl.ds(at, step)] = d
        here = e[1 : step + 1]
        if at == 0:
            e_zero, d_zero = here[0], d[0]
            values[level + 1][pl.ds(1, step - 1)] = here[1:] + (d[:-1] + d[1:]) * 0.25
        else:
            back = jnp.concatenate([d_prev, d[:-1]], axis=0)
            values[level + 1][pl.ds(at, step)] = here + (back + d) * 0.25
        d_prev = d[step - 1 :]
    values[level + 1][0] = e_zero + (before(d_prev[0], lane) + d_zero) * 0.25


def inverse(values, details, level, lane, keep, before, after):
    pairs = (LANES >> level) // 2
    dst = values[level]
    coarse = values[level + 1]

    def kept(at, count):
        return jnp.where(keep[None], details[level][pl.ds(at, count)], 0.0)

    step = min(CHUNK, pairs)
    back = before(kept(pairs - 1, 1)[0], lane)[None]
    for at in range(0, pairs, step):
        k = kept(at, step)
        shifted = jnp.concatenate([back, k[:-1]], axis=0)
        dst[pl.ds(2 * at, step, stride=2)] = coarse[pl.ds(at, step)] - (shifted + k) * 0.25
        back = k[step - 1 :]
    e_first = dst[pl.ds(0, 2, stride=2)]
    pre = before(dst[2 * pairs - 2], lane)[None]
    post = jnp.stack([after(e_first[0], lane), after(e_first[1], lane)])
    for at in range(0, pairs, step):
        lo, hi = max(at - 1, 0), min(at + step + 2, pairs)
        e = dst[pl.ds(2 * lo, hi - lo, stride=2)]
        if at == 0:
            e = jnp.concatenate([pre, e], axis=0)
        need = step + 3 - e.shape[0]
        if need:
            e = jnp.concatenate([e, post[:need]], axis=0)
        dst[pl.ds(2 * at + 1, step, stride=2)] = kept(at, step) + predict(e)


def transform(values, details, lane, level_of, before, after):
    for level in range(LEVELS):
        forward(values, details, level, lane, before, after)
    for level in reversed(range(LEVELS)):
        inverse(values, details, level, lane, level_of > level, before, after)


def lanes_and_sublanes():
    return (
        lax.broadcasted_iota(jnp.int32, (8, LANES), 1),
        lax.broadcasted_iota(jnp.int32, (8, LANES), 0),
    )


PARTS = 8
PART = LANES // PARTS
STRIP_ROWS = (72, 24, 16, 16, 16, 16, 40, 16)
STRIP_FIRST = (-32, -8, -2, -4, -3, -2, -16, -2)


def rows_away(value, by):
    return pltpu.roll(value, (-by * SIDES) % LANES, 1) if by else value


def parts_away(here, beyond, by, sublane):
    turn = (-by) % PARTS
    inside = sublane < PARTS - by if by > 0 else sublane >= -by
    return jnp.where(inside, pltpu.roll(here, turn, 0), pltpu.roll(beyond, turn, 0))


def predicted(before, here, after, later):
    return (here + after) * (9.0 / 16.0) - (before + later) * (1.0 / 16.0)


def both_away(pair, by, sublane):
    here, beyond = pair
    return parts_away(here, beyond, by, sublane), parts_away(beyond, here, by, sublane)


class Strip:
    def __init__(self, buffer, first):
        self.buffer, self.first = buffer, first

    def put(self, place, value, apart=1):
        self.buffer[pl.ds(place - self.first, 8, stride=apart), :] = value

    def get(self, place, apart=1):
        return self.buffer[pl.ds(place - self.first, 8, stride=apart), :]


class Kept:
    def __init__(self, values, sublane):
        self.values, self.sublane, self.seen = values, sublane, {}

    def __getitem__(self, place):
        if place not in self.seen:
            part, slot = divmod(place, len(self.values))
            value = self.values[slot]
            if part:
                beyond = rows_away(value, 1 if part > 0 else -1)
                value = parts_away(value, beyond, part, self.sublane)
            self.seen[place] = value
        return self.seen[place]


def scaled(before, here, after, twice_before, twice_after):
    return here * (23.0 / 32.0) - (before + after) * 0.125 + (twice_before + twice_after) * (1.0 / 64.0)


def lift_strips(value, level_of, buffers):
    line, above, evens, kept, kept_above, back, levels, done = (
        Strip(buffer, first) for buffer, first in zip(buffers, STRIP_FIRST)
    )
    for row in range(-3, 4):
        line.put(row * PARTS, rows_away(value, row))
    for row in range(-2, 3):
        levels.put(row * PARTS, rows_away(level_of, row))

    def approached(strip, first):
        at = lambda by: strip.get(2 * first + by, 2)
        return scaled(at(-2), at(0), at(2), at(-4), at(4)) + (at(-1) + at(1)) * 0.25

    def detailed(strip, first, level, apart):
        at = lambda by: strip.get(2 * first + by, 2)
        detail = at(1) - predicted(at(-2), at(0), at(2), at(4))
        return jnp.where(levels.get(apart * (2 * first + 1), 2 * apart) > level, detail, 0.0)

    for first in (-8, 0, 8):
        above.put(first, approached(line, first))
    for first in (-4, 4):
        kept.put(first, detailed(line, first, LEVELS - 2, 1))
    evens.put(-2, approached(above, -2))
    kept_above.put(-3, detailed(above, -3, LEVELS - 1, 2))
    for y, k, to in ((evens, kept_above, back), (back, kept, done)):
        to.put(-2, y.get(-1) - (k.get(-2) + k.get(-1)) * 0.25, 2)
        to.put(
            -1,
            scaled(k.get(-2), k.get(-1), k.get(0), k.get(-3), k.get(1))
            + predicted(y.get(-2), y.get(-1), y.get(0), y.get(1)),
            2,
        )
    return done


def lift_window(inner, outer, level_of, sublane, buffers):
    kept = []
    level = 0
    pairs = list(zip(inner, outer))
    while len(pairs) > 1:
        even, odd = pairs[0::2], pairs[1::2]
        half = len(even)
        last = both_away(even[-1], -1, sublane)
        ahead = [last] + even + [
            both_away(even[i % half], 1 + i // half, sublane) for i in range(2)
        ]
        detail = [
            tuple(odd[i][n] - predicted(*(e[n] for e in ahead[i : i + 4])) for n in (0, 1))
            for i in range(half)
        ]
        back = [both_away(detail[-1], -1, sublane)] + detail
        pairs = [
            tuple(even[i][n] + (back[i][n] + back[i + 1][n]) * 0.25 for n in (0, 1)) for i in range(half)
        ]
        kept.append(Kept([jnp.where(level_of > level, d[0], 0.0) for d in detail], sublane))
        level += 1
    done = lift_strips(pairs[0][0], level_of, buffers)
    wanted = [range(0, PART)]
    for _ in kept:
        low = [n // 2 - 1 if n % 2 else n // 2 for n in wanted[-1]]
        high = [n // 2 + 2 if n % 2 else n // 2 for n in wanted[-1]]
        wanted.append(range(min(low), max(high) + 1))
    current = {place: done.get(place) for place in wanted.pop()}
    while kept:
        k = kept.pop()
        even = {i: value - (k[i - 1] + k[i]) * 0.25 for i, value in current.items()}
        current = {}
        for n in wanted.pop():
            i = n // 2
            if n % 2:
                current[n] = k[i] + predicted(even[i - 1], even[i], even[i + 1], even[i + 2])
            else:
                current[n] = even[i]
    return [current[n] for n in range(PART)]


def exchange_kernel(sizes, x_ref, refine_ref, ob, win, level_ref, xb, near_level, *rest):
    values, details = rest[: LEVELS + 1], rest[LEVELS + 1 : 2 * LEVELS + 1]
    in_sem, send_sem, recv_sem, level_send_sem, level_recv_sem, here_sem = rest[2 * LEVELS + 1 :]
    rows = x_ref.shape[0]
    left, right, left_seam, right_seam = neighbours(sizes)
    barrier = pltpu.get_barrier_semaphore()
    pl.semaphore_signal(barrier, inc=1, device_id=left, device_id_type=LOGICAL)

    @pl.when(jnp.logical_not(right_seam))
    def _():
        pl.semaphore_signal(barrier, inc=1, device_id=right, device_id_type=LOGICAL)

    def remote(src, dst, sent, come, device):
        return pltpu.make_async_remote_copy(
            src_ref=src,
            dst_ref=dst,
            send_sem=sent,
            recv_sem=come,
            device_id=device,
            device_id_type=LOGICAL,
        )

    low, high = pl.ds(0, COMP), pl.ds(COMP, COMP)
    level_right = remote(
        refine_ref, near_level.at[0], level_send_sem, level_recv_sem, right
    )
    level_left = remote(refine_ref, near_level.at[1], level_send_sem, level_recv_sem, left)
    to_right = [
        remote(
            x_ref.at[pl.ds(rows - HALO, HALO)], win.at[pl.ds(0, HALO), low, :], send_sem, recv_sem, right
        ),
        level_right,
    ]
    to_left = [
        remote(
            x_ref.at[pl.ds(0, HALO)], win.at[pl.ds(2 * HALO, HALO), high, :], send_sem, recv_sem, left
        ),
        level_left,
    ]
    pl.semaphore_wait(barrier, jnp.where(left_seam, 1, 2))
    for copy in to_right:
        copy.start()

    @pl.when(right_seam)
    def _():
        pl.semaphore_signal(here_sem, inc=1, device_id=right, device_id_type=LOGICAL)

    @pl.when(jnp.logical_not(left_seam))
    def _():
        for copy in to_left:
            copy.start()

    for c in range(COMP):
        pltpu.make_async_copy(x_ref.at[:, c, :], xb.at[c], in_sem).start()
    pltpu.make_async_copy(xb, xb, in_sem).wait()

    lane, sublane = lanes_and_sublanes()
    own = refine_ref[0]
    for c in range(COMP):
        win[pl.ds(HALO, 2 * HALO), c, :] = xb[c, pl.ds(0, 2 * HALO), :]
        win[pl.ds(0, 2 * HALO), COMP + c, :] = xb[c, pl.ds(rows - 2 * HALO, 2 * HALO), :]
    for c in range(COMP):
        for half in range(2):
            values[0][:, 2 * c + half, :] = xb[c, pl.ds(half * LANES, LANES), :].T
    transform(
        values, details, lane, jnp.full((8, LANES), own, jnp.int32), before_with_carry, after_with_carry
    )
    for c in range(COMP):
        for half in range(2):
            ob[c, pl.ds(half * LANES, LANES), :] = values[0][:, 2 * c + half, :].T

    @pl.when(left_seam)
    def _():
        pl.semaphore_wait(here_sem, 1)
        for c in range(COMP):
            remote(
                xb.at[c, pl.ds(0, HALO), :],
                win.at[pl.ds(2 * HALO, HALO), COMP + c, :],
                send_sem,
                recv_sem,
                left,
            ).start()
        level_left.start()

    wait_for_rows(2 * HALO * COMP, xb, send_sem)
    for semaphore in (level_send_sem, level_recv_sem):
        pltpu.make_async_copy(near_level, near_level, semaphore).wait()
    wait_for_rows(2 * HALO * COMP, xb, recv_sem)
    side, row = lane % SIDES, lane // SIDES
    from_left = (side < COMP) & (row < HALO)
    from_right = (side >= COMP) & (row >= 2 * HALO)
    level_ref[...] = jnp.where(
        from_left, near_level[0, 0], jnp.where(from_right, near_level[1, 0], own)
    )


def ends_kernel(ob, win, level_ref, out_ref, wout, turned, beyond, out_sem, *strips):
    rows = out_ref.shape[0]
    for c in range(COMP):
        pltpu.make_async_copy(
            ob.at[c, pl.ds(HALO, rows - 2 * HALO), :],
            out_ref.at[pl.ds(HALO, rows - 2 * HALO), c, :],
            out_sem,
        ).start()
    lane, sublane = lanes_and_sublanes()
    used = WIN * SIDES
    rows_here = win[...]
    rows_next = jnp.concatenate([rows_here[1:], rows_here[:1]], axis=0)
    rows_last = jnp.concatenate([rows_here[WIN - 1 :], rows_here[: WIN - 1]], axis=0)
    cell = lax.broadcasted_iota(jnp.int32, rows_here.shape, 2)
    around = jnp.where(cell < LANES // 2, rows_next, rows_last)
    turned[:, :used] = rows_here.reshape(used, LANES).T
    beyond[:, :used] = around.reshape(used, LANES).T
    inner = [turned[pl.ds(k, PARTS, stride=PART), :] for k in range(PART)]
    outer = [beyond[pl.ds(k, PARTS, stride=PART), :] for k in range(PART)]
    for k, value in enumerate(lift_window(inner, outer, level_ref[...], sublane, strips)):
        turned[pl.ds(k, PARTS, stride=PART), :] = value
    redone = turned[...].T[HALO * SIDES : 2 * HALO * SIDES]
    wout[...] = redone.reshape(HALO, SIDES, LANES)
    for side, first in ((0, 0), (1, rows - HALO)):
        pltpu.make_async_copy(
            wout.at[:, pl.ds(side * COMP, COMP), :], out_ref.at[pl.ds(first, HALO)], out_sem
        ).start()
    pltpu.make_async_copy(ob, ob, out_sem).wait()


def lifting_scratch():
    f32 = jnp.float32
    return [pltpu.VMEM((LANES >> level, 8, LANES), f32) for level in range(LEVELS + 1)] + [
        pltpu.VMEM(((LANES >> level) // 2, 8, LANES), f32) for level in range(LEVELS)
    ]


def per_device(sizes, velocity, refine):
    rows = velocity.shape[1] // LANES
    x = velocity.reshape(COMP, rows, LANES).transpose(1, 0, 2)
    x = pltpu.with_memory_space_constraint(x, pltpu.HBM)
    f32 = jnp.float32
    vmem = pl.BlockSpec(memory_space=pltpu.VMEM)
    ob, win, level_of = pl.pallas_call(
        functools.partial(exchange_kernel, sizes),
        out_shape=[
            jax.ShapeDtypeStruct((COMP, rows, LANES), f32),
            jax.ShapeDtypeStruct((WIN, SIDES, LANES), f32),
            jax.ShapeDtypeStruct((8, LANES), jnp.int32),
        ],
        in_specs=[pl.BlockSpec(memory_space=pltpu.HBM), pl.BlockSpec(memory_space=pltpu.SMEM)],
        out_specs=[vmem] * 3,
        scratch_shapes=[
            pltpu.VMEM((COMP, rows, LANES), f32),
            pltpu.SMEM((2, 1), jnp.int32),
        ]
        + lifting_scratch()
        + [
            pltpu.SemaphoreType.DMA,
            pltpu.SemaphoreType.DMA,
            pltpu.SemaphoreType.DMA,
            pltpu.SemaphoreType.DMA,
            pltpu.SemaphoreType.DMA,
            pltpu.SemaphoreType.REGULAR,
        ],
        compiler_params=pltpu.CompilerParams(
            collective_id=0, has_side_effects=True, vmem_limit_bytes=VMEM_LIMIT
        ),
    )(x, refine)
    out = pl.pallas_call(
        ends_kernel,
        out_shape=jax.ShapeDtypeStruct(x.shape, f32),
        in_specs=[vmem] * 3,
        out_specs=pl.BlockSpec(memory_space=pltpu.HBM),
        scratch_shapes=[
            pltpu.VMEM((HALO, SIDES, LANES), f32),
            pltpu.VMEM((LANES, LANES), f32),
            pltpu.VMEM((LANES, LANES), f32),
            pltpu.SemaphoreType.DMA,
        ]
        + [
            pltpu.VMEM((count, LANES), jnp.int32 if first == -16 else f32)
            for count, first in zip(STRIP_ROWS, STRIP_FIRST)
        ],
        compiler_params=pltpu.CompilerParams(vmem_limit_bytes=VMEM_LIMIT),
    )(ob, win, level_of)
    return out.transpose(1, 0, 2).reshape(velocity.shape)


def solution(mesh):
    sizes = tuple(mesh.shape[name] for name in AXES)
    return jax.shard_map(
        functools.partial(per_device, sizes),
        mesh=mesh,
        in_specs=(P(None, AXES), P(AXES)),
        out_specs=P(None, AXES),
        check_vma=False,
    )
```

```python
import functools

import jax
import jax.numpy as jnp
from jax import lax
from jax.experimental import pallas as pl
from jax.experimental.pallas import tpu as pltpu
from jax.sharding import PartitionSpec as P

AXES = ("node", "rank", "chip")
LEVELS = 6
LANES = 128
COMP = 3
LOGICAL = pl.DeviceIdType.LOGICAL
HALO = 3
WIN = 3 * HALO
SIDES = 8
CHUNK = 8
VMEM_LIMIT = 8 << 20


def neighbours(sizes):
    nodes, ranks, chips = sizes
    total = nodes * ranks * chips
    node, rank, chip = (lax.axis_index(name) for name in AXES)
    place = rank * chips + chip
    me = node * (ranks * chips) + place
    left = jnp.where(me == 0, total - 1, me - 1)
    right = jnp.where(me == total - 1, 0, me + 1)
    left_seam = (place == 0) | (place == ranks * chips - 1)
    right_seam = (place == ranks * chips - 1) | (place == ranks * chips - 2)
    return left, right, left_seam, right_seam


def wait_for_rows(count, buffer, semaphore):
    rows = buffer.at[0, pl.ds(0, count), :]
    pltpu.make_async_copy(rows, rows, semaphore).wait()


def after_with_carry(row, lane):
    rolled = pltpu.roll(row, LANES - 1, 1)
    carried = pltpu.roll(rolled, 7, 0)
    return jnp.where(lane == LANES - 1, carried, rolled)


def before_with_carry(row, lane):
    rolled = pltpu.roll(row, 1, 1)
    carried = pltpu.roll(rolled, 1, 0)
    return jnp.where(lane == 0, carried, rolled)


def predict(e):
    n = e.shape[0] - 3
    return (e[1 : n + 1] + e[2 : n + 2]) * (9.0 / 16.0) - (e[0:n] + e[3 : n + 3]) * (1.0 / 16.0)


def forward(values, details, level, lane, before, after):
    pairs = (LANES >> level) // 2
    src = values[level]
    e_first = src[pl.ds(0, 2, stride=2)]
    pre = before(src[2 * pairs - 2], lane)[None]
    post = jnp.stack([after(e_first[0], lane), after(e_first[1], lane)])
    step = min(CHUNK, pairs)
    d_prev, e_zero, d_zero = None, None, None
    for at in range(0, pairs, step):
        lo, hi = max(at - 1, 0), min(at + step + 2, pairs)
        e = src[pl.ds(2 * lo, hi - lo, stride=2)]
        if at == 0:
            e = jnp.concatenate([pre, e], axis=0)
        need = step + 3 - e.shape[0]
        if need:
            e = jnp.concatenate([e, post[:need]], axis=0)
        d = src[pl.ds(2 * at + 1, step, stride=2)] - predict(e)
        details[level][pl.ds(at, step)] = d
        here = e[1 : step + 1]
        if at == 0:
            e_zero, d_zero = here[0], d[0]
            values[level + 1][pl.ds(1, step - 1)] = here[1:] + (d[:-1] + d[1:]) * 0.25
        else:
            back = jnp.concatenate([d_prev, d[:-1]], axis=0)
            values[level + 1][pl.ds(at, step)] = here + (back + d) * 0.25
        d_prev = d[step - 1 :]
    values[level + 1][0] = e_zero + (before(d_prev[0], lane) + d_zero) * 0.25


def inverse(values, details, level, lane, keep, before, after):
    pairs = (LANES >> level) // 2
    dst = values[level]
    coarse = values[level + 1]

    def kept(at, count):
        return jnp.where(keep[None], details[level][pl.ds(at, count)], 0.0)

    step = min(CHUNK, pairs)
    back = before(kept(pairs - 1, 1)[0], lane)[None]
    for at in range(0, pairs, step):
        k = kept(at, step)
        shifted = jnp.concatenate([back, k[:-1]], axis=0)
        dst[pl.ds(2 * at, step, stride=2)] = coarse[pl.ds(at, step)] - (shifted + k) * 0.25
        back = k[step - 1 :]
    e_first = dst[pl.ds(0, 2, stride=2)]
    pre = before(dst[2 * pairs - 2], lane)[None]
    post = jnp.stack([after(e_first[0], lane), after(e_first[1], lane)])
    for at in range(0, pairs, step):
        lo, hi = max(at - 1, 0), min(at + step + 2, pairs)
        e = dst[pl.ds(2 * lo, hi - lo, stride=2)]
        if at == 0:
            e = jnp.concatenate([pre, e], axis=0)
        need = step + 3 - e.shape[0]
        if need:
            e = jnp.concatenate([e, post[:need]], axis=0)
        dst[pl.ds(2 * at + 1, step, stride=2)] = kept(at, step) + predict(e)


def transform(values, details, lane, level_of, before, after):
    for level in range(LEVELS):
        forward(values, details, level, lane, before, after)
    for level in reversed(range(LEVELS)):
        inverse(values, details, level, lane, level_of > level, before, after)


def lanes_and_sublanes():
    return (
        lax.broadcasted_iota(jnp.int32, (8, LANES), 1),
        lax.broadcasted_iota(jnp.int32, (8, LANES), 0),
    )


PARTS = 8
PART = LANES // PARTS
STRIP_ROWS = (72, 24, 16, 16, 16, 16, 40, 16)
STRIP_FIRST = (-32, -8, -2, -4, -3, -2, -16, -2)


def rows_away(value, by):
    return pltpu.roll(value, (-by * SIDES) % LANES, 1) if by else value


def parts_away(here, beyond, by, sublane):
    turn = (-by) % PARTS
    inside = sublane < PARTS - by if by > 0 else sublane >= -by
    return jnp.where(inside, pltpu.roll(here, turn, 0), pltpu.roll(beyond, turn, 0))


def predicted(before, here, after, later):
    return (here + after) * (9.0 / 16.0) - (before + later) * (1.0 / 16.0)


def both_away(pair, by, sublane):
    here, beyond = pair
    return parts_away(here, beyond, by, sublane), parts_away(beyond, here, by, sublane)


class Strip:
    def __init__(self, buffer, first):
        self.buffer, self.first = buffer, first

    def put(self, place, value, apart=1):
        self.buffer[pl.ds(place - self.first, 8, stride=apart), :] = value

    def get(self, place, apart=1):
        return self.buffer[pl.ds(place - self.first, 8, stride=apart), :]


class Kept:
    def __init__(self, values, sublane):
        self.values, self.sublane, self.seen = values, sublane, {}

    def __getitem__(self, place):
        if place not in self.seen:
            part, slot = divmod(place, len(self.values))
            value = self.values[slot]
            if part:
                beyond = rows_away(value, 1 if part > 0 else -1)
                value = parts_away(value, beyond, part, self.sublane)
            self.seen[place] = value
        return self.seen[place]


def scaled(before, here, after, twice_before, twice_after):
    return here * (23.0 / 32.0) - (before + after) * 0.125 + (twice_before + twice_after) * (1.0 / 64.0)


def lift_strips(value, level_of, buffers):
    line, above, evens, kept, kept_above, back, levels, done = (
        Strip(buffer, first) for buffer, first in zip(buffers, STRIP_FIRST)
    )
    for row in range(-3, 4):
        line.put(row * PARTS, rows_away(value, row))
    for row in range(-2, 3):
        levels.put(row * PARTS, rows_away(level_of, row))

    def approached(strip, first):
        at = lambda by: strip.get(2 * first + by, 2)
        return scaled(at(-2), at(0), at(2), at(-4), at(4)) + (at(-1) + at(1)) * 0.25

    def detailed(strip, first, level, apart):
        at = lambda by: strip.get(2 * first + by, 2)
        detail = at(1) - predicted(at(-2), at(0), at(2), at(4))
        return jnp.where(levels.get(apart * (2 * first + 1), 2 * apart) > level, detail, 0.0)

    for first in (-8, 0, 8):
        above.put(first, approached(line, first))
    for first in (-4, 4):
        kept.put(first, detailed(line, first, LEVELS - 2, 1))
    evens.put(-2, approached(above, -2))
    kept_above.put(-3, detailed(above, -3, LEVELS - 1, 2))
    for y, k, to in ((evens, kept_above, back), (back, kept, done)):
        to.put(-2, y.get(-1) - (k.get(-2) + k.get(-1)) * 0.25, 2)
        to.put(
            -1,
            scaled(k.get(-2), k.get(-1), k.get(0), k.get(-3), k.get(1))
            + predicted(y.get(-2), y.get(-1), y.get(0), y.get(1)),
            2,
        )
    return done


def lift_window(inner, outer, level_of, sublane, buffers):
    kept = []
    level = 0
    pairs = list(zip(inner, outer))
    while len(pairs) > 1:
        even, odd = pairs[0::2], pairs[1::2]
        half = len(even)
        last = both_away(even[-1], -1, sublane)
        ahead = [last] + even + [
            both_away(even[i % half], 1 + i // half, sublane) for i in range(2)
        ]
        detail = [
            tuple(odd[i][n] - predicted(*(e[n] for e in ahead[i : i + 4])) for n in (0, 1))
            for i in range(half)
        ]
        back = [both_away(detail[-1], -1, sublane)] + detail
        pairs = [
            tuple(even[i][n] + (back[i][n] + back[i + 1][n]) * 0.25 for n in (0, 1)) for i in range(half)
        ]
        kept.append(Kept([jnp.where(level_of > level, d[0], 0.0) for d in detail], sublane))
        level += 1
    done = lift_strips(pairs[0][0], level_of, buffers)
    wanted = [range(0, PART)]
    for _ in kept:
        low = [n // 2 - 1 if n % 2 else n // 2 for n in wanted[-1]]
        high = [n // 2 + 2 if n % 2 else n // 2 for n in wanted[-1]]
        wanted.append(range(min(low), max(high) + 1))
    current = {place: done.get(place) for place in wanted.pop()}
    while kept:
        k = kept.pop()
        even = {i: value - (k[i - 1] + k[i]) * 0.25 for i, value in current.items()}
        current = {}
        for n in wanted.pop():
            i = n // 2
            if n % 2:
                current[n] = k[i] + predicted(even[i - 1], even[i], even[i + 1], even[i + 2])
            else:
                current[n] = even[i]
    return [current[n] for n in range(PART)]


def exchange_kernel(sizes, x_ref, refine_ref, ob, win, level_ref, xb, near_level, *rest):
    values, details = rest[: LEVELS + 1], rest[LEVELS + 1 : 2 * LEVELS + 1]
    recv_sem, level_recv_sem, here_sem = rest[2 * LEVELS + 1 :]
    rows = x_ref.shape[0]
    left, right, left_seam, right_seam = neighbours(sizes)
    barrier = pltpu.get_barrier_semaphore()
    pl.semaphore_signal(barrier, inc=1, device_id=left, device_id_type=LOGICAL)

    @pl.when(jnp.logical_not(right_seam))
    def _():
        pl.semaphore_signal(barrier, inc=1, device_id=right, device_id_type=LOGICAL)

    lane, sublane = lanes_and_sublanes()
    own = refine_ref[0]
    side, row = lane % SIDES, lane // SIDES
    from_left = (side < COMP) & (row < HALO)
    from_right = (side >= COMP) & (row >= 2 * HALO)

    def send_and_lift(in_sem, send_sem, level_send_sem):
        def remote(src, dst, sent, come, device):
            return pltpu.make_async_remote_copy(
                src_ref=src,
                dst_ref=dst,
                send_sem=sent,
                recv_sem=come,
                device_id=device,
                device_id_type=LOGICAL,
            )

        low, high = pl.ds(0, COMP), pl.ds(COMP, COMP)
        level_right = remote(
            refine_ref, near_level.at[0], level_send_sem, level_recv_sem, right
        )
        level_left = remote(refine_ref, near_level.at[1], level_send_sem, level_recv_sem, left)
        to_right = [
            remote(
                x_ref.at[pl.ds(rows - HALO, HALO)], win.at[pl.ds(0, HALO), low, :], send_sem, recv_sem, right
            ),
            level_right,
        ]
        to_left = [
            remote(
                x_ref.at[pl.ds(0, HALO)], win.at[pl.ds(2 * HALO, HALO), high, :], send_sem, recv_sem, left
            ),
            level_left,
        ]
        pl.semaphore_wait(barrier, jnp.where(left_seam, 1, 2))
        for copy in to_right:
            copy.start()

        @pl.when(right_seam)
        def _():
            pl.semaphore_signal(here_sem, inc=1, device_id=right, device_id_type=LOGICAL)

        @pl.when(jnp.logical_not(left_seam))
        def _():
            for copy in to_left:
                copy.start()

        for c in range(COMP):
            pltpu.make_async_copy(x_ref.at[:, c, :], xb.at[c], in_sem).start()
        pltpu.make_async_copy(xb, xb, in_sem).wait()

        for c in range(COMP):
            win[pl.ds(HALO, 2 * HALO), c, :] = xb[c, pl.ds(0, 2 * HALO), :]
            win[pl.ds(0, 2 * HALO), COMP + c, :] = xb[c, pl.ds(rows - 2 * HALO, 2 * HALO), :]
        for c in range(COMP):
            for half in range(2):
                values[0][:, 2 * c + half, :] = xb[c, pl.ds(half * LANES, LANES), :].T
        transform(
            values, details, lane, jnp.full((8, LANES), own, jnp.int32), before_with_carry, after_with_carry
        )
        for c in range(COMP):
            for half in range(2):
                ob[c, pl.ds(half * LANES, LANES), :] = values[0][:, 2 * c + half, :].T

        @pl.when(left_seam)
        def _():
            pl.semaphore_wait(here_sem, 1)
            for c in range(COMP):
                remote(
                    xb.at[c, pl.ds(0, HALO), :],
                    win.at[pl.ds(2 * HALO, HALO), COMP + c, :],
                    send_sem,
                    recv_sem,
                    left,
                ).start()
            level_left.start()

        wait_for_rows(2 * HALO * COMP, xb, send_sem)
        pltpu.make_async_copy(near_level, near_level, level_send_sem).wait()

    pl.run_scoped(send_and_lift, *[pltpu.SemaphoreType.DMA] * 3)
    pltpu.make_async_copy(near_level, near_level, level_recv_sem).wait()
    wait_for_rows(2 * HALO * COMP, xb, recv_sem)
    level_ref[...] = jnp.where(
        from_left, near_level[0, 0], jnp.where(from_right, near_level[1, 0], own)
    )


def ends_kernel(ob, win, level_ref, out_ref, wout, turned, beyond, out_sem, *strips):
    rows = out_ref.shape[0]
    for c in range(COMP):
        pltpu.make_async_copy(
            ob.at[c, pl.ds(HALO, rows - 2 * HALO), :],
            out_ref.at[pl.ds(HALO, rows - 2 * HALO), c, :],
            out_sem,
        ).start()
    lane, sublane = lanes_and_sublanes()
    used = WIN * SIDES
    rows_here = win[...]
    rows_next = jnp.concatenate([rows_here[1:], rows_here[:1]], axis=0)
    rows_last = jnp.concatenate([rows_here[WIN - 1 :], rows_here[: WIN - 1]], axis=0)
    cell = lax.broadcasted_iota(jnp.int32, rows_here.shape, 2)
    around = jnp.where(cell < LANES // 2, rows_next, rows_last)
    turned[:, :used] = rows_here.reshape(used, LANES).T
    beyond[:, :used] = around.reshape(used, LANES).T
    inner = [turned[pl.ds(k, PARTS, stride=PART), :] for k in range(PART)]
    outer = [beyond[pl.ds(k, PARTS, stride=PART), :] for k in range(PART)]
    for k, value in enumerate(lift_window(inner, outer, level_ref[...], sublane, strips)):
        turned[pl.ds(k, PARTS, stride=PART), :] = value
    redone = turned[...].T[HALO * SIDES : 2 * HALO * SIDES]
    wout[...] = redone.reshape(HALO, SIDES, LANES)
    for side, first in ((0, 0), (1, rows - HALO)):
        pltpu.make_async_copy(
            wout.at[:, pl.ds(side * COMP, COMP), :], out_ref.at[pl.ds(first, HALO)], out_sem
        ).start()
    pltpu.make_async_copy(ob, ob, out_sem).wait()


def lifting_scratch():
    f32 = jnp.float32
    return [pltpu.VMEM((LANES >> level, 8, LANES), f32) for level in range(LEVELS + 1)] + [
        pltpu.VMEM(((LANES >> level) // 2, 8, LANES), f32) for level in range(LEVELS)
    ]


def per_device(sizes, velocity, refine):
    rows = velocity.shape[1] // LANES
    x = velocity.reshape(COMP, rows, LANES).transpose(1, 0, 2)
    x = pltpu.with_memory_space_constraint(x, pltpu.HBM)
    f32 = jnp.float32
    vmem = pl.BlockSpec(memory_space=pltpu.VMEM)
    ob, win, level_of = pl.pallas_call(
        functools.partial(exchange_kernel, sizes),
        out_shape=[
            jax.ShapeDtypeStruct((COMP, rows, LANES), f32),
            jax.ShapeDtypeStruct((WIN, SIDES, LANES), f32),
            jax.ShapeDtypeStruct((8, LANES), jnp.int32),
        ],
        in_specs=[pl.BlockSpec(memory_space=pltpu.HBM), pl.BlockSpec(memory_space=pltpu.SMEM)],
        out_specs=[vmem] * 3,
        scratch_shapes=[
            pltpu.VMEM((COMP, rows, LANES), f32),
            pltpu.SMEM((2, 1), jnp.int32),
        ]
        + lifting_scratch()
        + [
            pltpu.SemaphoreType.DMA,
            pltpu.SemaphoreType.DMA,
            pltpu.SemaphoreType.REGULAR,
        ],
        compiler_params=pltpu.CompilerParams(
            collective_id=0, has_side_effects=True, vmem_limit_bytes=VMEM_LIMIT
        ),
    )(x, refine)
    out = pl.pallas_call(
        ends_kernel,
        out_shape=jax.ShapeDtypeStruct(x.shape, f32),
        in_specs=[vmem] * 3,
        out_specs=pl.BlockSpec(memory_space=pltpu.HBM),
        scratch_shapes=[
            pltpu.VMEM((HALO, SIDES, LANES), f32),
            pltpu.VMEM((LANES, LANES), f32),
            pltpu.VMEM((LANES, LANES), f32),
            pltpu.SemaphoreType.DMA,
        ]
        + [
            pltpu.VMEM((count, LANES), jnp.int32 if first == -16 else f32)
            for count, first in zip(STRIP_ROWS, STRIP_FIRST)
        ],
        compiler_params=pltpu.CompilerParams(vmem_limit_bytes=VMEM_LIMIT),
    )(ob, win, level_of)
    return out.transpose(1, 0, 2).reshape(velocity.shape)


def solution(mesh):
    sizes = tuple(mesh.shape[name] for name in AXES)
    return jax.shard_map(
        functools.partial(per_device, sizes),
        mesh=mesh,
        in_specs=(P(None, AXES), P(AXES)),
        out_specs=P(None, AXES),
        check_vma=False,
    )
```

```python
import functools

import jax
import jax.numpy as jnp
from jax import lax
from jax.experimental import pallas as pl
from jax.experimental.pallas import tpu as pltpu
from jax.sharding import PartitionSpec as P

AXES = ("node", "rank", "chip")
LEVELS = 6
LANES = 128
COMP = 3
LOGICAL = pl.DeviceIdType.LOGICAL
HALO = 3
WIN = 3 * HALO
SIDES = 8
CHUNK = 8
VMEM_LIMIT = 8 << 20


def neighbours(sizes):
    nodes, ranks, chips = sizes
    total = nodes * ranks * chips
    node, rank, chip = (lax.axis_index(name) for name in AXES)
    place = rank * chips + chip
    me = node * (ranks * chips) + place
    left = jnp.where(me == 0, total - 1, me - 1)
    right = jnp.where(me == total - 1, 0, me + 1)
    left_seam = (place == 0) | (place == ranks * chips - 1)
    right_seam = (place == ranks * chips - 1) | (place == ranks * chips - 2)
    return left, right, left_seam, right_seam


def wait_for_rows(count, buffer, semaphore):
    rows = buffer.at[0, pl.ds(0, count), :]
    pltpu.make_async_copy(rows, rows, semaphore).wait()


def after_with_carry(row, lane):
    rolled = pltpu.roll(row, LANES - 1, 1)
    carried = pltpu.roll(rolled, 7, 0)
    return jnp.where(lane == LANES - 1, carried, rolled)


def before_with_carry(row, lane):
    rolled = pltpu.roll(row, 1, 1)
    carried = pltpu.roll(rolled, 1, 0)
    return jnp.where(lane == 0, carried, rolled)


def predict(e):
    n = e.shape[0] - 3
    return (e[1 : n + 1] + e[2 : n + 2]) * (9.0 / 16.0) - (e[0:n] + e[3 : n + 3]) * (1.0 / 16.0)


def forward(values, details, level, lane, before, after):
    pairs = (LANES >> level) // 2
    src = values[level]
    e_first = src[pl.ds(0, 2, stride=2)]
    pre = before(src[2 * pairs - 2], lane)[None]
    post = jnp.stack([after(e_first[0], lane), after(e_first[1], lane)])
    step = min(CHUNK, pairs)
    d_prev, e_zero, d_zero = None, None, None
    for at in range(0, pairs, step):
        lo, hi = max(at - 1, 0), min(at + step + 2, pairs)
        e = src[pl.ds(2 * lo, hi - lo, stride=2)]
        if at == 0:
            e = jnp.concatenate([pre, e], axis=0)
        need = step + 3 - e.shape[0]
        if need:
            e = jnp.concatenate([e, post[:need]], axis=0)
        d = src[pl.ds(2 * at + 1, step, stride=2)] - predict(e)
        details[level][pl.ds(at, step)] = d
        here = e[1 : step + 1]
        if at == 0:
            e_zero, d_zero = here[0], d[0]
            values[level + 1][pl.ds(1, step - 1)] = here[1:] + (d[:-1] + d[1:]) * 0.25
        else:
            back = jnp.concatenate([d_prev, d[:-1]], axis=0)
            values[level + 1][pl.ds(at, step)] = here + (back + d) * 0.25
        d_prev = d[step - 1 :]
    values[level + 1][0] = e_zero + (before(d_prev[0], lane) + d_zero) * 0.25


def inverse(values, details, level, lane, keep, before, after):
    pairs = (LANES >> level) // 2
    dst = values[level]
    coarse = values[level + 1]

    def kept(at, count):
        return jnp.where(keep[None], details[level][pl.ds(at, count)], 0.0)

    step = min(CHUNK, pairs)
    back = before(kept(pairs - 1, 1)[0], lane)[None]
    for at in range(0, pairs, step):
        k = kept(at, step)
        shifted = jnp.concatenate([back, k[:-1]], axis=0)
        dst[pl.ds(2 * at, step, stride=2)] = coarse[pl.ds(at, step)] - (shifted + k) * 0.25
        back = k[step - 1 :]
    e_first = dst[pl.ds(0, 2, stride=2)]
    pre = before(dst[2 * pairs - 2], lane)[None]
    post = jnp.stack([after(e_first[0], lane), after(e_first[1], lane)])
    for at in range(0, pairs, step):
        lo, hi = max(at - 1, 0), min(at + step + 2, pairs)
        e = dst[pl.ds(2 * lo, hi - lo, stride=2)]
        if at == 0:
            e = jnp.concatenate([pre, e], axis=0)
        need = step + 3 - e.shape[0]
        if need:
            e = jnp.concatenate([e, post[:need]], axis=0)
        dst[pl.ds(2 * at + 1, step, stride=2)] = kept(at, step) + predict(e)


def transform(values, details, lane, level_of, before, after):
    for level in range(LEVELS):
        forward(values, details, level, lane, before, after)
    for level in reversed(range(LEVELS)):
        inverse(values, details, level, lane, level_of > level, before, after)


def lanes_and_sublanes():
    return (
        lax.broadcasted_iota(jnp.int32, (8, LANES), 1),
        lax.broadcasted_iota(jnp.int32, (8, LANES), 0),
    )


PARTS = 8
PART = LANES // PARTS
PITCH = PART + 1
STRIP_ROWS = (72, 24, 16, 16, 16, 16, 40, 16)
STRIP_FIRST = (-32, -8, -2, -4, -3, -2, -16, -2)


def rows_away(value, by):
    return pltpu.roll(value, (-by * SIDES) % LANES, 1) if by else value


def parts_away(here, beyond, by, sublane):
    turn = (-by) % PARTS
    inside = sublane < PARTS - by if by > 0 else sublane >= -by
    return jnp.where(inside, pltpu.roll(here, turn, 0), pltpu.roll(beyond, turn, 0))


def predicted(before, here, after, later):
    return (here + after) * (9.0 / 16.0) - (before + later) * (1.0 / 16.0)


def both_away(pair, by, sublane):
    here, beyond = pair
    return parts_away(here, beyond, by, sublane), parts_away(beyond, here, by, sublane)


class Strip:
    def __init__(self, buffer, first):
        self.buffer, self.first = buffer, first

    def put(self, place, value, apart=1):
        self.buffer[pl.ds(place - self.first, 8, stride=apart), :] = value

    def get(self, place, apart=1):
        return self.buffer[pl.ds(place - self.first, 8, stride=apart), :]


class Kept:
    def __init__(self, values, sublane):
        self.values, self.sublane, self.seen = values, sublane, {}

    def __getitem__(self, place):
        if place not in self.seen:
            part, slot = divmod(place, len(self.values))
            value = self.values[slot]
            if part:
                beyond = rows_away(value, 1 if part > 0 else -1)
                value = parts_away(value, beyond, part, self.sublane)
            self.seen[place] = value
        return self.seen[place]


def scaled(before, here, after, twice_before, twice_after):
    return here * (23.0 / 32.0) - (before + after) * 0.125 + (twice_before + twice_after) * (1.0 / 64.0)


def lift_strips(value, level_of, buffers):
    line, above, evens, kept, kept_above, back, levels, done = (
        Strip(buffer, first) for buffer, first in zip(buffers, STRIP_FIRST)
    )
    for row in range(-3, 4):
        line.put(row * PARTS, rows_away(value, row))
    for row in range(-2, 3):
        levels.put(row * PARTS, rows_away(level_of, row))

    def approached(strip, first):
        at = lambda by: strip.get(2 * first + by, 2)
        return scaled(at(-2), at(0), at(2), at(-4), at(4)) + (at(-1) + at(1)) * 0.25

    def detailed(strip, first, level, apart):
        at = lambda by: strip.get(2 * first + by, 2)
        detail = at(1) - predicted(at(-2), at(0), at(2), at(4))
        return jnp.where(levels.get(apart * (2 * first + 1), 2 * apart) > level, detail, 0.0)

    for first in (-8, 0, 8):
        above.put(first, approached(line, first))
    for first in (-4, 4):
        kept.put(first, detailed(line, first, LEVELS - 2, 1))
    evens.put(-2, approached(above, -2))
    kept_above.put(-3, detailed(above, -3, LEVELS - 1, 2))
    for y, k, to in ((evens, kept_above, back), (back, kept, done)):
        to.put(-2, y.get(-1) - (k.get(-2) + k.get(-1)) * 0.25, 2)
        to.put(
            -1,
            scaled(k.get(-2), k.get(-1), k.get(0), k.get(-3), k.get(1))
            + predicted(y.get(-2), y.get(-1), y.get(0), y.get(1)),
            2,
        )
    return done


def lift_window(inner, outer, level_of, sublane, buffers):
    kept = []
    level = 0
    pairs = list(zip(inner, outer))
    while len(pairs) > 1:
        even, odd = pairs[0::2], pairs[1::2]
        half = len(even)
        last = both_away(even[-1], -1, sublane)
        ahead = [last] + even + [
            both_away(even[i % half], 1 + i // half, sublane) for i in range(2)
        ]
        detail = [
            tuple(odd[i][n] - predicted(*(e[n] for e in ahead[i : i + 4])) for n in (0, 1))
            for i in range(half)
        ]
        back = [both_away(detail[-1], -1, sublane)] + detail
        pairs = [
            tuple(even[i][n] + (back[i][n] + back[i + 1][n]) * 0.25 for n in (0, 1)) for i in range(half)
        ]
        kept.append(Kept([jnp.where(level_of > level, d[0], 0.0) for d in detail], sublane))
        level += 1
    done = lift_strips(pairs[0][0], level_of, buffers)
    wanted = [range(0, PART)]
    for _ in kept:
        low = [n // 2 - 1 if n % 2 else n // 2 for n in wanted[-1]]
        high = [n // 2 + 2 if n % 2 else n // 2 for n in wanted[-1]]
        wanted.append(range(min(low), max(high) + 1))
    current = {place: done.get(place) for place in wanted.pop()}
    while kept:
        k = kept.pop()
        even = {i: value - (k[i - 1] + k[i]) * 0.25 for i, value in current.items()}
        current = {}
        for n in wanted.pop():
            i = n // 2
            if n % 2:
                current[n] = k[i] + predicted(even[i - 1], even[i], even[i + 1], even[i + 2])
            else:
                current[n] = even[i]
    return [current[n] for n in range(PART)]


def exchange_kernel(sizes, x_ref, refine_ref, ob, win, level_ref, xb, near_level, *rest):
    values, details = rest[: LEVELS + 1], rest[LEVELS + 1 : 2 * LEVELS + 1]
    recv_sem, level_recv_sem, here_sem = rest[2 * LEVELS + 1 :]
    rows = x_ref.shape[0]
    left, right, left_seam, right_seam = neighbours(sizes)
    barrier = pltpu.get_barrier_semaphore()
    pl.semaphore_signal(barrier, inc=1, device_id=left, device_id_type=LOGICAL)

    @pl.when(jnp.logical_not(right_seam))
    def _():
        pl.semaphore_signal(barrier, inc=1, device_id=right, device_id_type=LOGICAL)

    lane, sublane = lanes_and_sublanes()
    own = refine_ref[0]
    side, row = lane % SIDES, lane // SIDES
    from_left = (side < COMP) & (row < HALO)
    from_right = (side >= COMP) & (row >= 2 * HALO)

    def send_and_lift(in_sem, send_sem, level_send_sem):
        def remote(src, dst, sent, come, device):
            return pltpu.make_async_remote_copy(
                src_ref=src,
                dst_ref=dst,
                send_sem=sent,
                recv_sem=come,
                device_id=device,
                device_id_type=LOGICAL,
            )

        low, high = pl.ds(0, COMP), pl.ds(COMP, COMP)
        level_right = remote(
            refine_ref, near_level.at[0], level_send_sem, level_recv_sem, right
        )
        level_left = remote(refine_ref, near_level.at[1], level_send_sem, level_recv_sem, left)
        to_right = [
            remote(
                x_ref.at[pl.ds(rows - HALO, HALO)], win.at[pl.ds(0, HALO), low, :], send_sem, recv_sem, right
            ),
            level_right,
        ]
        to_left = [
            remote(
                x_ref.at[pl.ds(0, HALO)], win.at[pl.ds(2 * HALO, HALO), high, :], send_sem, recv_sem, left
            ),
            level_left,
        ]
        pl.semaphore_wait(barrier, jnp.where(left_seam, 1, 2))
        for copy in to_right:
            copy.start()

        @pl.when(right_seam)
        def _():
            pl.semaphore_signal(here_sem, inc=1, device_id=right, device_id_type=LOGICAL)

        @pl.when(jnp.logical_not(left_seam))
        def _():
            for copy in to_left:
                copy.start()

        for c in range(COMP):
            pltpu.make_async_copy(x_ref.at[:, c, :], xb.at[c], in_sem).start()
        pltpu.make_async_copy(xb, xb, in_sem).wait()

        for c in range(COMP):
            win[pl.ds(HALO, 2 * HALO), c, :] = xb[c, pl.ds(0, 2 * HALO), :]
            win[pl.ds(0, 2 * HALO), COMP + c, :] = xb[c, pl.ds(rows - 2 * HALO, 2 * HALO), :]
        for c in range(COMP):
            for half in range(2):
                values[0][:, 2 * c + half, :] = xb[c, pl.ds(half * LANES, LANES), :].T
        transform(
            values, details, lane, jnp.full((8, LANES), own, jnp.int32), before_with_carry, after_with_carry
        )
        for c in range(COMP):
            for half in range(2):
                ob[c, pl.ds(half * LANES, LANES), :] = values[0][:, 2 * c + half, :].T

        @pl.when(left_seam)
        def _():
            pl.semaphore_wait(here_sem, 1)
            for c in range(COMP):
                remote(
                    xb.at[c, pl.ds(0, HALO), :],
                    win.at[pl.ds(2 * HALO, HALO), COMP + c, :],
                    send_sem,
                    recv_sem,
                    left,
                ).start()
            level_left.start()

        wait_for_rows(2 * HALO * COMP, xb, send_sem)
        pltpu.make_async_copy(near_level, near_level, level_send_sem).wait()

    pl.run_scoped(send_and_lift, *[pltpu.SemaphoreType.DMA] * 3)
    pltpu.make_async_copy(near_level, near_level, level_recv_sem).wait()
    wait_for_rows(2 * HALO * COMP, xb, recv_sem)
    level_ref[...] = jnp.where(
        from_left, near_level[0, 0], jnp.where(from_right, near_level[1, 0], own)
    )


def ends_kernel(ob, win, level_ref, out_ref, wout, turned, beyond, out_sem, *strips):
    rows = out_ref.shape[0]
    for c in range(COMP):
        pltpu.make_async_copy(
            ob.at[c, pl.ds(HALO, rows - 2 * HALO), :],
            out_ref.at[pl.ds(HALO, rows - 2 * HALO), c, :],
            out_sem,
        ).start()
    lane, sublane = lanes_and_sublanes()
    used = WIN * SIDES
    rows_here = win[...]
    rows_next = jnp.concatenate([rows_here[1:], rows_here[:1]], axis=0)
    rows_last = jnp.concatenate([rows_here[WIN - 1 :], rows_here[: WIN - 1]], axis=0)
    cell = lax.broadcasted_iota(jnp.int32, rows_here.shape, 2)
    around = jnp.where(cell < LANES // 2, rows_next, rows_last)
    for buffer, value in ((turned, rows_here), (beyond, around)):
        cells = value.reshape(used, LANES).T
        for part in range(PARTS):
            buffer[pl.ds(part * PITCH, PART), :used] = cells[part * PART : (part + 1) * PART]
    inner = [turned[pl.ds(k, PARTS, stride=PITCH), :] for k in range(PART)]
    outer = [beyond[pl.ds(k, PARTS, stride=PITCH), :] for k in range(PART)]
    for k, value in enumerate(lift_window(inner, outer, level_ref[...], sublane, strips)):
        turned[pl.ds(k, PARTS, stride=PITCH), :] = value
    cells = jnp.concatenate([turned[pl.ds(part * PITCH, PART), :] for part in range(PARTS)], axis=0)
    redone = cells.T[HALO * SIDES : 2 * HALO * SIDES]
    wout[...] = redone.reshape(HALO, SIDES, LANES)
    for side, first in ((0, 0), (1, rows - HALO)):
        pltpu.make_async_copy(
            wout.at[:, pl.ds(side * COMP, COMP), :], out_ref.at[pl.ds(first, HALO)], out_sem
        ).start()
    pltpu.make_async_copy(ob, ob, out_sem).wait()


def lifting_scratch():
    f32 = jnp.float32
    return [pltpu.VMEM((LANES >> level, 8, LANES), f32) for level in range(LEVELS + 1)] + [
        pltpu.VMEM(((LANES >> level) // 2, 8, LANES), f32) for level in range(LEVELS)
    ]


def per_device(sizes, velocity, refine):
    rows = velocity.shape[1] // LANES
    x = velocity.reshape(COMP, rows, LANES).transpose(1, 0, 2)
    x = pltpu.with_memory_space_constraint(x, pltpu.HBM)
    f32 = jnp.float32
    vmem = pl.BlockSpec(memory_space=pltpu.VMEM)
    ob, win, level_of = pl.pallas_call(
        functools.partial(exchange_kernel, sizes),
        out_shape=[
            jax.ShapeDtypeStruct((COMP, rows, LANES), f32),
            jax.ShapeDtypeStruct((WIN, SIDES, LANES), f32),
            jax.ShapeDtypeStruct((8, LANES), jnp.int32),
        ],
        in_specs=[pl.BlockSpec(memory_space=pltpu.HBM), pl.BlockSpec(memory_space=pltpu.SMEM)],
        out_specs=[vmem] * 3,
        scratch_shapes=[
            pltpu.VMEM((COMP, rows, LANES), f32),
            pltpu.SMEM((2, 1), jnp.int32),
        ]
        + lifting_scratch()
        + [
            pltpu.SemaphoreType.DMA,
            pltpu.SemaphoreType.DMA,
            pltpu.SemaphoreType.REGULAR,
        ],
        compiler_params=pltpu.CompilerParams(
            collective_id=0, has_side_effects=True, vmem_limit_bytes=VMEM_LIMIT
        ),
    )(x, refine)
    out = pl.pallas_call(
        ends_kernel,
        out_shape=jax.ShapeDtypeStruct(x.shape, f32),
        in_specs=[vmem] * 3,
        out_specs=pl.BlockSpec(memory_space=pltpu.HBM),
        scratch_shapes=[
            pltpu.VMEM((HALO, SIDES, LANES), f32),
            pltpu.VMEM((PARTS * PITCH, LANES), f32),
            pltpu.VMEM((PARTS * PITCH, LANES), f32),
            pltpu.SemaphoreType.DMA,
        ]
        + [
            pltpu.VMEM((count, LANES), jnp.int32 if first == -16 else f32)
            for count, first in zip(STRIP_ROWS, STRIP_FIRST)
        ],
        compiler_params=pltpu.CompilerParams(vmem_limit_bytes=VMEM_LIMIT),
    )(ob, win, level_of)
    return out.transpose(1, 0, 2).reshape(velocity.shape)


def solution(mesh):
    sizes = tuple(mesh.shape[name] for name in AXES)
    return jax.shard_map(
        functools.partial(per_device, sizes),
        mesh=mesh,
        in_specs=(P(None, AXES), P(AXES)),
        out_specs=P(None, AXES),
        check_vma=False,
    )
```

```python
import functools

import jax
import jax.numpy as jnp
from jax import lax
from jax.experimental import pallas as pl
from jax.experimental.pallas import tpu as pltpu
from jax.sharding import PartitionSpec as P

AXES = ("node", "rank", "chip")
LEVELS = 6
LANES = 128
COMP = 3
LOGICAL = pl.DeviceIdType.LOGICAL
HALO = 3
WIN = 3 * HALO
SIDES = 8
CHUNK = 8
VMEM_LIMIT = 8 << 20


def neighbours(sizes):
    nodes, ranks, chips = sizes
    total = nodes * ranks * chips
    node, rank, chip = (lax.axis_index(name) for name in AXES)
    place = rank * chips + chip
    me = node * (ranks * chips) + place
    left = jnp.where(me == 0, total - 1, me - 1)
    right = jnp.where(me == total - 1, 0, me + 1)
    left_seam = (place == 0) | (place == ranks * chips - 1)
    right_seam = (place == ranks * chips - 1) | (place == ranks * chips - 2)
    return left, right, left_seam, right_seam


def wait_for_rows(count, buffer, semaphore):
    rows = buffer.at[0, pl.ds(0, count), :]
    pltpu.make_async_copy(rows, rows, semaphore).wait()


def after_with_carry(row, lane):
    rolled = pltpu.roll(row, LANES - 1, 1)
    carried = pltpu.roll(rolled, 7, 0)
    return jnp.where(lane == LANES - 1, carried, rolled)


def before_with_carry(row, lane):
    rolled = pltpu.roll(row, 1, 1)
    carried = pltpu.roll(rolled, 1, 0)
    return jnp.where(lane == 0, carried, rolled)


def predict(e):
    n = e.shape[0] - 3
    return (e[1 : n + 1] + e[2 : n + 2]) * (9.0 / 16.0) - (e[0:n] + e[3 : n + 3]) * (1.0 / 16.0)


def forward(values, details, level, lane, before, after):
    pairs = (LANES >> level) // 2
    src = values[level]
    e_first = src[pl.ds(0, 2, stride=2)]
    pre = before(src[2 * pairs - 2], lane)[None]
    post = jnp.stack([after(e_first[0], lane), after(e_first[1], lane)])
    step = min(CHUNK, pairs)
    d_prev, e_zero, d_zero = None, None, None
    for at in range(0, pairs, step):
        lo, hi = max(at - 1, 0), min(at + step + 2, pairs)
        e = src[pl.ds(2 * lo, hi - lo, stride=2)]
        if at == 0:
            e = jnp.concatenate([pre, e], axis=0)
        need = step + 3 - e.shape[0]
        if need:
            e = jnp.concatenate([e, post[:need]], axis=0)
        d = src[pl.ds(2 * at + 1, step, stride=2)] - predict(e)
        details[level][pl.ds(at, step)] = d
        here = e[1 : step + 1]
        if at == 0:
            e_zero, d_zero = here[0], d[0]
            values[level + 1][pl.ds(1, step - 1)] = here[1:] + (d[:-1] + d[1:]) * 0.25
        else:
            back = jnp.concatenate([d_prev, d[:-1]], axis=0)
            values[level + 1][pl.ds(at, step)] = here + (back + d) * 0.25
        d_prev = d[step - 1 :]
    values[level + 1][0] = e_zero + (before(d_prev[0], lane) + d_zero) * 0.25


def inverse(values, details, level, lane, keep, before, after):
    pairs = (LANES >> level) // 2
    dst = values[level]
    coarse = values[level + 1]

    def kept(at, count):
        return jnp.where(keep[None], details[level][pl.ds(at, count)], 0.0)

    step = min(CHUNK, pairs)
    back = before(kept(pairs - 1, 1)[0], lane)[None]
    for at in range(0, pairs, step):
        k = kept(at, step)
        shifted = jnp.concatenate([back, k[:-1]], axis=0)
        dst[pl.ds(2 * at, step, stride=2)] = coarse[pl.ds(at, step)] - (shifted + k) * 0.25
        back = k[step - 1 :]
    e_first = dst[pl.ds(0, 2, stride=2)]
    pre = before(dst[2 * pairs - 2], lane)[None]
    post = jnp.stack([after(e_first[0], lane), after(e_first[1], lane)])
    for at in range(0, pairs, step):
        lo, hi = max(at - 1, 0), min(at + step + 2, pairs)
        e = dst[pl.ds(2 * lo, hi - lo, stride=2)]
        if at == 0:
            e = jnp.concatenate([pre, e], axis=0)
        need = step + 3 - e.shape[0]
        if need:
            e = jnp.concatenate([e, post[:need]], axis=0)
        dst[pl.ds(2 * at + 1, step, stride=2)] = kept(at, step) + predict(e)


def transform(values, details, lane, level_of, before, after):
    for level in range(LEVELS):
        forward(values, details, level, lane, before, after)
    for level in reversed(range(LEVELS)):
        inverse(values, details, level, lane, level_of > level, before, after)


def lanes_and_sublanes():
    return (
        lax.broadcasted_iota(jnp.int32, (8, LANES), 1),
        lax.broadcasted_iota(jnp.int32, (8, LANES), 0),
    )


PARTS = 8
PART = LANES // PARTS
PITCH = PART + 1
STRIP_ROWS = (72, 24, 16, 16, 16, 16, 40, 16)
STRIP_FIRST = (-32, -8, -2, -4, -3, -2, -16, -2)


def rows_away(value, by):
    return pltpu.roll(value, (-by * SIDES) % LANES, 1) if by else value


def parts_away(here, beyond, by, sublane):
    turn = (-by) % PARTS
    inside = sublane < PARTS - by if by > 0 else sublane >= -by
    return jnp.where(inside, pltpu.roll(here, turn, 0), pltpu.roll(beyond, turn, 0))


def predicted(before, here, after, later):
    return (here + after) * (9.0 / 16.0) - (before + later) * (1.0 / 16.0)


def both_away(pair, by, sublane):
    here, beyond = pair
    return parts_away(here, beyond, by, sublane), parts_away(beyond, here, by, sublane)


class Strip:
    def __init__(self, buffer, first):
        self.buffer, self.first = buffer, first

    def put(self, place, value, apart=1):
        self.buffer[pl.ds(place - self.first, 8, stride=apart), :] = value

    def get(self, place, apart=1):
        return self.buffer[pl.ds(place - self.first, 8, stride=apart), :]


class Kept:
    def __init__(self, values, sublane):
        self.values, self.sublane, self.seen = values, sublane, {}

    def __getitem__(self, place):
        if place not in self.seen:
            part, slot = divmod(place, len(self.values))
            value = self.values[slot]
            if part:
                beyond = rows_away(value, 1 if part > 0 else -1)
                value = parts_away(value, beyond, part, self.sublane)
            self.seen[place] = value
        return self.seen[place]


def scaled(before, here, after, twice_before, twice_after):
    return here * (23.0 / 32.0) - (before + after) * 0.125 + (twice_before + twice_after) * (1.0 / 64.0)


def lift_strips(value, level_of, buffers):
    line, above, evens, kept, kept_above, back, levels, done = (
        Strip(buffer, first) for buffer, first in zip(buffers, STRIP_FIRST)
    )
    for row in range(-3, 4):
        line.put(row * PARTS, rows_away(value, row))
    for row in range(-2, 3):
        levels.put(row * PARTS, rows_away(level_of, row))

    def approached(strip, first):
        at = lambda by: strip.get(2 * first + by, 2)
        return scaled(at(-2), at(0), at(2), at(-4), at(4)) + (at(-1) + at(1)) * 0.25

    def detailed(strip, first, level, apart):
        at = lambda by: strip.get(2 * first + by, 2)
        detail = at(1) - predicted(at(-2), at(0), at(2), at(4))
        return jnp.where(levels.get(apart * (2 * first + 1), 2 * apart) > level, detail, 0.0)

    for first in (-8, 0, 8):
        above.put(first, approached(line, first))
    for first in (-4, 4):
        kept.put(first, detailed(line, first, LEVELS - 2, 1))
    evens.put(-2, approached(above, -2))
    kept_above.put(-3, detailed(above, -3, LEVELS - 1, 2))
    for y, k, to in ((evens, kept_above, back), (back, kept, done)):
        to.put(-2, y.get(-1) - (k.get(-2) + k.get(-1)) * 0.25, 2)
        to.put(
            -1,
            scaled(k.get(-2), k.get(-1), k.get(0), k.get(-3), k.get(1))
            + predicted(y.get(-2), y.get(-1), y.get(0), y.get(1)),
            2,
        )
    return done


def lift_window(inner, outer, level_of, sublane, buffers):
    kept = []
    level = 0
    pairs = list(zip(inner, outer))
    while len(pairs) > 1:
        even, odd = pairs[0::2], pairs[1::2]
        half = len(even)
        last = both_away(even[-1], -1, sublane)
        ahead = [last] + even + [
            both_away(even[i % half], 1 + i // half, sublane) for i in range(2)
        ]
        detail = [
            tuple(odd[i][n] - predicted(*(e[n] for e in ahead[i : i + 4])) for n in (0, 1))
            for i in range(half)
        ]
        back = [both_away(detail[-1], -1, sublane)] + detail
        pairs = [
            tuple(even[i][n] + (back[i][n] + back[i + 1][n]) * 0.25 for n in (0, 1)) for i in range(half)
        ]
        kept.append(Kept([jnp.where(level_of > level, d[0], 0.0) for d in detail], sublane))
        level += 1
    done = lift_strips(pairs[0][0], level_of, buffers)
    wanted = [range(0, PART)]
    for _ in kept:
        low = [n // 2 - 1 if n % 2 else n // 2 for n in wanted[-1]]
        high = [n // 2 + 2 if n % 2 else n // 2 for n in wanted[-1]]
        wanted.append(range(min(low), max(high) + 1))
    current = {place: done.get(place) for place in wanted.pop()}
    while kept:
        k = kept.pop()
        even = {i: value - (k[i - 1] + k[i]) * 0.25 for i, value in current.items()}
        current = {}
        for n in wanted.pop():
            i = n // 2
            if n % 2:
                current[n] = k[i] + predicted(even[i - 1], even[i], even[i + 1], even[i + 2])
            else:
                current[n] = even[i]
    return [current[n] for n in range(PART)]


def exchange_kernel(sizes, x_ref, refine_ref, ob, win, level_ref, xb, near_level, *rest):
    values, details = rest[: LEVELS + 1], rest[LEVELS + 1 : 2 * LEVELS + 1]
    recv_sem, level_recv_sem, here_sem = rest[2 * LEVELS + 1 :]
    rows = x_ref.shape[0]
    left, right, left_seam, right_seam = neighbours(sizes)
    barrier = pltpu.get_barrier_semaphore()
    pl.semaphore_signal(barrier, inc=1, device_id=left, device_id_type=LOGICAL)

    @pl.when(jnp.logical_not(right_seam))
    def _():
        pl.semaphore_signal(barrier, inc=1, device_id=right, device_id_type=LOGICAL)

    def send_and_lift(in_sem, send_sem, level_send_sem):
        def remote(src, dst, sent, come, device):
            return pltpu.make_async_remote_copy(
                src_ref=src,
                dst_ref=dst,
                send_sem=sent,
                recv_sem=come,
                device_id=device,
                device_id_type=LOGICAL,
            )

        low, high = pl.ds(0, COMP), pl.ds(COMP, COMP)
        level_right = remote(
            refine_ref, near_level.at[0], level_send_sem, level_recv_sem, right
        )
        level_left = remote(refine_ref, near_level.at[1], level_send_sem, level_recv_sem, left)
        to_right = [
            remote(
                x_ref.at[pl.ds(rows - HALO, HALO)], win.at[pl.ds(0, HALO), low, :], send_sem, recv_sem, right
            ),
            level_right,
        ]
        to_left = [
            remote(
                x_ref.at[pl.ds(0, HALO)], win.at[pl.ds(2 * HALO, HALO), high, :], send_sem, recv_sem, left
            ),
            level_left,
        ]
        pl.semaphore_wait(barrier, jnp.where(left_seam, 1, 2))
        for copy in to_right:
            copy.start()

        @pl.when(right_seam)
        def _():
            pl.semaphore_signal(here_sem, inc=1, device_id=right, device_id_type=LOGICAL)

        @pl.when(jnp.logical_not(left_seam))
        def _():
            for copy in to_left:
                copy.start()

        for c in range(COMP):
            pltpu.make_async_copy(x_ref.at[:, c, :], xb.at[c], in_sem).start()
        pltpu.make_async_copy(xb, xb, in_sem).wait()

        lane, sublane = lanes_and_sublanes()
        own = refine_ref[0]
        for c in range(COMP):
            win[pl.ds(HALO, 2 * HALO), c, :] = xb[c, pl.ds(0, 2 * HALO), :]
            win[pl.ds(0, 2 * HALO), COMP + c, :] = xb[c, pl.ds(rows - 2 * HALO, 2 * HALO), :]
        for c in range(COMP):
            for half in range(2):
                values[0][:, 2 * c + half, :] = xb[c, pl.ds(half * LANES, LANES), :].T
        transform(
            values, details, lane, jnp.full((8, LANES), own, jnp.int32), before_with_carry, after_with_carry
        )
        for c in range(COMP):
            for half in range(2):
                ob[c, pl.ds(half * LANES, LANES), :] = values[0][:, 2 * c + half, :].T

        side = lane & (SIDES - 1)
        from_left = (side < COMP) & (lane < HALO * SIDES)
        from_right = (side >= COMP) & (lane >= 2 * HALO * SIDES)
        level_ref[...] = jnp.where(from_left, 1, jnp.where(from_right, 2, 0))

        @pl.when(left_seam)
        def _():
            pl.semaphore_wait(here_sem, 1)
            for c in range(COMP):
                remote(
                    xb.at[c, pl.ds(0, HALO), :],
                    win.at[pl.ds(2 * HALO, HALO), COMP + c, :],
                    send_sem,
                    recv_sem,
                    left,
                ).start()
            level_left.start()

        wait_for_rows(2 * HALO * COMP, xb, send_sem)
        pltpu.make_async_copy(near_level, near_level, level_send_sem).wait()

    pl.run_scoped(send_and_lift, *[pltpu.SemaphoreType.DMA] * 3)
    pltpu.make_async_copy(near_level, near_level, level_recv_sem).wait()
    wait_for_rows(2 * HALO * COMP, xb, recv_sem)
    whose = level_ref[...]
    level_ref[...] = jnp.where(
        whose == 1, near_level[0, 0], jnp.where(whose == 2, near_level[1, 0], refine_ref[0])
    )


def ends_kernel(ob, win, level_ref, out_ref, wout, turned, beyond, out_sem, *strips):
    rows = out_ref.shape[0]
    for c in range(COMP):
        pltpu.make_async_copy(
            ob.at[c, pl.ds(HALO, rows - 2 * HALO), :],
            out_ref.at[pl.ds(HALO, rows - 2 * HALO), c, :],
            out_sem,
        ).start()
    lane, sublane = lanes_and_sublanes()
    used = WIN * SIDES
    rows_here = win[...]
    rows_next = jnp.concatenate([rows_here[1:], rows_here[:1]], axis=0)
    rows_last = jnp.concatenate([rows_here[WIN - 1 :], rows_here[: WIN - 1]], axis=0)
    cell = lax.broadcasted_iota(jnp.int32, rows_here.shape, 2)
    around = jnp.where(cell < LANES // 2, rows_next, rows_last)
    for buffer, value in ((turned, rows_here), (beyond, around)):
        cells = value.reshape(used, LANES).T
        for part in range(PARTS):
            buffer[pl.ds(part * PITCH, PART), :used] = cells[part * PART : (part + 1) * PART]
    inner = [turned[pl.ds(k, PARTS, stride=PITCH), :] for k in range(PART)]
    outer = [beyond[pl.ds(k, PARTS, stride=PITCH), :] for k in range(PART)]
    for k, value in enumerate(lift_window(inner, outer, level_ref[...], sublane, strips)):
        turned[pl.ds(k, PARTS, stride=PITCH), :] = value
    cells = jnp.concatenate([turned[pl.ds(part * PITCH, PART), :] for part in range(PARTS)], axis=0)
    redone = cells.T[HALO * SIDES : 2 * HALO * SIDES]
    wout[...] = redone.reshape(HALO, SIDES, LANES)
    for side, first in ((0, 0), (1, rows - HALO)):
        pltpu.make_async_copy(
            wout.at[:, pl.ds(side * COMP, COMP), :], out_ref.at[pl.ds(first, HALO)], out_sem
        ).start()
    pltpu.make_async_copy(ob, ob, out_sem).wait()


def lifting_scratch():
    f32 = jnp.float32
    return [pltpu.VMEM((LANES >> level, 8, LANES), f32) for level in range(LEVELS + 1)] + [
        pltpu.VMEM(((LANES >> level) // 2, 8, LANES), f32) for level in range(LEVELS)
    ]


def per_device(sizes, velocity, refine):
    rows = velocity.shape[1] // LANES
    x = velocity.reshape(COMP, rows, LANES).transpose(1, 0, 2)
    x = pltpu.with_memory_space_constraint(x, pltpu.HBM)
    f32 = jnp.float32
    vmem = pl.BlockSpec(memory_space=pltpu.VMEM)
    ob, win, level_of = pl.pallas_call(
        functools.partial(exchange_kernel, sizes),
        out_shape=[
            jax.ShapeDtypeStruct((COMP, rows, LANES), f32),
            jax.ShapeDtypeStruct((WIN, SIDES, LANES), f32),
            jax.ShapeDtypeStruct((8, LANES), jnp.int32),
        ],
        in_specs=[pl.BlockSpec(memory_space=pltpu.HBM), pl.BlockSpec(memory_space=pltpu.SMEM)],
        out_specs=[vmem] * 3,
        scratch_shapes=[
            pltpu.VMEM((COMP, rows, LANES), f32),
            pltpu.SMEM((2, 1), jnp.int32),
        ]
        + lifting_scratch()
        + [
            pltpu.SemaphoreType.DMA,
            pltpu.SemaphoreType.DMA,
            pltpu.SemaphoreType.REGULAR,
        ],
        compiler_params=pltpu.CompilerParams(
            collective_id=0, has_side_effects=True, vmem_limit_bytes=VMEM_LIMIT
        ),
    )(x, refine)
    out = pl.pallas_call(
        ends_kernel,
        out_shape=jax.ShapeDtypeStruct(x.shape, f32),
        in_specs=[vmem] * 3,
        out_specs=pl.BlockSpec(memory_space=pltpu.HBM),
        scratch_shapes=[
            pltpu.VMEM((HALO, SIDES, LANES), f32),
            pltpu.VMEM((PARTS * PITCH, LANES), f32),
            pltpu.VMEM((PARTS * PITCH, LANES), f32),
            pltpu.SemaphoreType.DMA,
        ]
        + [
            pltpu.VMEM((count, LANES), jnp.int32 if first == -16 else f32)
            for count, first in zip(STRIP_ROWS, STRIP_FIRST)
        ],
        compiler_params=pltpu.CompilerParams(vmem_limit_bytes=VMEM_LIMIT),
    )(ob, win, level_of)
    return out.transpose(1, 0, 2).reshape(velocity.shape)


def solution(mesh):
    sizes = tuple(mesh.shape[name] for name in AXES)
    return jax.shard_map(
        functools.partial(per_device, sizes),
        mesh=mesh,
        in_specs=(P(None, AXES), P(AXES)),
        out_specs=P(None, AXES),
        check_vma=False,
    )
```

```python
import functools

import jax
import jax.numpy as jnp
from jax import lax
from jax.experimental import pallas as pl
from jax.experimental.pallas import tpu as pltpu
from jax.sharding import PartitionSpec as P

AXES = ("node", "rank", "chip")
LEVELS = 6
LANES = 128
COMP = 3
LOGICAL = pl.DeviceIdType.LOGICAL
HALO = 3
WIN = 3 * HALO
SIDES = 8
CHUNK = 8
VMEM_LIMIT = 8 << 20


def neighbours(sizes):
    nodes, ranks, chips = sizes
    total = nodes * ranks * chips
    node, rank, chip = (lax.axis_index(name) for name in AXES)
    place = rank * chips + chip
    me = node * (ranks * chips) + place
    left = jnp.where(me == 0, total - 1, me - 1)
    right = jnp.where(me == total - 1, 0, me + 1)
    left_seam = (place == 0) | (place == ranks * chips - 1)
    right_seam = (place == ranks * chips - 1) | (place == ranks * chips - 2)
    return left, right, left_seam, right_seam, place == ranks * chips - 1


def wait_for_rows(count, buffer, semaphore):
    rows = buffer.at[0, pl.ds(0, count), :]
    pltpu.make_async_copy(rows, rows, semaphore).wait()


def after_with_carry(row, lane):
    rolled = pltpu.roll(row, LANES - 1, 1)
    carried = pltpu.roll(rolled, 7, 0)
    return jnp.where(lane == LANES - 1, carried, rolled)


def before_with_carry(row, lane):
    rolled = pltpu.roll(row, 1, 1)
    carried = pltpu.roll(rolled, 1, 0)
    return jnp.where(lane == 0, carried, rolled)


def predict(e):
    n = e.shape[0] - 3
    return (e[1 : n + 1] + e[2 : n + 2]) * (9.0 / 16.0) - (e[0:n] + e[3 : n + 3]) * (1.0 / 16.0)


def forward(values, details, level, lane, before, after):
    pairs = (LANES >> level) // 2
    src = values[level]
    e_first = src[pl.ds(0, 2, stride=2)]
    pre = before(src[2 * pairs - 2], lane)[None]
    post = jnp.stack([after(e_first[0], lane), after(e_first[1], lane)])
    step = min(CHUNK, pairs)
    d_prev, e_zero, d_zero = None, None, None
    for at in range(0, pairs, step):
        lo, hi = max(at - 1, 0), min(at + step + 2, pairs)
        e = src[pl.ds(2 * lo, hi - lo, stride=2)]
        if at == 0:
            e = jnp.concatenate([pre, e], axis=0)
        need = step + 3 - e.shape[0]
        if need:
            e = jnp.concatenate([e, post[:need]], axis=0)
        d = src[pl.ds(2 * at + 1, step, stride=2)] - predict(e)
        details[level][pl.ds(at, step)] = d
        here = e[1 : step + 1]
        if at == 0:
            e_zero, d_zero = here[0], d[0]
            values[level + 1][pl.ds(1, step - 1)] = here[1:] + (d[:-1] + d[1:]) * 0.25
        else:
            back = jnp.concatenate([d_prev, d[:-1]], axis=0)
            values[level + 1][pl.ds(at, step)] = here + (back + d) * 0.25
        d_prev = d[step - 1 :]
    values[level + 1][0] = e_zero + (before(d_prev[0], lane) + d_zero) * 0.25


def inverse(values, details, level, lane, keep, before, after):
    pairs = (LANES >> level) // 2
    dst = values[level]
    coarse = values[level + 1]

    def kept(at, count):
        return jnp.where(keep[None], details[level][pl.ds(at, count)], 0.0)

    step = min(CHUNK, pairs)
    back = before(kept(pairs - 1, 1)[0], lane)[None]
    for at in range(0, pairs, step):
        k = kept(at, step)
        shifted = jnp.concatenate([back, k[:-1]], axis=0)
        dst[pl.ds(2 * at, step, stride=2)] = coarse[pl.ds(at, step)] - (shifted + k) * 0.25
        back = k[step - 1 :]
    e_first = dst[pl.ds(0, 2, stride=2)]
    pre = before(dst[2 * pairs - 2], lane)[None]
    post = jnp.stack([after(e_first[0], lane), after(e_first[1], lane)])
    for at in range(0, pairs, step):
        lo, hi = max(at - 1, 0), min(at + step + 2, pairs)
        e = dst[pl.ds(2 * lo, hi - lo, stride=2)]
        if at == 0:
            e = jnp.concatenate([pre, e], axis=0)
        need = step + 3 - e.shape[0]
        if need:
            e = jnp.concatenate([e, post[:need]], axis=0)
        dst[pl.ds(2 * at + 1, step, stride=2)] = kept(at, step) + predict(e)


def transform(values, details, lane, level_of, before, after):
    for level in range(LEVELS):
        forward(values, details, level, lane, before, after)
    for level in reversed(range(LEVELS)):
        inverse(values, details, level, lane, level_of > level, before, after)


def lanes_and_sublanes():
    return (
        lax.broadcasted_iota(jnp.int32, (8, LANES), 1),
        lax.broadcasted_iota(jnp.int32, (8, LANES), 0),
    )


PARTS = 8
PART = LANES // PARTS
PITCH = PART + 1
STRIP_ROWS = (72, 24, 16, 16, 16, 16, 40, 16)
STRIP_FIRST = (-32, -8, -2, -4, -3, -2, -16, -2)


def rows_away(value, by):
    return pltpu.roll(value, (-by * SIDES) % LANES, 1) if by else value


def parts_away(here, beyond, by, sublane):
    turn = (-by) % PARTS
    inside = sublane < PARTS - by if by > 0 else sublane >= -by
    return jnp.where(inside, pltpu.roll(here, turn, 0), pltpu.roll(beyond, turn, 0))


def predicted(before, here, after, later):
    return (here + after) * (9.0 / 16.0) - (before + later) * (1.0 / 16.0)


def both_away(pair, by, sublane):
    here, beyond = pair
    return parts_away(here, beyond, by, sublane), parts_away(beyond, here, by, sublane)


class Strip:
    def __init__(self, buffer, first):
        self.buffer, self.first = buffer, first

    def put(self, place, value, apart=1):
        self.buffer[pl.ds(place - self.first, 8, stride=apart), :] = value

    def get(self, place, apart=1):
        return self.buffer[pl.ds(place - self.first, 8, stride=apart), :]


class Kept:
    def __init__(self, values, sublane):
        self.values, self.sublane, self.seen = values, sublane, {}

    def __getitem__(self, place):
        if place not in self.seen:
            part, slot = divmod(place, len(self.values))
            value = self.values[slot]
            if part:
                beyond = rows_away(value, 1 if part > 0 else -1)
                value = parts_away(value, beyond, part, self.sublane)
            self.seen[place] = value
        return self.seen[place]


def scaled(before, here, after, twice_before, twice_after):
    return here * (23.0 / 32.0) - (before + after) * 0.125 + (twice_before + twice_after) * (1.0 / 64.0)


def lift_strips(value, level_of, buffers):
    line, above, evens, kept, kept_above, back, levels, done = (
        Strip(buffer, first) for buffer, first in zip(buffers, STRIP_FIRST)
    )
    for row in range(-3, 4):
        line.put(row * PARTS, rows_away(value, row))
    for row in range(-2, 3):
        levels.put(row * PARTS, rows_away(level_of, row))

    def approached(strip, first):
        at = lambda by: strip.get(2 * first + by, 2)
        return scaled(at(-2), at(0), at(2), at(-4), at(4)) + (at(-1) + at(1)) * 0.25

    def detailed(strip, first, level, apart):
        at = lambda by: strip.get(2 * first + by, 2)
        detail = at(1) - predicted(at(-2), at(0), at(2), at(4))
        return jnp.where(levels.get(apart * (2 * first + 1), 2 * apart) > level, detail, 0.0)

    for first in (-8, 0, 8):
        above.put(first, approached(line, first))
    for first in (-4, 4):
        kept.put(first, detailed(line, first, LEVELS - 2, 1))
    evens.put(-2, approached(above, -2))
    kept_above.put(-3, detailed(above, -3, LEVELS - 1, 2))
    for y, k, to in ((evens, kept_above, back), (back, kept, done)):
        to.put(-2, y.get(-1) - (k.get(-2) + k.get(-1)) * 0.25, 2)
        to.put(
            -1,
            scaled(k.get(-2), k.get(-1), k.get(0), k.get(-3), k.get(1))
            + predicted(y.get(-2), y.get(-1), y.get(0), y.get(1)),
            2,
        )
    return done


def lift_window(inner, outer, level_of, sublane, buffers):
    kept = []
    level = 0
    pairs = list(zip(inner, outer))
    while len(pairs) > 1:
        even, odd = pairs[0::2], pairs[1::2]
        half = len(even)
        last = both_away(even[-1], -1, sublane)
        ahead = [last] + even + [
            both_away(even[i % half], 1 + i // half, sublane) for i in range(2)
        ]
        detail = [
            tuple(odd[i][n] - predicted(*(e[n] for e in ahead[i : i + 4])) for n in (0, 1))
            for i in range(half)
        ]
        back = [both_away(detail[-1], -1, sublane)] + detail
        pairs = [
            tuple(even[i][n] + (back[i][n] + back[i + 1][n]) * 0.25 for n in (0, 1)) for i in range(half)
        ]
        kept.append(Kept([jnp.where(level_of > level, d[0], 0.0) for d in detail], sublane))
        level += 1
    done = lift_strips(pairs[0][0], level_of, buffers)
    wanted = [range(0, PART)]
    for _ in kept:
        low = [n // 2 - 1 if n % 2 else n // 2 for n in wanted[-1]]
        high = [n // 2 + 2 if n % 2 else n // 2 for n in wanted[-1]]
        wanted.append(range(min(low), max(high) + 1))
    current = {place: done.get(place) for place in wanted.pop()}
    while kept:
        k = kept.pop()
        even = {i: value - (k[i - 1] + k[i]) * 0.25 for i, value in current.items()}
        current = {}
        for n in wanted.pop():
            i = n // 2
            if n % 2:
                current[n] = k[i] + predicted(even[i - 1], even[i], even[i + 1], even[i + 2])
            else:
                current[n] = even[i]
    return [current[n] for n in range(PART)]


def exchange_kernel(sizes, x_ref, refine_ref, ob, win, level_ref, xb, near_level, *rest):
    values, details = rest[: LEVELS + 1], rest[LEVELS + 1 : 2 * LEVELS + 1]
    recv_sem, level_recv_sem, here_sem = rest[2 * LEVELS + 1 :]
    rows = x_ref.shape[0]
    left, right, left_seam, right_seam, last_place = neighbours(sizes)
    barrier = pltpu.get_barrier_semaphore()

    def greet_left():
        pl.semaphore_signal(barrier, inc=1, device_id=left, device_id_type=LOGICAL)

    pl.when(jnp.logical_not(last_place))(greet_left)

    @pl.when(jnp.logical_not(right_seam))
    def _():
        pl.semaphore_signal(barrier, inc=1, device_id=right, device_id_type=LOGICAL)

    def send_and_lift(in_sem, send_sem, level_send_sem):
        def remote(src, dst, sent, come, device):
            return pltpu.make_async_remote_copy(
                src_ref=src,
                dst_ref=dst,
                send_sem=sent,
                recv_sem=come,
                device_id=device,
                device_id_type=LOGICAL,
            )

        low, high = pl.ds(0, COMP), pl.ds(COMP, COMP)
        level_right = remote(
            refine_ref, near_level.at[0], level_send_sem, level_recv_sem, right
        )
        level_left = remote(refine_ref, near_level.at[1], level_send_sem, level_recv_sem, left)
        to_right = [
            remote(
                x_ref.at[pl.ds(rows - HALO, HALO)], win.at[pl.ds(0, HALO), low, :], send_sem, recv_sem, right
            ),
            level_right,
        ]
        to_left = [
            remote(
                x_ref.at[pl.ds(0, HALO)], win.at[pl.ds(2 * HALO, HALO), high, :], send_sem, recv_sem, left
            ),
            level_left,
        ]
        pl.semaphore_wait(barrier, jnp.where(left_seam, 1, 2))
        for copy in to_right:
            copy.start()
        pl.when(last_place)(greet_left)

        @pl.when(right_seam)
        def _():
            pl.semaphore_signal(here_sem, inc=1, device_id=right, device_id_type=LOGICAL)

        @pl.when(jnp.logical_not(left_seam))
        def _():
            for copy in to_left:
                copy.start()

        for c in range(COMP):
            pltpu.make_async_copy(x_ref.at[:, c, :], xb.at[c], in_sem).start()
        pltpu.make_async_copy(xb, xb, in_sem).wait()

        lane, sublane = lanes_and_sublanes()
        own = refine_ref[0]
        for c in range(COMP):
            win[pl.ds(HALO, 2 * HALO), c, :] = xb[c, pl.ds(0, 2 * HALO), :]
            win[pl.ds(0, 2 * HALO), COMP + c, :] = xb[c, pl.ds(rows - 2 * HALO, 2 * HALO), :]
        for c in range(COMP):
            for half in range(2):
                values[0][:, 2 * c + half, :] = xb[c, pl.ds(half * LANES, LANES), :].T
        transform(
            values, details, lane, jnp.full((8, LANES), own, jnp.int32), before_with_carry, after_with_carry
        )
        for c in range(COMP):
            for half in range(2):
                ob[c, pl.ds(half * LANES, LANES), :] = values[0][:, 2 * c + half, :].T

        side = lane & (SIDES - 1)
        from_left = (side < COMP) & (lane < HALO * SIDES)
        from_right = (side >= COMP) & (lane >= 2 * HALO * SIDES)
        level_ref[...] = jnp.where(from_left, 1, jnp.where(from_right, 2, 0))

        @pl.when(left_seam)
        def _():
            pl.semaphore_wait(here_sem, 1)
            for c in range(COMP):
                remote(
                    xb.at[c, pl.ds(0, HALO), :],
                    win.at[pl.ds(2 * HALO, HALO), COMP + c, :],
                    send_sem,
                    recv_sem,
                    left,
                ).start()
            level_left.start()

        wait_for_rows(2 * HALO * COMP, xb, send_sem)
        pltpu.make_async_copy(near_level, near_level, level_send_sem).wait()

    pl.run_scoped(send_and_lift, *[pltpu.SemaphoreType.DMA] * 3)
    pltpu.make_async_copy(near_level, near_level, level_recv_sem).wait()
    wait_for_rows(2 * HALO * COMP, xb, recv_sem)
    whose = level_ref[...]
    level_ref[...] = jnp.where(
        whose == 1, near_level[0, 0], jnp.where(whose == 2, near_level[1, 0], refine_ref[0])
    )


def ends_kernel(ob, win, level_ref, out_ref, wout, turned, beyond, out_sem, *strips):
    rows = out_ref.shape[0]
    for c in range(COMP):
        pltpu.make_async_copy(
            ob.at[c, pl.ds(HALO, rows - 2 * HALO), :],
            out_ref.at[pl.ds(HALO, rows - 2 * HALO), c, :],
            out_sem,
        ).start()
    lane, sublane = lanes_and_sublanes()
    used = WIN * SIDES
    rows_here = win[...]
    rows_next = jnp.concatenate([rows_here[1:], rows_here[:1]], axis=0)
    rows_last = jnp.concatenate([rows_here[WIN - 1 :], rows_here[: WIN - 1]], axis=0)
    cell = lax.broadcasted_iota(jnp.int32, rows_here.shape, 2)
    around = jnp.where(cell < LANES // 2, rows_next, rows_last)
    for buffer, value in ((turned, rows_here), (beyond, around)):
        cells = value.reshape(used, LANES).T
        for part in range(PARTS):
            buffer[pl.ds(part * PITCH, PART), :used] = cells[part * PART : (part + 1) * PART]
    inner = [turned[pl.ds(k, PARTS, stride=PITCH), :] for k in range(PART)]
    outer = [beyond[pl.ds(k, PARTS, stride=PITCH), :] for k in range(PART)]
    for k, value in enumerate(lift_window(inner, outer, level_ref[...], sublane, strips)):
        turned[pl.ds(k, PARTS, stride=PITCH), :] = value
    cells = jnp.concatenate([turned[pl.ds(part * PITCH, PART), :] for part in range(PARTS)], axis=0)
    redone = cells.T[HALO * SIDES : 2 * HALO * SIDES]
    wout[...] = redone.reshape(HALO, SIDES, LANES)
    for side, first in ((0, 0), (1, rows - HALO)):
        pltpu.make_async_copy(
            wout.at[:, pl.ds(side * COMP, COMP), :], out_ref.at[pl.ds(first, HALO)], out_sem
        ).start()
    pltpu.make_async_copy(ob, ob, out_sem).wait()


def lifting_scratch():
    f32 = jnp.float32
    return [pltpu.VMEM((LANES >> level, 8, LANES), f32) for level in range(LEVELS + 1)] + [
        pltpu.VMEM(((LANES >> level) // 2, 8, LANES), f32) for level in range(LEVELS)
    ]


def per_device(sizes, velocity, refine):
    rows = velocity.shape[1] // LANES
    x = velocity.reshape(COMP, rows, LANES).transpose(1, 0, 2)
    x = pltpu.with_memory_space_constraint(x, pltpu.HBM)
    f32 = jnp.float32
    vmem = pl.BlockSpec(memory_space=pltpu.VMEM)
    ob, win, level_of = pl.pallas_call(
        functools.partial(exchange_kernel, sizes),
        out_shape=[
            jax.ShapeDtypeStruct((COMP, rows, LANES), f32),
            jax.ShapeDtypeStruct((WIN, SIDES, LANES), f32),
            jax.ShapeDtypeStruct((8, LANES), jnp.int32),
        ],
        in_specs=[pl.BlockSpec(memory_space=pltpu.HBM), pl.BlockSpec(memory_space=pltpu.SMEM)],
        out_specs=[vmem] * 3,
        scratch_shapes=[
            pltpu.VMEM((COMP, rows, LANES), f32),
            pltpu.SMEM((2, 1), jnp.int32),
        ]
        + lifting_scratch()
        + [
            pltpu.SemaphoreType.DMA,
            pltpu.SemaphoreType.DMA,
            pltpu.SemaphoreType.REGULAR,
        ],
        compiler_params=pltpu.CompilerParams(
            collective_id=0, has_side_effects=True, vmem_limit_bytes=VMEM_LIMIT
        ),
    )(x, refine)
    out = pl.pallas_call(
        ends_kernel,
        out_shape=jax.ShapeDtypeStruct(x.shape, f32),
        in_specs=[vmem] * 3,
        out_specs=pl.BlockSpec(memory_space=pltpu.HBM),
        scratch_shapes=[
            pltpu.VMEM((HALO, SIDES, LANES), f32),
            pltpu.VMEM((PARTS * PITCH, LANES), f32),
            pltpu.VMEM((PARTS * PITCH, LANES), f32),
            pltpu.SemaphoreType.DMA,
        ]
        + [
            pltpu.VMEM((count, LANES), jnp.int32 if first == -16 else f32)
            for count, first in zip(STRIP_ROWS, STRIP_FIRST)
        ],
        compiler_params=pltpu.CompilerParams(vmem_limit_bytes=VMEM_LIMIT),
    )(ob, win, level_of)
    return out.transpose(1, 0, 2).reshape(velocity.shape)


def solution(mesh):
    sizes = tuple(mesh.shape[name] for name in AXES)
    return jax.shard_map(
        functools.partial(per_device, sizes),
        mesh=mesh,
        in_specs=(P(None, AXES), P(AXES)),
        out_specs=P(None, AXES),
        check_vma=False,
    )
```

```python
import functools

import jax
import jax.numpy as jnp
from jax import lax
from jax.experimental import pallas as pl
from jax.experimental.pallas import tpu as pltpu
from jax.sharding import PartitionSpec as P

AXES = ("node", "rank", "chip")
LEVELS = 6
LANES = 128
COMP = 3
LOGICAL = pl.DeviceIdType.LOGICAL
HALO = 3
WIN = 3 * HALO
SIDES = 8
CHUNK = 8
VMEM_LIMIT = 8 << 20


def neighbours(sizes):
    nodes, ranks, chips = sizes
    total = nodes * ranks * chips
    node, rank, chip = (lax.axis_index(name) for name in AXES)
    place = rank * chips + chip
    me = node * (ranks * chips) + place
    left = jnp.where(me == 0, total - 1, me - 1)
    right = jnp.where(me == total - 1, 0, me + 1)
    left_seam = (place == 0) | (place == ranks * chips - 1)
    right_seam = (place == ranks * chips - 1) | (place == ranks * chips - 2)
    return left, right, left_seam, right_seam


def wait_for_rows(count, buffer, semaphore):
    rows = buffer.at[0, pl.ds(0, count), :]
    pltpu.make_async_copy(rows, rows, semaphore).wait()


def after_with_carry(row, lane):
    rolled = pltpu.roll(row, LANES - 1, 1)
    carried = pltpu.roll(rolled, 7, 0)
    return jnp.where(lane == LANES - 1, carried, rolled)


def before_with_carry(row, lane):
    rolled = pltpu.roll(row, 1, 1)
    carried = pltpu.roll(rolled, 1, 0)
    return jnp.where(lane == 0, carried, rolled)


def predict(e):
    n = e.shape[0] - 3
    return (e[1 : n + 1] + e[2 : n + 2]) * (9.0 / 16.0) - (e[0:n] + e[3 : n + 3]) * (1.0 / 16.0)


def forward(values, details, level, lane, before, after):
    pairs = (LANES >> level) // 2
    src = values[level]
    e_first = src[pl.ds(0, 2, stride=2)]
    pre = before(src[2 * pairs - 2], lane)[None]
    post = jnp.stack([after(e_first[0], lane), after(e_first[1], lane)])
    step = min(CHUNK, pairs)
    d_prev, e_zero, d_zero = None, None, None
    for at in range(0, pairs, step):
        lo, hi = max(at - 1, 0), min(at + step + 2, pairs)
        e = src[pl.ds(2 * lo, hi - lo, stride=2)]
        if at == 0:
            e = jnp.concatenate([pre, e], axis=0)
        need = step + 3 - e.shape[0]
        if need:
            e = jnp.concatenate([e, post[:need]], axis=0)
        d = src[pl.ds(2 * at + 1, step, stride=2)] - predict(e)
        details[level][pl.ds(at, step)] = d
        here = e[1 : step + 1]
        if at == 0:
            e_zero, d_zero = here[0], d[0]
            values[level + 1][pl.ds(1, step - 1)] = here[1:] + (d[:-1] + d[1:]) * 0.25
        else:
            back = jnp.concatenate([d_prev, d[:-1]], axis=0)
            values[level + 1][pl.ds(at, step)] = here + (back + d) * 0.25
        d_prev = d[step - 1 :]
    values[level + 1][0] = e_zero + (before(d_prev[0], lane) + d_zero) * 0.25


def inverse(values, details, level, lane, keep, before, after):
    pairs = (LANES >> level) // 2
    dst = values[level]
    coarse = values[level + 1]

    def kept(at, count):
        return jnp.where(keep[None], details[level][pl.ds(at, count)], 0.0)

    step = min(CHUNK, pairs)
    back = before(kept(pairs - 1, 1)[0], lane)[None]
    for at in range(0, pairs, step):
        k = kept(at, step)
        shifted = jnp.concatenate([back, k[:-1]], axis=0)
        dst[pl.ds(2 * at, step, stride=2)] = coarse[pl.ds(at, step)] - (shifted + k) * 0.25
        back = k[step - 1 :]
    e_first = dst[pl.ds(0, 2, stride=2)]
    pre = before(dst[2 * pairs - 2], lane)[None]
    post = jnp.stack([after(e_first[0], lane), after(e_first[1], lane)])
    for at in range(0, pairs, step):
        lo, hi = max(at - 1, 0), min(at + step + 2, pairs)
        e = dst[pl.ds(2 * lo, hi - lo, stride=2)]
        if at == 0:
            e = jnp.concatenate([pre, e], axis=0)
        need = step + 3 - e.shape[0]
        if need:
            e = jnp.concatenate([e, post[:need]], axis=0)
        dst[pl.ds(2 * at + 1, step, stride=2)] = kept(at, step) + predict(e)


def transform(values, details, lane, level_of, before, after):
    for level in range(LEVELS):
        forward(values, details, level, lane, before, after)
    for level in reversed(range(LEVELS)):
        inverse(values, details, level, lane, level_of > level, before, after)


def lanes_and_sublanes():
    return (
        lax.broadcasted_iota(jnp.int32, (8, LANES), 1),
        lax.broadcasted_iota(jnp.int32, (8, LANES), 0),
    )


PARTS = 8
PART = LANES // PARTS
PITCH = PART + 1
STRIP_ROWS = (72, 24, 16, 16, 16, 16, 40, 16)
STRIP_FIRST = (-32, -8, -2, -4, -3, -2, -16, -2)


def rows_away(value, by):
    return pltpu.roll(value, (-by * SIDES) % LANES, 1) if by else value


def parts_away(here, beyond, by, sublane):
    turn = (-by) % PARTS
    inside = sublane < PARTS - by if by > 0 else sublane >= -by
    return jnp.where(inside, pltpu.roll(here, turn, 0), pltpu.roll(beyond, turn, 0))


def predicted(before, here, after, later):
    return (here + after) * (9.0 / 16.0) - (before + later) * (1.0 / 16.0)


def both_away(pair, by, sublane):
    here, beyond = pair
    return parts_away(here, beyond, by, sublane), parts_away(beyond, here, by, sublane)


class Strip:
    def __init__(self, buffer, first):
        self.buffer, self.first = buffer, first

    def put(self, place, value, apart=1):
        self.buffer[pl.ds(place - self.first, 8, stride=apart), :] = value

    def get(self, place, apart=1):
        return self.buffer[pl.ds(place - self.first, 8, stride=apart), :]


class Kept:
    def __init__(self, values, sublane):
        self.values, self.sublane, self.seen = values, sublane, {}

    def __getitem__(self, place):
        if place not in self.seen:
            part, slot = divmod(place, len(self.values))
            value = self.values[slot]
            if part:
                beyond = rows_away(value, 1 if part > 0 else -1)
                value = parts_away(value, beyond, part, self.sublane)
            self.seen[place] = value
        return self.seen[place]


def scaled(before, here, after, twice_before, twice_after):
    return here * (23.0 / 32.0) - (before + after) * 0.125 + (twice_before + twice_after) * (1.0 / 64.0)


def lift_strips(value, level_of, buffers):
    line, above, evens, kept, kept_above, back, levels, done = (
        Strip(buffer, first) for buffer, first in zip(buffers, STRIP_FIRST)
    )
    for row in range(-3, 4):
        line.put(row * PARTS, rows_away(value, row))
    for row in range(-2, 3):
        levels.put(row * PARTS, rows_away(level_of, row))

    def approached(strip, first):
        at = lambda by: strip.get(2 * first + by, 2)
        return scaled(at(-2), at(0), at(2), at(-4), at(4)) + (at(-1) + at(1)) * 0.25

    def detailed(strip, first, level, apart):
        at = lambda by: strip.get(2 * first + by, 2)
        detail = at(1) - predicted(at(-2), at(0), at(2), at(4))
        return jnp.where(levels.get(apart * (2 * first + 1), 2 * apart) > level, detail, 0.0)

    for first in (-8, 0, 8):
        above.put(first, approached(line, first))
    for first in (-4, 4):
        kept.put(first, detailed(line, first, LEVELS - 2, 1))
    evens.put(-2, approached(above, -2))
    kept_above.put(-3, detailed(above, -3, LEVELS - 1, 2))
    for y, k, to in ((evens, kept_above, back), (back, kept, done)):
        to.put(-2, y.get(-1) - (k.get(-2) + k.get(-1)) * 0.25, 2)
        to.put(
            -1,
            scaled(k.get(-2), k.get(-1), k.get(0), k.get(-3), k.get(1))
            + predicted(y.get(-2), y.get(-1), y.get(0), y.get(1)),
            2,
        )
    return done


def lift_window(inner, outer, level_of, sublane, buffers):
    kept = []
    level = 0
    pairs = list(zip(inner, outer))
    while len(pairs) > 1:
        even, odd = pairs[0::2], pairs[1::2]
        half = len(even)
        last = both_away(even[-1], -1, sublane)
        ahead = [last] + even + [
            both_away(even[i % half], 1 + i // half, sublane) for i in range(2)
        ]
        detail = [
            tuple(odd[i][n] - predicted(*(e[n] for e in ahead[i : i + 4])) for n in (0, 1))
            for i in range(half)
        ]
        back = [both_away(detail[-1], -1, sublane)] + detail
        pairs = [
            tuple(even[i][n] + (back[i][n] + back[i + 1][n]) * 0.25 for n in (0, 1)) for i in range(half)
        ]
        kept.append(Kept([jnp.where(level_of > level, d[0], 0.0) for d in detail], sublane))
        level += 1
    done = lift_strips(pairs[0][0], level_of, buffers)
    wanted = [range(0, PART)]
    for _ in kept:
        low = [n // 2 - 1 if n % 2 else n // 2 for n in wanted[-1]]
        high = [n // 2 + 2 if n % 2 else n // 2 for n in wanted[-1]]
        wanted.append(range(min(low), max(high) + 1))
    current = {place: done.get(place) for place in wanted.pop()}
    while kept:
        k = kept.pop()
        even = {i: value - (k[i - 1] + k[i]) * 0.25 for i, value in current.items()}
        current = {}
        for n in wanted.pop():
            i = n // 2
            if n % 2:
                current[n] = k[i] + predicted(even[i - 1], even[i], even[i + 1], even[i + 2])
            else:
                current[n] = even[i]
    return [current[n] for n in range(PART)]


def exchange_kernel(sizes, x_ref, refine_ref, ob, win, level_ref, xb, near_level, *rest):
    values, details = rest[: LEVELS + 1], rest[LEVELS + 1 : 2 * LEVELS + 1]
    recv_sem, level_recv_sem, here_sem = rest[2 * LEVELS + 1 :]
    rows = x_ref.shape[0]
    left, right, left_seam, right_seam = neighbours(sizes)
    barrier = pltpu.get_barrier_semaphore()
    pl.semaphore_signal(barrier, inc=1, device_id=left, device_id_type=LOGICAL)

    @pl.when(jnp.logical_not(right_seam))
    def _():
        pl.semaphore_signal(barrier, inc=1, device_id=right, device_id_type=LOGICAL)

    def send_and_lift(in_sem, send_sem, level_send_sem):
        def remote(src, dst, sent, come, device):
            return pltpu.make_async_remote_copy(
                src_ref=src,
                dst_ref=dst,
                send_sem=sent,
                recv_sem=come,
                device_id=device,
                device_id_type=LOGICAL,
            )

        low, high = pl.ds(0, COMP), pl.ds(COMP, COMP)
        level_right = remote(
            refine_ref, near_level.at[0], level_send_sem, level_recv_sem, right
        )
        level_left = remote(refine_ref, near_level.at[1], level_send_sem, level_recv_sem, left)
        to_right = [
            remote(
                x_ref.at[pl.ds(rows - HALO, HALO)], win.at[pl.ds(0, HALO), low, :], send_sem, recv_sem, right
            ),
            level_right,
        ]
        to_left = [
            remote(
                x_ref.at[pl.ds(0, HALO)], win.at[pl.ds(2 * HALO, HALO), high, :], send_sem, recv_sem, left
            ),
            level_left,
        ]
        pl.semaphore_wait(barrier, jnp.where(left_seam, 1, 2))
        for copy in to_right:
            copy.start()

        @pl.when(right_seam)
        def _():
            pl.semaphore_signal(here_sem, inc=1, device_id=right, device_id_type=LOGICAL)

        @pl.when(jnp.logical_not(left_seam))
        def _():
            for copy in to_left:
                copy.start()

        for c in range(COMP):
            pltpu.make_async_copy(x_ref.at[:, c, :], xb.at[c], in_sem).start()
        pltpu.make_async_copy(xb, xb, in_sem).wait()

        lane, sublane = lanes_and_sublanes()
        own = refine_ref[0]
        for c in range(COMP):
            win[pl.ds(HALO, 2 * HALO), c, :] = xb[c, pl.ds(0, 2 * HALO), :]
            win[pl.ds(0, 2 * HALO), COMP + c, :] = xb[c, pl.ds(rows - 2 * HALO, 2 * HALO), :]
        for c in range(COMP):
            for half in range(2):
                values[0][:, 2 * c + half, :] = xb[c, pl.ds(half * LANES, LANES), :].T
        transform(
            values, details, lane, jnp.full((8, LANES), own, jnp.int32), before_with_carry, after_with_carry
        )
        for c in range(COMP):
            for half in range(2):
                ob[c, pl.ds(half * LANES, LANES), :] = values[0][:, 2 * c + half, :].T

        side = lane & (SIDES - 1)
        from_left = (side < COMP) & (lane < HALO * SIDES)
        from_right = (side >= COMP) & (lane >= 2 * HALO * SIDES)
        level_ref[...] = jnp.where(from_left, 1, jnp.where(from_right, 2, 0))

        @pl.when(left_seam)
        def _():
            pl.semaphore_wait(here_sem, 1)
            for c in range(COMP):
                remote(
                    xb.at[c, pl.ds(0, HALO), :],
                    win.at[pl.ds(2 * HALO, HALO), COMP + c, :],
                    send_sem,
                    recv_sem,
                    left,
                ).start()
            level_left.start()

        wait_for_rows(2 * HALO * COMP, xb, send_sem)
        pltpu.make_async_copy(near_level, near_level, level_send_sem).wait()

    pl.run_scoped(send_and_lift, *[pltpu.SemaphoreType.DMA] * 3)
    pltpu.make_async_copy(near_level, near_level, level_recv_sem).wait()
    wait_for_rows(2 * HALO * COMP, xb, recv_sem)
    whose = level_ref[...]
    level_ref[...] = jnp.where(
        whose == 1, near_level[0, 0], jnp.where(whose == 2, near_level[1, 0], refine_ref[0])
    )


def write_ends(ob, win, level_ref, out_ref, wout, turned, beyond, strips, out_sem):
    rows = out_ref.shape[0]
    for c in range(COMP):
        pltpu.make_async_copy(
            ob.at[c, pl.ds(HALO, rows - 2 * HALO), :],
            out_ref.at[pl.ds(HALO, rows - 2 * HALO), c, :],
            out_sem,
        ).start()
    lane, sublane = lanes_and_sublanes()
    used = WIN * SIDES
    rows_here = win[...]
    rows_next = jnp.concatenate([rows_here[1:], rows_here[:1]], axis=0)
    rows_last = jnp.concatenate([rows_here[WIN - 1 :], rows_here[: WIN - 1]], axis=0)
    cell = lax.broadcasted_iota(jnp.int32, rows_here.shape, 2)
    around = jnp.where(cell < LANES // 2, rows_next, rows_last)
    for buffer, value in ((turned, rows_here), (beyond, around)):
        cells = value.reshape(used, LANES).T
        for part in range(PARTS):
            buffer[pl.ds(part * PITCH, PART), :used] = cells[part * PART : (part + 1) * PART]
    inner = [turned[pl.ds(k, PARTS, stride=PITCH), :] for k in range(PART)]
    outer = [beyond[pl.ds(k, PARTS, stride=PITCH), :] for k in range(PART)]
    for k, value in enumerate(lift_window(inner, outer, level_ref[...], sublane, strips)):
        turned[pl.ds(k, PARTS, stride=PITCH), :] = value
    cells = jnp.concatenate([turned[pl.ds(part * PITCH, PART), :] for part in range(PARTS)], axis=0)
    redone = cells.T[HALO * SIDES : 2 * HALO * SIDES]
    wout[...] = redone.reshape(HALO, SIDES, LANES)
    for side, first in ((0, 0), (1, rows - HALO)):
        pltpu.make_async_copy(
            wout.at[:, pl.ds(side * COMP, COMP), :], out_ref.at[pl.ds(first, HALO)], out_sem
        ).start()
    pltpu.make_async_copy(ob, ob, out_sem).wait()


def ends_kernel(ob, win, level_ref, out_ref, wout, turned, beyond, *strips):
    pl.run_scoped(
        functools.partial(write_ends, ob, win, level_ref, out_ref, wout, turned, beyond, strips),
        pltpu.SemaphoreType.DMA,
    )


def lifting_scratch():
    f32 = jnp.float32
    return [pltpu.VMEM((LANES >> level, 8, LANES), f32) for level in range(LEVELS + 1)] + [
        pltpu.VMEM(((LANES >> level) // 2, 8, LANES), f32) for level in range(LEVELS)
    ]


def per_device(sizes, velocity, refine):
    rows = velocity.shape[1] // LANES
    x = velocity.reshape(COMP, rows, LANES).transpose(1, 0, 2)
    x = pltpu.with_memory_space_constraint(x, pltpu.HBM)
    f32 = jnp.float32
    vmem = pl.BlockSpec(memory_space=pltpu.VMEM)
    ob, win, level_of = pl.pallas_call(
        functools.partial(exchange_kernel, sizes),
        out_shape=[
            jax.ShapeDtypeStruct((COMP, rows, LANES), f32),
            jax.ShapeDtypeStruct((WIN, SIDES, LANES), f32),
            jax.ShapeDtypeStruct((8, LANES), jnp.int32),
        ],
        in_specs=[pl.BlockSpec(memory_space=pltpu.HBM), pl.BlockSpec(memory_space=pltpu.SMEM)],
        out_specs=[vmem] * 3,
        scratch_shapes=[
            pltpu.VMEM((COMP, rows, LANES), f32),
            pltpu.SMEM((2, 1), jnp.int32),
        ]
        + lifting_scratch()
        + [
            pltpu.SemaphoreType.DMA,
            pltpu.SemaphoreType.DMA,
            pltpu.SemaphoreType.REGULAR,
        ],
        compiler_params=pltpu.CompilerParams(
            collective_id=0, has_side_effects=True, vmem_limit_bytes=VMEM_LIMIT
        ),
    )(x, refine)
    out = pl.pallas_call(
        ends_kernel,
        out_shape=jax.ShapeDtypeStruct(x.shape, f32),
        in_specs=[vmem] * 3,
        out_specs=pl.BlockSpec(memory_space=pltpu.HBM),
        scratch_shapes=[
            pltpu.VMEM((HALO, SIDES, LANES), f32),
            pltpu.VMEM((PARTS * PITCH, LANES), f32),
            pltpu.VMEM((PARTS * PITCH, LANES), f32),
        ]
        + [
            pltpu.VMEM((count, LANES), jnp.int32 if first == -16 else f32)
            for count, first in zip(STRIP_ROWS, STRIP_FIRST)
        ],
        compiler_params=pltpu.CompilerParams(vmem_limit_bytes=VMEM_LIMIT),
    )(ob, win, level_of)
    return out.transpose(1, 0, 2).reshape(velocity.shape)


def solution(mesh):
    sizes = tuple(mesh.shape[name] for name in AXES)
    return jax.shard_map(
        functools.partial(per_device, sizes),
        mesh=mesh,
        in_specs=(P(None, AXES), P(AXES)),
        out_specs=P(None, AXES),
        check_vma=False,
    )
```

```python
import functools

import jax
import jax.numpy as jnp
from jax import lax
from jax.experimental import pallas as pl
from jax.experimental.pallas import tpu as pltpu
from jax.sharding import PartitionSpec as P

AXES = ("node", "rank", "chip")
LEVELS = 6
LANES = 128
COMP = 3
LOGICAL = pl.DeviceIdType.LOGICAL
HALO = 3
WIN = 3 * HALO
SIDES = 8
CHUNK = 8
VMEM_LIMIT = 8 << 20


def neighbours(sizes):
    nodes, ranks, chips = sizes
    total = nodes * ranks * chips
    node, rank, chip = (lax.axis_index(name) for name in AXES)
    place = rank * chips + chip
    me = node * (ranks * chips) + place
    left = jnp.where(me == 0, total - 1, me - 1)
    right = jnp.where(me == total - 1, 0, me + 1)
    left_seam = (place == 0) | (place == ranks * chips - 1)
    right_seam = (place == ranks * chips - 1) | (place == ranks * chips - 2)
    return left, right, left_seam, right_seam


def wait_for_rows(count, buffer, semaphore):
    rows = buffer.at[0, pl.ds(0, count), :]
    pltpu.make_async_copy(rows, rows, semaphore).wait()


def after_with_carry(row, lane):
    rolled = pltpu.roll(row, LANES - 1, 1)
    carried = pltpu.roll(rolled, 7, 0)
    return jnp.where(lane == LANES - 1, carried, rolled)


def before_with_carry(row, lane):
    rolled = pltpu.roll(row, 1, 1)
    carried = pltpu.roll(rolled, 1, 0)
    return jnp.where(lane == 0, carried, rolled)


def predict(e):
    n = e.shape[0] - 3
    return (e[1 : n + 1] + e[2 : n + 2]) * (9.0 / 16.0) - (e[0:n] + e[3 : n + 3]) * (1.0 / 16.0)


def forward(values, details, level, lane, before, after):
    pairs = (LANES >> level) // 2
    src = values[level]
    e_first = src[pl.ds(0, 2, stride=2)]
    pre = before(src[2 * pairs - 2], lane)[None]
    post = jnp.stack([after(e_first[0], lane), after(e_first[1], lane)])
    step = min(CHUNK, pairs)
    d_prev, e_zero, d_zero = None, None, None
    for at in range(0, pairs, step):
        lo, hi = max(at - 1, 0), min(at + step + 2, pairs)
        e = src[pl.ds(2 * lo, hi - lo, stride=2)]
        if at == 0:
            e = jnp.concatenate([pre, e], axis=0)
        need = step + 3 - e.shape[0]
        if need:
            e = jnp.concatenate([e, post[:need]], axis=0)
        d = src[pl.ds(2 * at + 1, step, stride=2)] - predict(e)
        details[level][pl.ds(at, step)] = d
        here = e[1 : step + 1]
        if at == 0:
            e_zero, d_zero = here[0], d[0]
            values[level + 1][pl.ds(1, step - 1)] = here[1:] + (d[:-1] + d[1:]) * 0.25
        else:
            back = jnp.concatenate([d_prev, d[:-1]], axis=0)
            values[level + 1][pl.ds(at, step)] = here + (back + d) * 0.25
        d_prev = d[step - 1 :]
    values[level + 1][0] = e_zero + (before(d_prev[0], lane) + d_zero) * 0.25


def inverse(values, details, level, lane, keep, before, after):
    pairs = (LANES >> level) // 2
    dst = values[level]
    coarse = values[level + 1]

    def kept(at, count):
        return jnp.where(keep[None], details[level][pl.ds(at, count)], 0.0)

    step = min(CHUNK, pairs)
    back = before(kept(pairs - 1, 1)[0], lane)[None]
    for at in range(0, pairs, step):
        k = kept(at, step)
        shifted = jnp.concatenate([back, k[:-1]], axis=0)
        dst[pl.ds(2 * at, step, stride=2)] = coarse[pl.ds(at, step)] - (shifted + k) * 0.25
        back = k[step - 1 :]
    e_first = dst[pl.ds(0, 2, stride=2)]
    pre = before(dst[2 * pairs - 2], lane)[None]
    post = jnp.stack([after(e_first[0], lane), after(e_first[1], lane)])
    for at in range(0, pairs, step):
        lo, hi = max(at - 1, 0), min(at + step + 2, pairs)
        e = dst[pl.ds(2 * lo, hi - lo, stride=2)]
        if at == 0:
            e = jnp.concatenate([pre, e], axis=0)
        need = step + 3 - e.shape[0]
        if need:
            e = jnp.concatenate([e, post[:need]], axis=0)
        dst[pl.ds(2 * at + 1, step, stride=2)] = kept(at, step) + predict(e)


def transform(values, details, lane, level_of, before, after):
    for level in range(LEVELS):
        forward(values, details, level, lane, before, after)
    for level in reversed(range(LEVELS)):
        inverse(values, details, level, lane, level_of > level, before, after)


def lanes_and_sublanes():
    return (
        lax.broadcasted_iota(jnp.int32, (8, LANES), 1),
        lax.broadcasted_iota(jnp.int32, (8, LANES), 0),
    )


PARTS = 8
PART = LANES // PARTS
PITCH = PART + 1
STRIP_ROWS = (72, 24, 16, 16, 16, 16, 40, 16)
STRIP_FIRST = (-32, -8, -2, -4, -3, -2, -16, -2)


def rows_away(value, by):
    return pltpu.roll(value, (-by * SIDES) % LANES, 1) if by else value


def parts_away(here, beyond, by, sublane):
    turn = (-by) % PARTS
    inside = sublane < PARTS - by if by > 0 else sublane >= -by
    return jnp.where(inside, pltpu.roll(here, turn, 0), pltpu.roll(beyond, turn, 0))


def predicted(before, here, after, later):
    return (here + after) * (9.0 / 16.0) - (before + later) * (1.0 / 16.0)


def both_away(pair, by, sublane):
    here, beyond = pair
    return parts_away(here, beyond, by, sublane), parts_away(beyond, here, by, sublane)


class Strip:
    def __init__(self, buffer, first):
        self.buffer, self.first = buffer, first

    def put(self, place, value, apart=1):
        self.buffer[pl.ds(place - self.first, 8, stride=apart), :] = value

    def get(self, place, apart=1):
        return self.buffer[pl.ds(place - self.first, 8, stride=apart), :]


class Kept:
    def __init__(self, values, sublane):
        self.values, self.sublane, self.seen = values, sublane, {}

    def __getitem__(self, place):
        if place not in self.seen:
            part, slot = divmod(place, len(self.values))
            value = self.values[slot]
            if part:
                beyond = rows_away(value, 1 if part > 0 else -1)
                value = parts_away(value, beyond, part, self.sublane)
            self.seen[place] = value
        return self.seen[place]


def scaled(before, here, after, twice_before, twice_after):
    return here * (23.0 / 32.0) - (before + after) * 0.125 + (twice_before + twice_after) * (1.0 / 64.0)


def lift_strips(value, level_of, buffers):
    line, above, evens, kept, kept_above, back, levels, done = (
        Strip(buffer, first) for buffer, first in zip(buffers, STRIP_FIRST)
    )
    for row in range(-3, 4):
        line.put(row * PARTS, rows_away(value, row))
    for row in range(-2, 3):
        levels.put(row * PARTS, rows_away(level_of, row))

    def approached(strip, first):
        at = lambda by: strip.get(2 * first + by, 2)
        return scaled(at(-2), at(0), at(2), at(-4), at(4)) + (at(-1) + at(1)) * 0.25

    def detailed(strip, first, level, apart):
        at = lambda by: strip.get(2 * first + by, 2)
        detail = at(1) - predicted(at(-2), at(0), at(2), at(4))
        return jnp.where(levels.get(apart * (2 * first + 1), 2 * apart) > level, detail, 0.0)

    for first in (-8, 0, 8):
        above.put(first, approached(line, first))
    for first in (-4, 4):
        kept.put(first, detailed(line, first, LEVELS - 2, 1))
    evens.put(-2, approached(above, -2))
    kept_above.put(-3, detailed(above, -3, LEVELS - 1, 2))
    for y, k, to in ((evens, kept_above, back), (back, kept, done)):
        to.put(-2, y.get(-1) - (k.get(-2) + k.get(-1)) * 0.25, 2)
        to.put(
            -1,
            scaled(k.get(-2), k.get(-1), k.get(0), k.get(-3), k.get(1))
            + predicted(y.get(-2), y.get(-1), y.get(0), y.get(1)),
            2,
        )
    return done


def lift_window(inner, outer, level_of, sublane, buffers):
    kept = []
    level = 0
    pairs = list(zip(inner, outer))
    while len(pairs) > 1:
        even, odd = pairs[0::2], pairs[1::2]
        half = len(even)
        last = both_away(even[-1], -1, sublane)
        ahead = [last] + even + [
            both_away(even[i % half], 1 + i // half, sublane) for i in range(2)
        ]
        detail = [
            tuple(odd[i][n] - predicted(*(e[n] for e in ahead[i : i + 4])) for n in (0, 1))
            for i in range(half)
        ]
        back = [both_away(detail[-1], -1, sublane)] + detail
        pairs = [
            tuple(even[i][n] + (back[i][n] + back[i + 1][n]) * 0.25 for n in (0, 1)) for i in range(half)
        ]
        kept.append(Kept([jnp.where(level_of > level, d[0], 0.0) for d in detail], sublane))
        level += 1
    done = lift_strips(pairs[0][0], level_of, buffers)
    wanted = [range(0, PART)]
    for _ in kept:
        low = [n // 2 - 1 if n % 2 else n // 2 for n in wanted[-1]]
        high = [n // 2 + 2 if n % 2 else n // 2 for n in wanted[-1]]
        wanted.append(range(min(low), max(high) + 1))
    current = {place: done.get(place) for place in wanted.pop()}
    while kept:
        k = kept.pop()
        even = {i: value - (k[i - 1] + k[i]) * 0.25 for i, value in current.items()}
        current = {}
        for n in wanted.pop():
            i = n // 2
            if n % 2:
                current[n] = k[i] + predicted(even[i - 1], even[i], even[i + 1], even[i + 2])
            else:
                current[n] = even[i]
    return [current[n] for n in range(PART)]


def exchange_kernel(sizes, x_ref, refine_ref, ob, win, level_ref, xb, near_level, *rest):
    values, details = rest[: LEVELS + 1], rest[LEVELS + 1 : 2 * LEVELS + 1]
    recv_sem, level_recv_sem, here_sem = rest[2 * LEVELS + 1 :]
    rows = x_ref.shape[0]
    left, right, left_seam, right_seam = neighbours(sizes)
    barrier = pltpu.get_barrier_semaphore()
    pl.semaphore_signal(barrier, inc=1, device_id=left, device_id_type=LOGICAL)

    @pl.when(jnp.logical_not(right_seam))
    def _():
        pl.semaphore_signal(barrier, inc=1, device_id=right, device_id_type=LOGICAL)

    def send_and_lift(in_sem, send_sem, level_send_sem):
        def remote(src, dst, sent, come, device):
            return pltpu.make_async_remote_copy(
                src_ref=src,
                dst_ref=dst,
                send_sem=sent,
                recv_sem=come,
                device_id=device,
                device_id_type=LOGICAL,
            )

        low, high = pl.ds(0, COMP), pl.ds(COMP, COMP)
        level_right = remote(
            refine_ref, near_level.at[0], level_send_sem, level_recv_sem, right
        )
        level_left = remote(refine_ref, near_level.at[1], level_send_sem, level_recv_sem, left)
        to_right = [
            remote(
                x_ref.at[pl.ds(rows - HALO, HALO)], win.at[pl.ds(0, HALO), low, :], send_sem, recv_sem, right
            ),
            level_right,
        ]
        to_left = [
            remote(
                x_ref.at[pl.ds(0, HALO)], win.at[pl.ds(2 * HALO, HALO), high, :], send_sem, recv_sem, left
            ),
            level_left,
        ]
        pl.semaphore_wait(barrier, jnp.where(left_seam, 1, 2))
        for copy in to_right:
            copy.start()

        @pl.when(right_seam)
        def _():
            pl.semaphore_signal(here_sem, inc=1, device_id=right, device_id_type=LOGICAL)

        @pl.when(jnp.logical_not(left_seam))
        def _():
            for copy in to_left:
                copy.start()

        for c in range(COMP):
            pltpu.make_async_copy(x_ref.at[:, c, :], xb.at[c], in_sem).start()
        pltpu.make_async_copy(xb, xb, in_sem).wait()

        lane, sublane = lanes_and_sublanes()
        own = refine_ref[0]
        for c in range(COMP):
            win[pl.ds(HALO, 2 * HALO), c, :] = xb[c, pl.ds(0, 2 * HALO), :]
            win[pl.ds(0, 2 * HALO), COMP + c, :] = xb[c, pl.ds(rows - 2 * HALO, 2 * HALO), :]
        for c in range(COMP):
            for half in range(2):
                values[0][:, 2 * c + half, :] = xb[c, pl.ds(half * LANES, LANES), :].T
        transform(
            values, details, lane, jnp.full((8, LANES), own, jnp.int32), before_with_carry, after_with_carry
        )
        for c in range(COMP):
            for half in range(2):
                ob[c, pl.ds(half * LANES, LANES), :] = values[0][:, 2 * c + half, :].T

        side = lane & (SIDES - 1)
        from_left = (side < COMP) & (lane < HALO * SIDES)
        from_right = (side >= COMP) & (lane >= 2 * HALO * SIDES)
        level_ref[...] = jnp.where(from_left, 1, jnp.where(from_right, 2, 0))

        @pl.when(left_seam)
        def _():
            pl.semaphore_wait(here_sem, 1)
            for c in range(COMP):
                remote(
                    xb.at[c, pl.ds(0, HALO), :],
                    win.at[pl.ds(2 * HALO, HALO), COMP + c, :],
                    send_sem,
                    recv_sem,
                    left,
                ).start()
            level_left.start()

        wait_for_rows(2 * HALO * COMP, xb, send_sem)
        pltpu.make_async_copy(near_level, near_level, level_send_sem).wait()

    pl.run_scoped(send_and_lift, *[pltpu.SemaphoreType.DMA] * 3)
    pltpu.make_async_copy(near_level, near_level, level_recv_sem).wait()
    wait_for_rows(2 * HALO * COMP, xb, recv_sem)
    whose = level_ref[...]
    level_ref[...] = jnp.where(
        whose == 1, near_level[0, 0], jnp.where(whose == 2, near_level[1, 0], refine_ref[0])
    )


def ends_kernel(ob, win, level_ref, out_ref, wout, turned, beyond, out_sem, *strips):
    rows = out_ref.shape[0]
    for c in range(COMP):
        pltpu.make_async_copy(
            ob.at[c, pl.ds(HALO, rows - 2 * HALO), :],
            out_ref.at[pl.ds(HALO, rows - 2 * HALO), c, :],
            out_sem,
        ).start()
    lane, sublane = lanes_and_sublanes()
    used = WIN * SIDES
    rows_here = win[...]
    rows_next = jnp.concatenate([rows_here[1:], rows_here[:1]], axis=0)
    rows_last = jnp.concatenate([rows_here[WIN - 1 :], rows_here[: WIN - 1]], axis=0)
    cell = lax.broadcasted_iota(jnp.int32, rows_here.shape, 2)
    around = jnp.where(cell < LANES // 2, rows_next, rows_last)
    for buffer, value in ((turned, rows_here), (beyond, around)):
        cells = value.reshape(used, LANES).T
        for part in range(PARTS):
            buffer[pl.ds(part * PITCH, PART), :used] = cells[part * PART : (part + 1) * PART]
    inner = [turned[pl.ds(k, PARTS, stride=PITCH), :] for k in range(PART)]
    outer = [beyond[pl.ds(k, PARTS, stride=PITCH), :] for k in range(PART)]
    for k, value in enumerate(lift_window(inner, outer, level_ref[...], sublane, strips)):
        turned[pl.ds(k, PARTS, stride=PITCH), :] = value
    cells = jnp.concatenate([turned[pl.ds(part * PITCH, PART), :] for part in range(PARTS)], axis=0)
    redone = cells.T[HALO * SIDES : 2 * HALO * SIDES]
    wout[...] = redone.reshape(HALO, SIDES, LANES)
    for side, first in ((0, 0), (1, rows - HALO)):
        pltpu.make_async_copy(
            wout.at[:, pl.ds(side * COMP, COMP), :], out_ref.at[pl.ds(first, HALO)], out_sem
        ).start(priority=1)
    pltpu.make_async_copy(ob, ob, out_sem).wait()


def lifting_scratch():
    f32 = jnp.float32
    return [pltpu.VMEM((LANES >> level, 8, LANES), f32) for level in range(LEVELS + 1)] + [
        pltpu.VMEM(((LANES >> level) // 2, 8, LANES), f32) for level in range(LEVELS)
    ]


def per_device(sizes, velocity, refine):
    rows = velocity.shape[1] // LANES
    x = velocity.reshape(COMP, rows, LANES).transpose(1, 0, 2)
    x = pltpu.with_memory_space_constraint(x, pltpu.HBM)
    f32 = jnp.float32
    vmem = pl.BlockSpec(memory_space=pltpu.VMEM)
    ob, win, level_of = pl.pallas_call(
        functools.partial(exchange_kernel, sizes),
        out_shape=[
            jax.ShapeDtypeStruct((COMP, rows, LANES), f32),
            jax.ShapeDtypeStruct((WIN, SIDES, LANES), f32),
            jax.ShapeDtypeStruct((8, LANES), jnp.int32),
        ],
        in_specs=[pl.BlockSpec(memory_space=pltpu.HBM), pl.BlockSpec(memory_space=pltpu.SMEM)],
        out_specs=[vmem] * 3,
        scratch_shapes=[
            pltpu.VMEM((COMP, rows, LANES), f32),
            pltpu.SMEM((2, 1), jnp.int32),
        ]
        + lifting_scratch()
        + [
            pltpu.SemaphoreType.DMA,
            pltpu.SemaphoreType.DMA,
            pltpu.SemaphoreType.REGULAR,
        ],
        compiler_params=pltpu.CompilerParams(
            collective_id=0, has_side_effects=True, vmem_limit_bytes=VMEM_LIMIT
        ),
    )(x, refine)
    out = pl.pallas_call(
        ends_kernel,
        out_shape=jax.ShapeDtypeStruct(x.shape, f32),
        in_specs=[vmem] * 3,
        out_specs=pl.BlockSpec(memory_space=pltpu.HBM),
        scratch_shapes=[
            pltpu.VMEM((HALO, SIDES, LANES), f32),
            pltpu.VMEM((PARTS * PITCH, LANES), f32),
            pltpu.VMEM((PARTS * PITCH, LANES), f32),
            pltpu.SemaphoreType.DMA,
        ]
        + [
            pltpu.VMEM((count, LANES), jnp.int32 if first == -16 else f32)
            for count, first in zip(STRIP_ROWS, STRIP_FIRST)
        ],
        compiler_params=pltpu.CompilerParams(vmem_limit_bytes=VMEM_LIMIT),
    )(ob, win, level_of)
    return out.transpose(1, 0, 2).reshape(velocity.shape)


def solution(mesh):
    sizes = tuple(mesh.shape[name] for name in AXES)
    return jax.shard_map(
        functools.partial(per_device, sizes),
        mesh=mesh,
        in_specs=(P(None, AXES), P(AXES)),
        out_specs=P(None, AXES),
        check_vma=False,
    )
```
